32 devices in a mesh: dp: 8 (over y, x, core), expert: 4 (over z).
Axes of the slice: x: 2, y: 2, z: 4, core: 2. Of those that a mesh axis runs over, the one named last changes fastest.
Arguments:
- tokens: bfloat16 [8192, 1536], P(('dp', 'expert')), may hold values from -6 to 6
- attn_gain: bfloat16 [1536], P('dp'), may hold values from 0.5 to 1.5
- q_weight: bfloat16 [1536, 1536], P('dp'), may hold values from -0.15625 to 0.15625
- key_matrix: bfloat16 [1536, 512], P('dp'), may hold values from -0.15625 to 0.15625
- value_matrix: bfloat16 [1536, 512], P('dp'), may hold values from -0.15625 to 0.15625
- o_weight: bfloat16 [1536, 1536], P('dp'), may hold values from -0.75 to 0.75
- ffn_gain: bfloat16 [1536], P('dp'), may hold values from 0.5 to 1.5
- router_weight: bfloat16 [1536, 20], P('dp'), may hold values from -0.078125 to 0.078125
- expert_gate: bfloat16 [20, 1536, 512], P('expert', 'dp'), may hold values from -0.15625 to 0.15625
- expert_up: bfloat16 [20, 1536, 512], P('expert', 'dp'), may hold values from -0.15625 to 0.15625
- expert_down: bfloat16 [20, 512, 1536], P('expert', 'dp'), may hold values from -1 to 1
- routes: int32 [8192, 8], P(('dp', 'expert')), may hold values from 0 to 19, all different within a row; in each aligned block of 256 rows (0 to 255, 256 to 511, ...) at most 128 rows name the same one
- starts: int32 [8, 2], P('dp'), may hold values from 0 to 768, as said below
- cotangent: bfloat16 [8192, 1536], P(('dp', 'expert')), may hold values from -6 to 6
Outputs:
- output: bfloat16 [8192, 1536], P(('dp', 'expert'))
- input_grad: bfloat16 [8192, 1536], P(('dp', 'expert'))
- attn_gain_grad: float32 [1536], P('dp')
- q_grad: float32 [1536, 1536], P('dp')
- k_grad: float32 [1536, 512], P('dp')
- v_grad: float32 [1536, 512], P('dp')
- o_grad: float32 [1536, 1536], P('dp')
- ffn_gain_grad: float32 [1536], P('dp')
- router_grad: float32 [1536, 20], P('dp')
- gate_grad: float32 [20, 1536, 512], P('expert', 'dp')
- up_grad: float32 [20, 1536, 512], P('expert', 'dp')
- down_grad: float32 [20, 512, 1536], P('expert', 'dp')
The draws below stay inside these ranges and needn't reach their ends.
Inputs may be any that keep to these rules, and one draw needn't show every extreme that they name: `routes`: among the 256 tokens of one device no expert is named by more than 128 tokens, and in every draw some device has an expert named by exactly 128. `starts`: piece k of a sequence lies within positions k * 512 to (k + 1) * 512 - 1.
All inputs are finite; a program needn't handle non-finite values.
Results may differ from the reference program's by a relative error of at most 0.025.
Values may be sent and summed in bfloat16 or wider, within the bound.
A program may use at most 256 MiB of HBM per device.

```python
import math
import jax
import jax.numpy as jnp
import numpy as np
from jax import lax

MODEL_WIDTH = 1536
QUERY_HEADS = 24
KEY_VALUE_HEADS = 8
HEAD_SIZE = 64
FF = 512
TOPK = 8
PIECE_LEN = 256
PIECES = 2
EXPERTS = 20
SEQUENCE_TOKENS = 1024
TOK_DEV = 256
SEQS = 8
TOKENS = 8192
CAP = 128
N_EXPERT = 4


def draw_starts(key, part):
    span_len = SEQUENCE_TOKENS // PIECES
    offsets = jax.random.randint(key, (SEQS, PIECES), 0, span_len - PIECE_LEN + 1)
    return (offsets + jnp.arange(PIECES, dtype=jnp.int32)[None, :] * span_len).astype(jnp.int32)


def block_scale(rng, dims, split, least, top_value):
    level = 1.0
    for position, blocks in split:
        heights = jax.random.uniform(jax.random.fold_in(jax.random.fold_in(rng, 6), position), (blocks,), jnp.float32, least / len(split), top_value / len(split))
        level = level * jnp.repeat(jnp.exp(heights), dims[position] // blocks).reshape((-1,) + (1,) * (len(dims) - 1 - position))
    return level


def assign_block(stream_key, own, number, rows, amount, top, reach, skew):
    order = jax.random.permutation(stream_key, amount)
    packed, common = portions_of(amount, rows * top, reach, skew, True), portions_of(amount, rows * top, reach, skew, False)
    places = jnp.arange(amount)

    def named(sizes, turn):
        used = int((sizes > 0).sum())
        fixed = max(1, used // 4)
        moved = fixed + (places - fixed + turn * (used - fixed)) % max(1, amount - fixed)
        return jnp.zeros((amount,), jnp.int32).at[order[jnp.where(places < fixed, places, moved)]].set(jnp.asarray(sizes, jnp.int32))

    sizes = jnp.where(number % 4 == 0, named(packed, number // 4), named(common, number - number // 4 - 1))
    mixed = jax.random.permutation(jax.random.fold_in(own, 3), amount)
    donor, taker = mixed[0:amount // 2 * 2:2], mixed[1:amount // 2 * 2:2]
    slack = jnp.minimum(sizes[donor] - 1, reach - sizes[taker]) // 2
    slack = jnp.where((donor == order[0]) | (taker == order[0]) | (sizes[taker] == 0), 0, jnp.maximum(slack, 0))
    moved = jax.random.randint(jax.random.fold_in(own, 4), (amount // 2,), 0, 1 << 20) % (slack + 1)
    sizes = sizes.at[donor].add(-moved).at[taker].add(moved)
    members = jnp.searchsorted(jnp.cumsum(sizes), jnp.arange(rows * top), side="right").astype(jnp.int32)
    grid = members.reshape(top, rows).T
    grid = grid[jax.random.permutation(jax.random.fold_in(own, 1), rows)]
    turn = jax.random.randint(jax.random.fold_in(own, 2), (rows, 1), 0, top)
    return jnp.take_along_axis(grid, (jnp.arange(top)[None, :] + turn) % top, axis=1)


def portions_of(amount, total, limit, lean, full):
    loads = [(1 << 20) // math.isqrt(standing ** lean) + 1 for standing in range(1, amount + 1)]
    largest = limit if full else min(limit, max(-(-total // amount), total * loads[0] // sum(loads)))
    least = 1 if total - largest >= amount - 1 else 0
    counts, surplus = [largest] + [least] * (amount - 1), total - largest - least * (amount - 1)
    while surplus > 0:
        movable = [i for i in range(1, amount) if counts[i] < largest] or [i for i in range(1, amount) if counts[i] < limit]
        mass, budget = sum([loads[i] for i in movable]), surplus
        for i in movable:
            addition = min(limit - counts[i], max(1, budget * loads[i] // mass), surplus)
            counts[i] = counts[i] + addition
            surplus = surplus - addition
    return np.array(counts)


def centred(key, extent, spread, reach, cuts=(), held_as=jnp.bfloat16):
    level = block_scale(key, extent, cuts, -0.22, 0.18) if cuts else 1.0
    values = jax.random.normal(key, extent, jnp.float32) * spread * level
    return jnp.minimum(jnp.maximum(values, -reach), reach).astype(held_as)


def setup_inputs(seed: int = 0) -> dict:
    key_of = jax.random.split(jax.random.key(seed), 15)
    tokens = centred(key_of[0], (TOKENS, MODEL_WIDTH), 1.0, 6.0, ((0, 32),))
    attn_gain = jnp.clip(1.0 + 0.1 * jax.random.normal(key_of[1], (MODEL_WIDTH,), jnp.float32), 0.5, 1.5).astype(jnp.bfloat16)
    q_weight = centred(key_of[2], (MODEL_WIDTH, QUERY_HEADS * HEAD_SIZE), MODEL_WIDTH ** -0.5, 0.15625, ((0, 8),))
    key_matrix = centred(key_of[3], (MODEL_WIDTH, KEY_VALUE_HEADS * HEAD_SIZE), MODEL_WIDTH ** -0.5, 0.15625, ((0, 8),))
    value_matrix = centred(key_of[4], (MODEL_WIDTH, KEY_VALUE_HEADS * HEAD_SIZE), MODEL_WIDTH ** -0.5, 0.15625, ((0, 8),))
    o_weight = centred(key_of[5], (QUERY_HEADS * HEAD_SIZE, MODEL_WIDTH), HEAD_SIZE ** -0.5, 0.75, ((0, 8),))
    ffn_gain = jnp.clip(1.0 + 0.1 * jax.random.normal(key_of[6], (MODEL_WIDTH,), jnp.float32), 0.5, 1.5).astype(jnp.bfloat16)
    router_weight = centred(key_of[7], (MODEL_WIDTH, EXPERTS), (4 * MODEL_WIDTH) ** -0.5, 0.078125, ((0, 8),))
    expert_gate = centred(key_of[8], (EXPERTS, MODEL_WIDTH, FF), MODEL_WIDTH ** -0.5, 0.15625, ((0, 4), (1, 8)))
    expert_up = centred(key_of[9], (EXPERTS, MODEL_WIDTH, FF), MODEL_WIDTH ** -0.5, 0.15625, ((0, 4), (1, 8)))
    expert_down = centred(key_of[10], (EXPERTS, FF, MODEL_WIDTH), (FF // 16) ** -0.5, 1.0, ((0, 4), (1, 8)))
    routes_keys = jax.random.split(jax.random.fold_in(key_of[11], 1), TOKENS // TOK_DEV)
    routes_turns = jax.random.permutation(jax.random.fold_in(key_of[11], 3), TOKENS // TOK_DEV)
    routes = jax.vmap(lambda own, number: assign_block(jax.random.fold_in(key_of[11], 2), own, number, TOK_DEV, EXPERTS, TOPK, CAP, 1))(routes_keys, routes_turns).reshape((TOKENS, TOPK))
    starts = draw_starts(jax.random.fold_in(key_of[14], 71), 0)
    cotangent = centred(key_of[13], (TOKENS, MODEL_WIDTH), 1.0, 6.0, ((0, 32),))
    return dict(tokens=tokens, attn_gain=attn_gain, q_weight=q_weight, key_matrix=key_matrix, value_matrix=value_matrix, o_weight=o_weight, ffn_gain=ffn_gain, router_weight=router_weight, expert_gate=expert_gate, expert_up=expert_up, expert_down=expert_down, routes=routes, starts=starts, cotangent=cotangent)


EPSILON = 1e-05
THETA = 10000.0
HIGHEST = lax.Precision.HIGHEST

@jax.custom_vjp
def reduced_precision(v):
    return lax.optimization_barrier(v.astype(jnp.bfloat16)).astype(jnp.float32)

@jax.custom_vjp
def reduced_backward(v):
    return v

def low_keep(v):
    return (reduced_precision(v), None)

def low_pass(kept, grad):
    return (grad,)

def back_keep(v):
    return (v, None)

def back_low(kept, grad):
    return (reduced_precision(grad),)
reduced_precision.defvjp(low_keep, low_pass)
reduced_backward.defvjp(back_keep, back_low)

def matrix_product(left, right):
    return jnp.dot(left, right, precision=HIGHEST)

def rms_scale(value_rows, gain):
    return value_rows * lax.rsqrt(lax.optimization_barrier(jnp.mean(value_rows * value_rows, axis=-1, keepdims=True)) + EPSILON) * gain

def rotary_tables(positions):
    half_size = HEAD_SIZE // 2
    freqs = THETA ** (-(jnp.arange(half_size, dtype=jnp.float32) * 2.0 / HEAD_SIZE))
    angles = positions.astype(jnp.float32)[:, None] * freqs[None, :]
    return (jnp.cos(angles)[:, None, :], jnp.sin(angles)[:, None, :])

def rotate_halves_fn(value_rows, cosine_table, sine_values):
    half_size = value_rows.shape[-1] // 2
    first = value_rows[..., :half_size]
    second = value_rows[..., half_size:]
    return jnp.concatenate([first * cosine_table - second * sine_values, second * cosine_table + first * sine_values], axis=-1)

def piece_index(positions, starts_row):
    inside = (positions[:, None] >= starts_row[None, :]) & (positions[:, None] < starts_row[None, :] + PIECE_LEN)
    labels = jnp.arange(1, starts_row.shape[0] + 1, dtype=jnp.int32)[None, :]
    return lax.optimization_barrier(jnp.sum(jnp.where(inside, labels, 0), axis=-1)).astype(jnp.int32)

def visible(query_pos, query_piece, key_pos, key_piece):
    causal = key_pos[None, :] <= query_pos[:, None]
    shared = (query_piece[:, None] == key_piece[None, :]) & (query_piece[:, None] > 0)
    return causal | shared

def softmax_rows(scores):
    powers = jnp.exp(scores - lax.optimization_barrier(jnp.max(scores, axis=-1, keepdims=True)))
    return powers / lax.optimization_barrier(jnp.sum(powers, axis=-1, keepdims=True))

def slot_table(route_rows):
    flat_routes = route_rows.reshape(-1)
    picked = (flat_routes[:, None] == jnp.arange(EXPERTS, dtype=jnp.int32)[None, :]).astype(jnp.int32)
    ranks = lax.optimization_barrier(jnp.sum(jnp.cumsum(picked, axis=0) * picked, axis=-1)) - 1
    return (flat_routes * CAP + ranks).astype(jnp.int32)

def sequence_layer(weights, seq_rows, seq_routes, starts_row):
    gain_one, w_query, key_weight, value_weight, output_weight, gain_two, w_router, w_gate, w_up, w_down = weights
    first_norm = reduced_precision(rms_scale(seq_rows, gain_one))
    query_rows = reduced_backward(matrix_product(first_norm, w_query)).reshape(SEQUENCE_TOKENS, QUERY_HEADS, HEAD_SIZE)
    key_rows = reduced_backward(matrix_product(first_norm, key_weight)).reshape(SEQUENCE_TOKENS, KEY_VALUE_HEADS, HEAD_SIZE)
    value_rows = reduced_precision(reduced_backward(matrix_product(first_norm, value_weight))).reshape(SEQUENCE_TOKENS, KEY_VALUE_HEADS, HEAD_SIZE)
    positions = jnp.arange(SEQUENCE_TOKENS, dtype=jnp.int32)
    cosine_table, sine_values = rotary_tables(positions)
    query_rows = reduced_precision(rotate_halves_fn(query_rows, cosine_table, sine_values))
    key_rows = reduced_precision(rotate_halves_fn(key_rows, cosine_table, sine_values))
    pieces = piece_index(positions, starts_row)
    allowed = visible(positions, pieces, positions, pieces)
    grouped_rows = query_rows.reshape(SEQUENCE_TOKENS, KEY_VALUE_HEADS, QUERY_HEADS // KEY_VALUE_HEADS, HEAD_SIZE).transpose(1, 2, 0, 3)

    def head_group(inputs):
        q_group, k_group, v_group = inputs
        raw_scores = reduced_backward(jnp.einsum('rqd,kd->rqk', q_group, k_group, precision=HIGHEST))
        probs = reduced_precision(softmax_rows(jnp.where(allowed[None], raw_scores * HEAD_SIZE ** (-0.5), -1e+30)))
        return jnp.einsum('rqk,kd->rqd', probs, v_group, precision=HIGHEST)
    mixed = lax.map(jax.checkpoint(head_group), (grouped_rows, key_rows.transpose(1, 0, 2), value_rows.transpose(1, 0, 2)))
    attended = reduced_precision(reduced_backward(mixed.transpose(2, 0, 1, 3).reshape(SEQUENCE_TOKENS, QUERY_HEADS * HEAD_SIZE)))
    hidden = seq_rows + reduced_backward(matrix_product(attended, output_weight))
    norm_two = reduced_precision(rms_scale(hidden, gain_two))
    logits = reduced_backward(matrix_product(norm_two, w_router))
    picked = (seq_routes[:, :, None] == jnp.arange(EXPERTS, dtype=jnp.int32)[None, None, :]).astype(jnp.float32)
    gates = softmax_rows(lax.optimization_barrier(jnp.sum(picked * logits[:, None, :], axis=-1)))
    slots = jax.vmap(slot_table)(seq_routes.reshape(N_EXPERT, TOK_DEV, TOPK))
    block_base = jnp.arange(N_EXPERT, dtype=jnp.int32)[:, None] * (EXPERTS * CAP)
    flat_slots = (slots + block_base).reshape(-1).astype(jnp.int32)
    pair_rows = jnp.repeat(norm_two, TOPK, axis=0)
    buffer = jnp.zeros((N_EXPERT * EXPERTS * CAP, MODEL_WIDTH), jnp.float32).at[flat_slots].set(pair_rows)
    buffer = reduced_backward(buffer.reshape(N_EXPERT, EXPERTS, CAP, MODEL_WIDTH))
    gate_part = reduced_backward(jnp.einsum('becd,edf->becf', buffer, w_gate, precision=HIGHEST))
    up_part = reduced_backward(jnp.einsum('becd,edf->becf', buffer, w_up, precision=HIGHEST))
    active = reduced_precision(gate_part * jax.nn.sigmoid(gate_part) * up_part)
    result = reduced_precision(reduced_backward(jnp.einsum('becf,efd->becd', active, w_down, precision=HIGHEST)))
    pair_out = result.reshape(-1, MODEL_WIDTH)[flat_slots].reshape(SEQUENCE_TOKENS, TOPK, MODEL_WIDTH)
    return hidden + lax.optimization_barrier(jnp.sum(gates[:, :, None] * pair_out, axis=1))

def reference(tokens, attn_gain, q_weight, key_matrix, value_matrix, o_weight, ffn_gain, router_weight, expert_gate, expert_up, expert_down, routes, starts, cotangent):
    weights = tuple((weight.astype(jnp.float32) for weight in (attn_gain, q_weight, key_matrix, value_matrix, o_weight, ffn_gain, router_weight, expert_gate, expert_up, expert_down)))

    def forward(inputs, *params):
        seq_inputs = inputs.reshape(SEQS, SEQUENCE_TOKENS, MODEL_WIDTH)
        seq_routes = routes.reshape(SEQS, SEQUENCE_TOKENS, TOPK)

        def step(carried, items):
            return (carried, sequence_layer(params, items[0], items[1], items[2]))
        carried, outputs = lax.scan(jax.checkpoint(step), jnp.zeros((), jnp.float32), (seq_inputs, seq_routes, starts))
        return outputs.reshape(TOKENS, MODEL_WIDTH)
    result, pullback = jax.vjp(forward, tokens.astype(jnp.float32), *weights)
    grads = pullback(cotangent.astype(jnp.float32))
    return (result.astype(jnp.bfloat16), grads[0].astype(jnp.bfloat16), grads[1], grads[2], grads[3], grads[4], grads[5], grads[6], grads[7], grads[8], grads[9], grads[10])
```

```python
import functools

import jax
import jax.numpy as jnp
from jax import lax
from jax.experimental import pallas as pl
from jax.experimental.pallas import tpu as pltpu
from jax.sharding import PartitionSpec as P

MODEL_WIDTH = 1536
QUERY_HEADS = 24
KEY_VALUE_HEADS = 8
HEAD_SIZE = 64
TOPK = 8
PIECE_LEN = 256
EPSILON = 1e-05
THETA = 10000.0
BF16 = jnp.bfloat16
F32 = jnp.float32


def dot(left, right, dims=((1,), (0,))):
    return lax.dot_general(left, right, (dims, ((), ())), preferred_element_type=F32)


def dot_t(left, right):
    return dot(left, right, ((1,), (1,)))


def tdot(left, right):
    return dot(left, right, ((0,), (0,)))


DMA = pltpu.SemaphoreType.DMA
MESH = pl.DeviceIdType.MESH


def barrier_all(n, me):
    barrier = pltpu.get_barrier_semaphore()
    for d in range(n):

        @pl.when(d != me)
        def _():
            pl.semaphore_signal(barrier, inc=1, device_id={"expert": d}, device_id_type=MESH)

    pl.semaphore_wait(barrier, n - 1)


def remote(src, dst, send, recv, target):
    return pltpu.make_async_remote_copy(
        src_ref=src, dst_ref=dst, send_sem=send, recv_sem=recv,
        device_id={"expert": target}, device_id_type=MESH,
    )


class ChainGather:
    def __init__(self, n, me, slots, send, recv):
        self.n, self.me, self.slots, self.send, self.recv = n, me, slots, send, recv

    def copy(self, way, s, block, target):
        ref = self.slots.at[block]
        return remote(ref, ref, self.send.at[way, s], self.recv.at[way, s], target)

    def right(self, s):
        return self.copy(0, s, self.me - s, self.me + 1)

    def left(self, s):
        return self.copy(1, s, self.me + s, self.me - 1)

    def arrived(self, s):
        n, me = self.n, self.me

        @pl.when(me - 1 - s >= 0)
        def _():
            self.copy(0, s, me - 1 - s, me).wait_recv()

        @pl.when(me + 1 + s < n)
        def _():
            self.copy(1, s, me + 1 + s, me).wait_recv()

    def step(self, s):
        n, me = self.n, self.me
        if s >= 1:
            self.arrived(s - 1)

        @pl.when((me - s >= 0) & (me + 1 < n))
        def _():
            self.right(s).start()

        @pl.when((me + s < n) & (me > 0))
        def _():
            self.left(s).start()

    def finish(self):
        n, me = self.n, self.me
        self.arrived(n - 2)
        for s in range(n - 1):

            @pl.when((me - s >= 0) & (me + 1 < n))
            def _():
                self.right(s).wait_send()

            @pl.when((me + s < n) & (me > 0))
            def _():
                self.left(s).wait_send()


class Exchange:
    def __init__(self, n, me, source, slots, send, recv):
        self.n, self.me, self.source, self.slots = n, me, source, slots
        self.send, self.recv = send, recv

    def start(self, d):
        me = self.me

        @pl.when(d != me)
        def _():
            remote(
                self.source.at[d], self.slots.at[me], self.send.at[d], self.recv.at[me], d
            ).start()

    def finish(self):
        me = self.me
        for d in range(self.n):

            @pl.when(d != me)
            def _():
                desc = remote(
                    self.source.at[d], self.slots.at[d], self.send.at[d], self.recv.at[d], d
                )
                desc.wait_send()
                desc.wait_recv()


def chain_sems(n):
    return [pltpu.SemaphoreType.DMA((2, n - 1)), pltpu.SemaphoreType.DMA((2, n - 1))]


def direct_sems(n):
    return [pltpu.SemaphoreType.DMA((n,)), pltpu.SemaphoreType.DMA((n,))]


def call(kernel, outs, scratch, ident, name, flops, mib, args, far=()):
    vmem = pl.BlockSpec(memory_space=pltpu.VMEM)
    smem, anywhere = pl.BlockSpec(memory_space=pltpu.SMEM), pl.BlockSpec(memory_space=pl.ANY)
    nbytes = sum(a.size * a.dtype.itemsize for a in args)
    return pl.pallas_call(
        kernel,
        in_specs=[
            anywhere if j in far else smem if a.dtype == jnp.int32 else vmem
            for j, a in enumerate(args)
        ],
        out_specs=[vmem] * len(outs),
        out_shape=outs,
        scratch_shapes=scratch,
        compiler_params=pltpu.CompilerParams(
            collective_id=ident, has_side_effects=True, vmem_limit_bytes=mib * 1024 * 1024
        ),
        cost_estimate=pl.CostEstimate(flops=flops, transcendentals=0, bytes_accessed=nbytes),
        name=name,
    )(*args)


def gather_kernel(n, tokens_ref, chosen_ref, all_ref, every_ref, source, s0, r0, s1, r1):
    me = lax.axis_index("expert")
    barrier_all(n, me)
    all_ref[me] = tokens_ref[...]
    chain = ChainGather(n, me, all_ref, s0, r0)
    chain.step(0)
    every_ref[me] = chosen_ref[...]
    for d in range(n):
        source[d] = chosen_ref[...]
    small = Exchange(n, me, source, every_ref, s1, r1)
    for d in range(n):
        small.start(d)
    for s in range(1, n - 1):
        chain.step(s)
    chain.finish()
    small.finish()


def gather_tokens(n, tokens, chosen):
    rows, width = tokens.shape
    return call(
        functools.partial(gather_kernel, n),
        [
            jax.ShapeDtypeStruct((n, rows, width), BF16),
            jax.ShapeDtypeStruct((n,) + chosen.shape, F32),
        ],
        [pltpu.VMEM((n,) + chosen.shape, F32)] + chain_sems(n) + direct_sems(n),
        1, "gather_tokens", 10**6, 16, (tokens, chosen),
    )


def turn(x, cosine, sine):
    half = HEAD_SIZE // 2
    tiles = []
    for c in range(0, x.shape[1], 128):
        tile = x[:, c : c + 128]
        lane = lax.broadcasted_iota(jnp.int32, tile.shape, 1) % HEAD_SIZE
        other = jnp.where(lane < half, pltpu.roll(tile, 128 - half, 1), pltpu.roll(tile, half, 1))
        tiles.append(tile * cosine + other * sine)
    return jnp.concatenate(tiles, axis=1)


def bias_rows(starts_ref, q_pos, k_pos):
    seen = k_pos <= q_pos
    for k in range(starts_ref.shape[1]):
        a = starts_ref[0, k]
        q_in = (q_pos >= a) & (q_pos < a + PIECE_LEN)
        k_in = (k_pos >= a) & (k_pos < a + PIECE_LEN)
        seen = seen | (q_in & k_in)
    return jnp.where(seen, 0.0, -1e30)


def reach_of(block, rows, length, pieces):
    span = length // pieces
    return min(length, -(-((block + 1) * rows) // span) * span)


def attend_kernel(
    n, kv_local, tokens_ref, packed_ref, cos_ref, sin_ref, starts_ref, cot_ref,
    norm_ref, q_ref, k_ref, v_ref, lse_ref, out_ref, att_ref, cots_ref, small_ref,
    w_s, send_att, load, s0, r0, s1, r1,
):
    me = lax.axis_index("expert")
    per_key, length, tile = q_ref.shape
    rows = length // n
    q_cols, k_cols = per_key * tile, tile
    width, wide = w_s.shape
    weights = pltpu.make_async_copy(packed_ref.at[:, pl.ds(width, wide)], w_s, load)
    weights.start()
    barrier_all(n, me)
    cots_ref[me] = cot_ref[...]
    chain = ChainGather(n, me, cots_ref, s0, r0)
    chain.step(0)
    swap = Exchange(n, me, send_att, att_ref, s1, r1)
    pieces = starts_ref.shape[1]
    weights.wait()
    small = w_s[:, wide - 128 :].astype(F32).T
    small_ref[...] = small[: small_ref.shape[0], :]
    gain = small[:1, :]
    lane = lax.broadcasted_iota(jnp.int32, (rows, tile), 1)
    lane_w = lax.broadcasted_iota(jnp.int32, (rows, 128), 1)
    for i in range(n):
        part = slice(i * rows, (i + 1) * rows)
        x = tokens_ref[i].astype(F32)
        inverse = lax.rsqrt(jnp.mean(x * x, axis=1, keepdims=True) + EPSILON)
        norm = (x * inverse * gain).astype(BF16)
        norm_ref[i] = norm
        qkv = dot(norm, w_s[:, : wide - 128])
        qk = turn(qkv[:, : q_cols + k_cols], cos_ref[part, :], sin_ref[part, :]).astype(BF16)
        v_ref[part, :] = qkv[:, q_cols + k_cols : q_cols + 2 * k_cols].astype(BF16)
        k_ref[part, :] = qk[:, q_cols:]
        q = (qk[:, :q_cols].astype(F32) * HEAD_SIZE ** (-0.5)).astype(BF16)
        for t in range(per_key):
            for g in range(kv_local):
                at = (g * per_key + t) * HEAD_SIZE
                q_ref[t, part, g * HEAD_SIZE : (g + 1) * HEAD_SIZE] = q[:, at : at + HEAD_SIZE]
    if n > 2:
        chain.step(1)
    for i in range(n):
        reach = reach_of(i, rows, length, pieces)
        part = slice(i * rows, (i + 1) * rows)
        q_pos = lax.broadcasted_iota(jnp.int32, (rows, reach), 0) + i * rows
        k_pos = lax.broadcasted_iota(jnp.int32, (rows, reach), 1)
        bias = bias_rows(starts_ref, q_pos, k_pos)
        keys, values = k_ref[:reach, :], v_ref[:reach, :]
        k_lane = lax.broadcasted_iota(jnp.int32, (reach, tile), 1)

        def head(t, logs):
            q = q_ref[t, part, :]
            total = jnp.zeros((rows, tile), F32)
            for g in range(kv_local):
                mine = lane // HEAD_SIZE == g
                scores = dot_t(jnp.where(mine, q, jnp.zeros_like(q)), keys) + bias
                top = jnp.max(scores, axis=1, keepdims=True)
                powers = jnp.exp(scores - top)
                norm = jnp.sum(powers, axis=1, keepdims=True)
                value = jnp.where(k_lane // HEAD_SIZE == g, values, jnp.zeros_like(values))
                total = total + dot(powers.astype(BF16), value) * (1.0 / norm)
                logs = jnp.where(lane_w == t * kv_local + g, top + jnp.log(norm), logs)
            out_ref[t, part, :] = total
            return logs

        logs = lax.fori_loop(0, per_key, head, jnp.zeros((rows, 128), F32))
        lse_ref[:, part] = logs.T[: lse_ref.shape[0], :]
        for t in range(per_key):
            for g in range(kv_local):
                at = (g * per_key + t) * HEAD_SIZE
                send_att[i, :, at : at + HEAD_SIZE] = out_ref[
                    t, part, g * HEAD_SIZE : (g + 1) * HEAD_SIZE
                ].astype(BF16)
        swap.start(i)
        if i + 2 < n - 1:
            chain.step(i + 2)
    att_ref[me] = send_att[me]
    chain.finish()
    swap.finish()


def attend(n, kv_local, tokens_all, packed, cosine, sine, starts, cot):
    rows, width = cot.shape
    length = n * rows
    tile = kv_local * HEAD_SIZE
    per_key = QUERY_HEADS // KEY_VALUE_HEADS
    q_cols = per_key * tile
    wide = packed.shape[1] - width
    sds = jax.ShapeDtypeStruct
    lse_rows = -(-per_key * kv_local // 8) * 8
    return call(
        functools.partial(attend_kernel, n, kv_local),
        [
            sds((n, rows, width), BF16),
            sds((per_key, length, tile), BF16),
            sds((length, tile), BF16),
            sds((length, tile), BF16),
            sds((lse_rows, length), F32),
            sds((per_key, length, tile), F32),
            sds((n, rows, q_cols), BF16),
            sds((n, rows, width), BF16),
            sds((8 + 8 * n, width), F32),
        ],
        [pltpu.VMEM((width, wide), BF16), pltpu.VMEM((n, rows, q_cols), BF16), DMA]
        + chain_sems(n)
        + direct_sems(n),
        2, "attend", 5 * 10**9, 44, (tokens_all, packed, cosine, sine, starts, cot), (1,),
    )


def mix_kernel(
    n, tokens_ref, att_ref, packed_ref, small_ref, hidden_ref, norms_ref, own_ref, w_s, load, s0, r0
):
    me = lax.axis_index("expert")
    q_cols = att_ref.shape[2]
    width = w_s.shape[0]
    weights = pltpu.make_async_copy(packed_ref.at[:, pl.ds(0, width)], w_s, load)
    weights.start()
    hidden = tokens_ref[...].astype(F32)
    weights.wait()
    for s in range(n):
        hidden = hidden + dot(att_ref[s], w_s[s * q_cols : (s + 1) * q_cols, :])
    hidden_ref[...] = hidden
    inverse = lax.rsqrt(jnp.mean(hidden * hidden, axis=1, keepdims=True) + EPSILON)
    norm = (hidden * inverse * small_ref[1:2, :]).astype(BF16)
    own_ref[...] = norm
    barrier_all(n, me)
    norms_ref[me] = norm
    chain = ChainGather(n, me, norms_ref, s0, r0)
    for s in range(n - 1):
        chain.step(s)
    chain.finish()


def mix(n, tokens, att, packed, small):
    rows, width = tokens.shape
    sds = jax.ShapeDtypeStruct
    return call(
        functools.partial(mix_kernel, n),
        [sds((rows, width), F32), sds((n, rows, width), BF16), sds((rows, width), BF16)],
        [pltpu.VMEM((width, width), BF16), DMA] + chain_sems(n),
        3, "mix", 2 * 10**9, 32, (tokens, att, packed, small), (2,),
    )


class ChainReduce:
    def __init__(self, n, me, parts, from_left, from_right, send, recv):
        self.n, self.me, self.parts = n, me, parts
        self.slots, self.send, self.recv = (from_left, from_right), send, recv

    def copy(self, way, s, d, source):
        target = self.me + 1 if way == 0 else self.me - 1
        return remote(
            source.at[d], self.slots[way].at[d], self.send.at[way, s], self.recv.at[way, s], target
        )

    def step(self, s):
        n, me = self.n, self.me
        for way in (0, 1):
            d = n - 1 - s if way == 0 else s
            onward = me < d if way == 0 else me > d
            first = me == 0 if way == 0 else me == n - 1
            slot = self.slots[way]

            @pl.when(onward & first)
            def _():
                if s > 0:
                    self.copy(way, s - 1, d, self.parts).wait_send()
                self.copy(way, s, d, self.parts).start()

            @pl.when(onward & jnp.logical_not(first))
            def _():
                self.copy(way, s, d, slot).wait_recv()
                slot[d] = (slot[d].astype(F32) + self.parts[d].astype(F32)).astype(BF16)
                if s > 0:
                    self.copy(way, s - 1, d, slot).wait_send()
                self.copy(way, s, d, slot).start()

    def finish(self, total):
        n, me = self.n, self.me
        total[...] = self.parts[me].astype(F32)
        for way in (0, 1):
            last = n - 1 - me if way == 0 else me
            slot = self.slots[way]

            @pl.when(me > 0 if way == 0 else me < n - 1)
            def _():
                self.copy(way, last, me, slot).wait_recv()
                total[...] += slot[me].astype(F32)

            @pl.when(me < n - 1 if way == 0 else me > 0)
            def _():
                self.copy(way, last - 1, me, slot).wait_send()


def rms_back(grad, rows, gain):
    inverse = lax.rsqrt(jnp.mean(rows * rows, axis=1, keepdims=True) + EPSILON)
    scaled = grad * gain
    grad_gain = jnp.sum(grad * rows * inverse, axis=0, keepdims=True)
    mean = jnp.mean(scaled * rows, axis=1, keepdims=True)
    return inverse * scaled - rows * (inverse * inverse * inverse * mean), grad_gain


def softmax_chosen(logits, chosen):
    top = jnp.max(jnp.where(chosen > 0.0, logits, -1e30), axis=0, keepdims=True)
    powers = jnp.where(chosen > 0.0, jnp.exp(jnp.where(chosen > 0.0, logits - top, 0.0)), 0.0)
    return powers / jnp.sum(powers, axis=0, keepdims=True)


def return_kernel(
    n, parts_ref, gg_ref, chosen_ref, small_ref, hidden_ref, norm_ref, cot_ref, att_ref, packed_ref,
    grad_ref, ga_ref, o_ref, extra_ref,
    w_s, from_left, from_right, total, gg_s, send_ga, load, s0, r0, s1, r1, s2, r2,
):
    me = lax.axis_index("expert")
    width = w_s.shape[0]
    q_cols = ga_ref.shape[2]
    weights = pltpu.make_async_copy(packed_ref.at[:, pl.ds(0, width)], w_s, load)
    weights.start()
    barrier_all(n, me)
    chain = ChainReduce(n, me, parts_ref, from_left, from_right, s0, r0)
    chain.step(0)
    gates_swap = Exchange(n, me, gg_ref, gg_s, s1, r1)
    for d in range(n):
        gates_swap.start(d)
    gg_s[me] = gg_ref[me]
    router = small_ref[8:, :].astype(BF16)
    gates = softmax_chosen(dot_t(router, norm_ref[...]), chosen_ref[...])
    gates_swap.finish()
    grad_gates = gg_s[...].reshape(gates.shape)
    middle = jnp.sum(gates * grad_gates, axis=0, keepdims=True)
    grad_logits = (gates * (grad_gates - middle)).astype(BF16)
    extra_ref[8:, :] = dot(grad_logits, norm_ref[...])
    for s in range(1, n - 1):
        chain.step(s)
    chain.finish(total)
    grad_norm = total[...] + tdot(grad_logits, router)
    grad, grad_gain = rms_back(grad_norm, hidden_ref[...], small_ref[1:2, :])
    row = lax.broadcasted_iota(jnp.int32, (8, width), 0)
    extra_ref[:8, :] = jnp.where(row == 1, grad_gain, 0.0)
    grad = cot_ref[...].astype(F32) + grad
    grad_ref[...] = grad
    proj = grad.astype(BF16)
    weights.wait()
    swap = Exchange(n, me, send_ga, ga_ref, s2, r2)
    for d in range(n):
        send_ga[d] = dot_t(proj, w_s[d * q_cols : (d + 1) * q_cols, :]).astype(BF16)
        swap.start(d)
    ga_ref[me] = send_ga[me]
    for d in range(n):
        o_ref[d * q_cols : (d + 1) * q_cols, :] = tdot(att_ref[d], proj).astype(BF16)
    swap.finish()


def give_back(n, parts, gg, chosen, small, hidden, norm, cot, att, packed):
    rows, width = cot.shape
    q_cols = att.shape[2]
    sds, vm = jax.ShapeDtypeStruct, pltpu.VMEM
    return call(
        functools.partial(return_kernel, n),
        [
            sds((rows, width), F32), sds(att.shape, BF16), sds((width, width), BF16),
            sds(small.shape, F32),
        ],
        [
            vm((width, width), BF16), vm((n, rows, width), BF16), vm((n, rows, width), BF16),
            vm((rows, width), F32), vm(gg.shape, F32), vm((n, rows, q_cols), BF16), DMA,
        ]
        + chain_sems(n) + direct_sems(n) + direct_sems(n),
        4, "give_back", 4 * 10**9, 48,
        (parts, gg, chosen, small, hidden, norm, cot, att, packed), (8,),
    )


def attend_back_kernel(
    n, kv_local, q_ref, k_ref, v_ref, lse_ref, out_ref, ga_ref, starts_ref, cos_ref, sin_ref,
    norm_ref, packed_ref, tokens_ref, small_ref, grad_ref, hidden_ref, y_ref, extra_ref,
    output_ref, input_ref, dw_ref,
    w_s, gq_s, gk_s, gv_s, gqkv_s, ga_s, parts_s, y_left, y_right, b_left, b_right, total, load,
    s0, r0, s1, r1,
):
    me = lax.axis_index("expert")
    per_key, length, tile = q_ref.shape
    rows = length // n
    q_cols, k_cols = per_key * tile, tile
    width, wide = w_s.shape
    used = q_cols + 2 * k_cols
    scale = HEAD_SIZE ** (-0.5)
    pieces = starts_ref.shape[1]
    weights = pltpu.make_async_copy(packed_ref.at[:, pl.ds(width, wide)], w_s, load)
    weights.start()
    barrier_all(n, me)
    y_chain = ChainReduce(n, me, y_ref, y_left, y_right, s0, r0)
    y_chain.step(0)
    gk_s[...] = jnp.zeros_like(gk_s)
    gv_s[...] = jnp.zeros_like(gv_s)
    lane = lax.broadcasted_iota(jnp.int32, (rows, tile), 1)
    lane_w = lax.broadcasted_iota(jnp.int32, (rows, 128), 1)
    for i in range(n):
        reach = reach_of(i, rows, length, pieces)
        part = slice(i * rows, (i + 1) * rows)
        deltas = jnp.zeros((rows, 128), F32)
        for t in range(per_key):
            for g in range(kv_local):
                at = (g * per_key + t) * HEAD_SIZE
                ga_s[t, :, g * HEAD_SIZE : (g + 1) * HEAD_SIZE] = ga_ref[i, :, at : at + HEAD_SIZE]
            product = ga_s[t].astype(F32) * out_ref[t, part, :]
            for g in range(kv_local):
                own = jnp.where(lane // HEAD_SIZE == g, product, 0.0)
                deltas = jnp.where(
                    lane_w == t * kv_local + g, jnp.sum(own, axis=1, keepdims=True), deltas
                )
        delta_s = deltas.T
        k_pos = lax.broadcasted_iota(jnp.int32, (reach, rows), 0)
        q_pos = lax.broadcasted_iota(jnp.int32, (reach, rows), 1) + i * rows
        bias = bias_rows(starts_ref, q_pos, k_pos)
        keys, values = k_ref[:reach, :], v_ref[:reach, :]
        k_lane = lax.broadcasted_iota(jnp.int32, (reach, tile), 1)
        for t in range(per_key):
            q, ga = q_ref[t, part, :], ga_s[t]
            grad_q = jnp.zeros((rows, tile), F32)
            for g in range(kv_local):
                h = t * kv_local + g
                mine = lane // HEAD_SIZE == g
                q_g = jnp.where(mine, q, jnp.zeros_like(q))
                ga_g = jnp.where(mine, ga, jnp.zeros_like(ga))
                scores = dot_t(keys, q_g) + bias
                probs = jnp.exp(scores - lse_ref[h : h + 1, part])
                grad_probs = dot_t(values, ga_g)
                grad_raw = (probs * (grad_probs - delta_s[h : h + 1, :])).astype(BF16)
                gk_s[:reach, :] += dot(grad_raw, q_g)
                gv_s[:reach, :] += dot(probs.astype(BF16), ga_g)
                key = jnp.where(k_lane // HEAD_SIZE == g, keys, jnp.zeros_like(keys))
                grad_q = grad_q + tdot(grad_raw, key)
            for g in range(kv_local):
                at = (g * per_key + t) * HEAD_SIZE
                gq_s[part, at : at + HEAD_SIZE] = (
                    grad_q[:, g * HEAD_SIZE : (g + 1) * HEAD_SIZE] * scale
                )
        if i + 1 < n - 1:
            y_chain.step(i + 1)
    gq_s[:, q_cols:] = gk_s[...]
    weights.wait()
    if used < gqkv_s.shape[1]:
        gqkv_s[...] = jnp.zeros_like(gqkv_s)
    for i in range(n):
        part = slice(i * rows, (i + 1) * rows)
        qk = turn(gq_s[part, :], cos_ref[part, :], -sin_ref[part, :]).astype(BF16)
        gqkv_s[part, : q_cols + k_cols] = qk
        gqkv_s[part, q_cols + k_cols : used] = gv_s[part, :].astype(BF16)
        parts_s[i] = dot_t(gqkv_s[part, :], w_s[:, : wide - 128]).astype(BF16)
    chain = ChainReduce(n, me, parts_s, b_left, b_right, s1, r1)
    chain.step(0)
    y_chain.finish(total)
    output_ref[...] = (hidden_ref[...] + total[...]).astype(BF16)
    norms = norm_ref[...].reshape(length, width)
    dw_ref[:, : wide - 128] = tdot(norms, gqkv_s[...]).astype(BF16)
    for s in range(1, n - 1):
        chain.step(s)
    chain.finish(total)
    grad, grad_gain = rms_back(total[...], tokens_ref[...].astype(F32), small_ref[:1, :])
    input_ref[...] = (grad_ref[...] + grad).astype(BF16)
    extra = extra_ref[...]
    row = lax.broadcasted_iota(jnp.int32, extra.shape, 0)
    extra = jnp.where(row == 0, grad_gain, extra)
    extra = jnp.concatenate([extra, jnp.zeros((128 - extra.shape[0], width), F32)], axis=0)
    dw_ref[:, wide - 128 :] = extra.T.astype(BF16)


def attend_back(n, kv_local, saved, ga, starts, cosine, sine, norms, packed, tokens, small, grad, hidden, y, extra):
    q, k, v, lse, out = saved
    rows, width = tokens.shape
    per_key, length, tile = q.shape
    wide = packed.shape[1] - width
    sds, vm = jax.ShapeDtypeStruct, pltpu.VMEM
    qk = (per_key + 1) * tile
    block = vm((n, rows, width), BF16)
    return call(
        functools.partial(attend_back_kernel, n, kv_local),
        [sds((rows, width), BF16), sds((rows, width), BF16), sds((width, wide), BF16)],
        [
            vm((width, wide), BF16), vm((length, qk), F32), vm((length, tile), F32),
            vm((length, tile), F32), vm((length, wide - 128), BF16), vm((per_key, rows, tile), BF16),
            block, block, block, block, block, vm((rows, width), F32), DMA,
        ]
        + chain_sems(n) + chain_sems(n),
        5, "attend_back", 10 * 10**9, 58,
        (q, k, v, lse, out, ga, starts, cosine, sine, norms, packed, tokens, small, grad, hidden, y, extra),
        (10,),
    )


def expert_kernel(
    member_ref, chosen_ref, small_ref, n2_ref, cot_ref, wg_ref, wu_ref, wd_ref,
    dw_ref, y_ref, gx_ref, gg_ref,
    xe, ge, gr, act_s, ggp_s, gup_s, pick_s, gated_s, grows_s, gate_s, rank_s,
):
    e, phase = pl.program_id(0), pl.program_id(1)
    groups, rows, width = n2_ref.shape
    cap = xe.shape[0] // groups
    ff = act_s.shape[1]
    shards = wg_ref.shape[0]
    depth = ff // shards
    blocks = width // ff

    def whole(ref):
        return ref[...].reshape(width, ff)

    def down(j):
        return wd_ref[:, 0, j * depth:(j + 1) * depth, :].reshape(ff, ff)

    @pl.when((phase == 0) & (e == 0))
    def _():
        before = lax.broadcasted_iota(jnp.int32, (rows, rows), 0)
        upto = jnp.where(before <= lax.broadcasted_iota(jnp.int32, (rows, rows), 1), 1.0, 0.0)
        router = small_ref[8:, :].astype(BF16)
        for s in range(groups):
            chosen = chosen_ref[s]
            gate_s[s] = softmax_chosen(dot_t(router, n2_ref[s]), chosen)
            count = dot(chosen.astype(BF16), upto.astype(BF16))
            rank_s[s] = jnp.where(chosen > 0.0, count - 1.0, -1.0).astype(jnp.int32)
        gg_ref[...] = jnp.zeros_like(gg_ref)

    @pl.when(phase == 0)
    def _():
        mine = member_ref[0] * gg_ref.shape[1] + e
        picks, cols = [], []
        slot = lax.broadcasted_iota(jnp.int32, (cap, rows), 0)
        for s in range(groups):
            pick = slot == rank_s[s, pl.ds(mine, 1), :]
            picks.append(pick)
            hot = jnp.where(pick, 1.0, 0.0).astype(BF16)
            pick_s[s, pl.ds(pl.multiple_of(e * cap, cap), cap), :] = hot
            col = jnp.sum(jnp.where(pick, gate_s[s, pl.ds(mine, 1), :], 0.0), axis=1, keepdims=True)
            cols.append(col)
            part = slice(s * cap, (s + 1) * cap)
            xe[part, :] = dot(hot, n2_ref[s]).astype(BF16)
            g = dot(hot, cot_ref[s])
            ge[part, :] = g.astype(BF16)
            gr[part, :] = (col * g).astype(BF16)
        x = xe[...]
        gp = dot(x, whole(wg_ref))
        up = dot(x, whole(wu_ref))
        sigma = jax.nn.sigmoid(gp)
        silu = gp * sigma
        act = (silu * up).astype(BF16)
        act_s[...] = act
        grad_act = jnp.zeros_like(gp)
        gate_sums = [jnp.zeros((cap, 1), F32) for _ in range(groups)]
        for j in range(blocks):
            lanes = slice(j * ff, (j + 1) * ff)
            w = down(j)
            res = dot(act, w).astype(BF16).astype(F32)
            grad_act = grad_act + dot_t(gr[:, lanes], w)
            for s in range(groups):
                part = slice(s * cap, (s + 1) * cap)
                r = res[part, :]
                gated_s[s, pl.ds(pl.multiple_of(e * cap, cap), cap), lanes] = (cols[s] * r).astype(BF16)
                gate_sums[s] = gate_sums[s] + jnp.sum(ge[part, lanes].astype(F32) * r, axis=1, keepdims=True)
        for s in range(groups):
            gg_ref[s, pl.ds(e, 1), :] = jnp.sum(jnp.where(picks[s], gate_sums[s], 0.0), axis=0, keepdims=True)
        ggp = (grad_act * up * sigma * (1.0 + gp * (1.0 - sigma))).astype(BF16)
        ggp_s[...] = ggp
        gup_s[...] = (grad_act * silu).astype(BF16)
        dw_ref[...] = tdot(xe[...], ggp).astype(BF16).reshape(dw_ref.shape)

    @pl.when(phase == 1)
    def _():
        dw_ref[...] = tdot(xe[...], gup_s[...]).astype(BF16).reshape(dw_ref.shape)
        grows = (dot_t(ggp_s[...], whole(wg_ref)) + dot_t(gup_s[...], whole(wu_ref))).astype(BF16)
        for s in range(groups):
            grows_s[s, pl.ds(pl.multiple_of(e * cap, cap), cap), :] = grows[s * cap:(s + 1) * cap, :]

    @pl.when(phase == 2)
    def _():
        for j in range(blocks):
            lanes = slice(j * ff, (j + 1) * ff)
            dw_ref[:, 0, j * depth:(j + 1) * depth, :] = tdot(act_s[...], gr[:, lanes]).astype(BF16).reshape(shards, depth, ff)

    @pl.when((phase == 2) & (e == pl.num_programs(0) - 1))
    def _():
        for s in range(groups):
            y_ref[s] = tdot(pick_s[s], gated_s[s]).astype(BF16)
            gx_ref[s] = tdot(pick_s[s], grows_s[s]).astype(BF16)


def experts(member, chosen, small, n2, cot, w):
    groups, rows, width = n2.shape
    shards, local, depth, ff = w.shape
    local = local // 3
    cap = rows * TOPK * 5 // (4 * local * groups)
    tall = groups * cap
    padded = chosen.shape[1] // groups
    once = pl.Buffered(1)

    def const(shape):
        return pl.BlockSpec(shape, lambda e, p: (0,) * len(shape), pipeline_mode=once)

    def weight(k):
        return pl.BlockSpec((shards, 1, depth, ff), lambda e, p: (0, k * local + e, 0, 0))

    sds, vm = jax.ShapeDtypeStruct, pltpu.VMEM
    return pl.pallas_call(
        expert_kernel,
        grid=(local, 3),
        in_specs=[
            pl.BlockSpec(memory_space=pltpu.SMEM), const(chosen.shape), const(small.shape),
            const(n2.shape), const(n2.shape), weight(0), weight(1), weight(2),
        ],
        out_specs=[
            pl.BlockSpec((shards, 1, depth, ff), lambda e, p: (0, p * local + e, 0, 0)),
            const(n2.shape), const(n2.shape), const((groups, padded, rows)),
        ],
        out_shape=[
            sds(w.shape, BF16), sds(n2.shape, BF16), sds(n2.shape, BF16),
            sds((groups, padded, rows), F32),
        ],
        scratch_shapes=[
            vm((tall, width), BF16), vm((tall, width), BF16), vm((tall, width), BF16),
            vm((tall, ff), BF16), vm((tall, ff), BF16), vm((tall, ff), BF16),
            vm((groups, local * cap, rows), BF16), vm((groups, local * cap, width), BF16),
            vm((groups, local * cap, width), BF16), vm(chosen.shape, F32),
            vm(chosen.shape, jnp.int32),
        ],
        compiler_params=pltpu.CompilerParams(
            vmem_limit_bytes=60 * 1024 * 1024, dimension_semantics=("arbitrary", "arbitrary")
        ),
        cost_estimate=pl.CostEstimate(
            flops=40 * 10**9, transcendentals=0, bytes_accessed=60 * 10**6
        ),
        name="experts",
    )(member, chosen, small, n2, cot, w, w, w)


def per_device(
    tokens, attn_gain, q_weight, key_matrix, value_matrix, o_weight, ffn_gain, router_weight,
    expert_gate, expert_up, expert_down, routes, starts, cotangent,
):
    n = lax.axis_size("expert")
    member = lax.axis_index("expert")
    rows, width = tokens.shape
    length = rows * n
    kv_local = KEY_VALUE_HEADS // n
    q_cols = QUERY_HEADS // n * HEAD_SIZE
    k_cols = kv_local * HEAD_SIZE
    local, shard, ff = expert_gate.shape
    depth = expert_down.shape[1]
    blocks = width // ff
    padded = -(-local // 8) * 8

    wq = lax.dynamic_slice_in_dim(q_weight, member * q_cols, q_cols, 1)
    wk = lax.dynamic_slice_in_dim(key_matrix, member * k_cols, k_cols, 1)
    wv = lax.dynamic_slice_in_dim(value_matrix, member * k_cols, k_cols, 1)
    wide = width // 2
    used = q_cols + 2 * k_cols
    router = jnp.pad(
        router_weight.reshape(shard, n, local), ((0, 0), (0, 0), (0, padded - local))
    ).reshape(shard, n * padded)
    gains = jnp.stack([attn_gain, ffn_gain], axis=1)
    gap = jnp.zeros((shard, wide - 128 - used), BF16)
    packed = jnp.concatenate(
        [
            o_weight, wq, wk, wv, gap, jnp.pad(gains, ((0, 0), (0, 6))), router,
            jnp.zeros((shard, 120 - n * padded), BF16),
        ],
        axis=1,
    )
    packed = lax.all_gather(packed, "dp").reshape(width, -1)
    down_rows = expert_down.reshape(local, depth, blocks, ff).transpose(0, 2, 1, 3)
    stacked = jnp.concatenate(
        [expert_gate, expert_up, down_rows.reshape(local, shard, ff)], axis=0
    )
    experts_w = lax.all_gather(stacked, "dp")

    hot = routes[:, :, None] == jnp.arange(n * local, dtype=jnp.int32)
    chosen = jnp.any(hot, axis=1).astype(F32).T.reshape(n, local, rows)
    chosen = jnp.pad(chosen, ((0, 0), (0, padded - local), (0, 0))).reshape(n * padded, rows)
    half = HEAD_SIZE // 2
    freqs = THETA ** (-(jnp.arange(half, dtype=F32) * 2.0 / HEAD_SIZE))
    angles = jnp.arange(length, dtype=jnp.int32).astype(F32)[:, None] * freqs[None, :]
    cosine, sine = jnp.cos(angles), jnp.sin(angles)
    cosine = jnp.concatenate([cosine, cosine, cosine, cosine], axis=1)
    sine = jnp.concatenate([-sine, sine, -sine, sine], axis=1)

    tokens_all, chosen_all = gather_tokens(n, tokens, chosen)
    norms, q, k, v, lse, out, att, cots, small = attend(
        n, kv_local, tokens_all, packed, cosine, sine, starts, cotangent
    )
    hidden, twos, two = mix(n, tokens, att, packed, small)
    grad_experts, y, back, gg = experts(
        member.astype(jnp.int32)[None], chosen_all, small, twos, cots, experts_w
    )
    expert_grads = lax.psum_scatter(grad_experts, "dp", scatter_dimension=0).astype(F32)
    gate_grad, up_grad = expert_grads[:local], expert_grads[local : 2 * local]
    down_grad = expert_grads[2 * local :].reshape(local, blocks, depth, ff)
    down_grad = down_grad.transpose(0, 2, 1, 3).reshape(local, depth, width)
    grad_hidden, ga, grad_o, extra = give_back(
        n, back, gg, chosen, small, hidden, two, cotangent, att, packed
    )
    grad_o = lax.psum_scatter(grad_o.reshape(-1, shard, width), "dp", scatter_dimension=0)
    output, input_grad, grad_w = attend_back(
        n, kv_local, (q, k, v, lse, out), ga, starts, cosine, sine, norms, packed, tokens, small,
        grad_hidden, hidden, y, extra,
    )
    grad_w = lax.psum_scatter(grad_w.reshape(-1, shard, wide), "dp", scatter_dimension=0)
    o_grad = lax.psum(grad_o, "expert").astype(F32)
    shares = lax.all_gather(grad_w, "expert").astype(F32)
    q_grad = shares[:, :, :q_cols].transpose(1, 0, 2).reshape(shard, -1)
    k_grad = shares[:, :, q_cols : q_cols + k_cols].transpose(1, 0, 2).reshape(shard, -1)
    v_grad = shares[:, :, q_cols + k_cols : used].transpose(1, 0, 2).reshape(shard, -1)
    rest = jnp.sum(shares[:, :, wide - 128 :], axis=0)
    router_grad = rest[:, 8 : 8 + n * padded].reshape(shard, n, padded)[:, :, :local]
    return (
        output, input_grad, rest[:, 0], q_grad, k_grad, v_grad, o_grad, rest[:, 1],
        router_grad.reshape(shard, n * local), gate_grad, up_grad, down_grad,
    )


def solution(mesh):
    rows, split, expert = P(("dp", "expert"), None), P("dp", None), P("expert", "dp", None)
    return jax.shard_map(
        per_device,
        mesh=mesh,
        in_specs=(
            rows, P("dp"), split, split, split, split, P("dp"), split,
            expert, expert, expert, rows, split, rows,
        ),
        out_specs=(
            rows, rows, P("dp"), split, split, split, split, P("dp"), split,
            expert, expert, expert,
        ),
        check_vma=False,
    )
```

```python
import functools

import jax
import jax.numpy as jnp
import numpy as np
from jax import lax
from jax.experimental import pallas as pl
from jax.experimental.pallas import tpu as pltpu
from jax.sharding import PartitionSpec as P

MODEL_WIDTH = 1536
QUERY_HEADS = 24
KEY_VALUE_HEADS = 8
HEAD_SIZE = 64
TOPK = 8
PIECE_LEN = 256
EPSILON = 1e-05
THETA = 10000.0
BF16 = jnp.bfloat16
F32 = jnp.float32


def dot(left, right, dims=((1,), (0,))):
    return lax.dot_general(left, right, (dims, ((), ())), preferred_element_type=F32)


def dot_t(left, right):
    return dot(left, right, ((1,), (1,)))


def tdot(left, right):
    return dot(left, right, ((0,), (0,)))


DMA = pltpu.SemaphoreType.DMA
MESH = pl.DeviceIdType.MESH


def barrier_all(n, me):
    barrier = pltpu.get_barrier_semaphore()
    for d in range(n):

        @pl.when(d != me)
        def _():
            pl.semaphore_signal(barrier, inc=1, device_id={"expert": d}, device_id_type=MESH)

    pl.semaphore_wait(barrier, n - 1)


def barrier_plane(n, me, chips, place):
    barrier = pltpu.get_barrier_semaphore()
    core, chip = place % 2, place // 2
    for d in range(n):

        @pl.when(d != me)
        def _():
            pl.semaphore_signal(barrier, inc=1, device_id={"expert": d}, device_id_type=MESH)

    pl.semaphore_signal(
        barrier, inc=1, device_id={"dp": place + 1 - 2 * core}, device_id_type=MESH
    )
    for c in range(chips):

        @pl.when(c != chip)
        def _():
            pl.semaphore_signal(
                barrier, inc=1, device_id={"dp": 2 * c + core}, device_id_type=MESH
            )

    pl.semaphore_wait(barrier, n - 1 + chips)


def remote(src, dst, send, recv, target, axis="expert"):
    return pltpu.make_async_remote_copy(
        src_ref=src, dst_ref=dst, send_sem=send, recv_sem=recv,
        device_id={axis: target}, device_id_type=MESH,
    )


class ChainGather:
    def __init__(self, n, me, slots, send, recv):
        self.n, self.me, self.slots, self.send, self.recv = n, me, slots, send, recv

    def copy(self, way, s, block, target):
        ref = self.slots.at[block]
        return remote(ref, ref, self.send.at[way, s], self.recv.at[way, s], target)

    def right(self, s):
        return self.copy(0, s, self.me - s, self.me + 1)

    def left(self, s):
        return self.copy(1, s, self.me + s, self.me - 1)

    def arrived(self, s):
        n, me = self.n, self.me

        @pl.when(me - 1 - s >= 0)
        def _():
            self.copy(0, s, me - 1 - s, me).wait_recv()

        @pl.when(me + 1 + s < n)
        def _():
            self.copy(1, s, me + 1 + s, me).wait_recv()

    def step(self, s):
        n, me = self.n, self.me
        if s >= 1:
            self.arrived(s - 1)

        @pl.when((me - s >= 0) & (me + 1 < n))
        def _():
            self.right(s).start()

        @pl.when((me + s < n) & (me > 0))
        def _():
            self.left(s).start()

    def finish(self):
        n, me = self.n, self.me
        self.arrived(n - 2)
        for s in range(n - 1):

            @pl.when((me - s >= 0) & (me + 1 < n))
            def _():
                self.right(s).wait_send()

            @pl.when((me + s < n) & (me > 0))
            def _():
                self.left(s).wait_send()


class Exchange:
    def __init__(self, n, me, source, slots, send, recv):
        self.n, self.me, self.source, self.slots = n, me, source, slots
        self.send, self.recv = send, recv

    def start(self, d):
        me = self.me

        @pl.when(d != me)
        def _():
            remote(
                self.source.at[d], self.slots.at[me], self.send.at[d], self.recv.at[me], d
            ).start()

    def finish(self):
        me = self.me
        for d in range(self.n):

            @pl.when(d != me)
            def _():
                desc = remote(
                    self.source.at[d], self.slots.at[d], self.send.at[d], self.recv.at[d], d
                )
                desc.wait_send()
                desc.wait_recv()


class PairReduce:
    def __init__(self, chips, place, parts, first, sums, second, sems):
        self.chips, self.core, self.chip = chips, place % 2, place // 2
        self.partner = place + 1 - 2 * self.core
        self.parts, self.first, self.sums, self.second = parts, first, sums, second
        self.sems = sems

    def near(self, c):
        s, r, _, _ = self.sems
        source = self.parts.at[2 * c + 1 - self.core]
        return remote(source, self.first.at[c], s.at[c], r.at[c], self.partner, "dp")

    def across(self, c, slot):
        _, _, s, r = self.sems
        return remote(
            self.sums.at[c], self.second.at[slot], s.at[c], r.at[slot], 2 * c + self.core, "dp"
        )

    def start(self):
        for c in range(self.chips):
            self.near(c).start()

    def middle(self):
        for c in range(self.chips):
            self.near(c).wait_recv()
            mine = self.parts[2 * c + self.core].astype(F32)
            self.sums[c] = (mine + self.first[c].astype(F32)).astype(BF16)

            @pl.when(c != self.chip)
            def _():
                self.across(c, self.chip).start()

    def finish(self, total):
        total[...] = self.sums[self.chip].astype(F32)
        for c in range(self.chips):
            self.near(c).wait_send()

            @pl.when(c != self.chip)
            def _():
                self.across(c, self.chip).wait_send()
                self.across(c, c).wait_recv()
                total[...] += self.second[c].astype(F32)


def pair_sems(chips):
    return [pltpu.SemaphoreType.DMA((chips,)) for _ in range(4)]


def chain_sems(n):
    return [pltpu.SemaphoreType.DMA((2, n - 1)), pltpu.SemaphoreType.DMA((2, n - 1))]


def direct_sems(n):
    return [pltpu.SemaphoreType.DMA((n,)), pltpu.SemaphoreType.DMA((n,))]


def call(kernel, outs, scratch, ident, name, flops, mib, args, far=()):
    vmem = pl.BlockSpec(memory_space=pltpu.VMEM)
    smem, anywhere = pl.BlockSpec(memory_space=pltpu.SMEM), pl.BlockSpec(memory_space=pl.ANY)
    nbytes = sum(a.size * a.dtype.itemsize for a in args)
    return pl.pallas_call(
        kernel,
        in_specs=[
            anywhere if j in far else smem if a.dtype == jnp.int32 else vmem
            for j, a in enumerate(args)
        ],
        out_specs=[vmem] * len(outs),
        out_shape=outs,
        scratch_shapes=scratch,
        compiler_params=pltpu.CompilerParams(
            collective_id=ident, has_side_effects=True, vmem_limit_bytes=mib * 1024 * 1024
        ),
        cost_estimate=pl.CostEstimate(flops=flops, transcendentals=0, bytes_accessed=nbytes),
        name=name,
    )(*args)


def gather_kernel(n, tokens_ref, all_ref, s0, r0):
    me = lax.axis_index("expert")
    barrier_all(n, me)
    all_ref[me] = tokens_ref[...]
    chain = ChainGather(n, me, all_ref, s0, r0)
    for s in range(n - 1):
        chain.step(s)
    chain.finish()


def gather_tokens(n, tokens):
    rows, width = tokens.shape
    return call(
        functools.partial(gather_kernel, n),
        [jax.ShapeDtypeStruct((n, rows, width), BF16)],
        chain_sems(n), 1, "gather_tokens", 10**6, 16, (tokens,),
    )[0]


def turn(x, cosine, sine):
    half = HEAD_SIZE // 2
    tiles = []
    for c in range(0, x.shape[1], 128):
        tile = x[:, c : c + 128]
        lane = lax.broadcasted_iota(jnp.int32, tile.shape, 1) % HEAD_SIZE
        other = jnp.where(lane < half, pltpu.roll(tile, 128 - half, 1), pltpu.roll(tile, half, 1))
        tiles.append(tile * cosine + other * sine)
    return jnp.concatenate(tiles, axis=1)


def bias_rows(starts_ref, q_pos, k_pos):
    seen = k_pos <= q_pos
    for k in range(starts_ref.shape[1]):
        a = starts_ref[0, k]
        q_in = (q_pos >= a) & (q_pos < a + PIECE_LEN)
        k_in = (k_pos >= a) & (k_pos < a + PIECE_LEN)
        seen = seen | (q_in & k_in)
    return jnp.where(seen, 0.0, -1e30)


def reach_of(block, rows, length, pieces):
    span = length // pieces
    return min(length, -(-((block + 1) * rows) // span) * span)


def attend_kernel(
    n, kv_local, tokens_ref, packed_ref, cos_ref, sin_ref, starts_ref, cot_ref,
    chosen_ref, norm_ref, q_ref, k_ref, v_ref, lse_ref, out_ref, att_ref, cots_ref, small_ref,
    every_ref, w_s, send_att, send_chosen, load, s0, r0, s1, r1, s2, r2,
):
    me = lax.axis_index("expert")
    per_key, length, tile = q_ref.shape
    rows = length // n
    q_cols, k_cols = per_key * tile, tile
    width, wide = w_s.shape
    weights = pltpu.make_async_copy(packed_ref.at[:, pl.ds(width, wide)], w_s, load)
    weights.start()
    barrier_all(n, me)
    cots_ref[me] = cot_ref[...]
    chain = ChainGather(n, me, cots_ref, s0, r0)
    chain.step(0)
    swap = Exchange(n, me, send_att, att_ref, s1, r1)
    choice = Exchange(n, me, send_chosen, every_ref, s2, r2)
    every_ref[me] = chosen_ref[...]
    for d in range(n):
        send_chosen[d] = chosen_ref[...]
        choice.start(d)
    pieces = starts_ref.shape[1]
    weights.wait()
    small = w_s[:, wide - 128 :].astype(F32).T
    small_ref[...] = small[: small_ref.shape[0], :]
    gain = small[:1, :]
    lane = lax.broadcasted_iota(jnp.int32, (rows, tile), 1)
    lane_w = lax.broadcasted_iota(jnp.int32, (rows, 128), 1)
    for i in range(n):
        part = slice(i * rows, (i + 1) * rows)
        x = tokens_ref[i].astype(F32)
        inverse = lax.rsqrt(jnp.mean(x * x, axis=1, keepdims=True) + EPSILON)
        norm = (x * inverse * gain).astype(BF16)
        norm_ref[i] = norm
        qkv = dot(norm, w_s[:, : wide - 128])
        qk = turn(qkv[:, : q_cols + k_cols], cos_ref[part, :], sin_ref[part, :]).astype(BF16)
        v_ref[part, :] = qkv[:, q_cols + k_cols : q_cols + 2 * k_cols].astype(BF16)
        k_ref[part, :] = qk[:, q_cols:]
        q = (qk[:, :q_cols].astype(F32) * HEAD_SIZE ** (-0.5)).astype(BF16)
        for t in range(per_key):
            for g in range(kv_local):
                at = (g * per_key + t) * HEAD_SIZE
                q_ref[t, part, g * HEAD_SIZE : (g + 1) * HEAD_SIZE] = q[:, at : at + HEAD_SIZE]
    if n > 2:
        chain.step(1)
    for i in range(n):
        reach = reach_of(i, rows, length, pieces)
        part = slice(i * rows, (i + 1) * rows)
        q_pos = lax.broadcasted_iota(jnp.int32, (rows, reach), 0) + i * rows
        k_pos = lax.broadcasted_iota(jnp.int32, (rows, reach), 1)
        bias = bias_rows(starts_ref, q_pos, k_pos)
        keys, values = k_ref[:reach, :], v_ref[:reach, :]
        k_lane = lax.broadcasted_iota(jnp.int32, (reach, tile), 1)

        def head(t, logs):
            q = q_ref[t, part, :]
            total = jnp.zeros((rows, tile), F32)
            for g in range(kv_local):
                mine = lane // HEAD_SIZE == g
                scores = dot_t(jnp.where(mine, q, jnp.zeros_like(q)), keys) + bias
                top = jnp.max(scores, axis=1, keepdims=True)
                powers = jnp.exp(scores - top)
                norm = jnp.sum(powers, axis=1, keepdims=True)
                value = jnp.where(k_lane // HEAD_SIZE == g, values, jnp.zeros_like(values))
                total = total + dot(powers.astype(BF16), value) * (1.0 / norm)
                logs = jnp.where(lane_w == t * kv_local + g, top + jnp.log(norm), logs)
            out_ref[t, part, :] = total
            return logs

        logs = lax.fori_loop(0, per_key, head, jnp.zeros((rows, 128), F32))
        lse_ref[:, part] = logs.T[: lse_ref.shape[0], :]
        for t in range(per_key):
            for g in range(kv_local):
                at = (g * per_key + t) * HEAD_SIZE
                send_att[i, :, at : at + HEAD_SIZE] = out_ref[
                    t, part, g * HEAD_SIZE : (g + 1) * HEAD_SIZE
                ].astype(BF16)
        swap.start(i)
        if i + 2 < n - 1:
            chain.step(i + 2)
    att_ref[me] = send_att[me]
    choice.finish()
    chain.finish()
    swap.finish()


def attend(n, kv_local, tokens_all, packed, cosine, sine, starts, cot, chosen):
    rows, width = cot.shape
    length = n * rows
    tile = kv_local * HEAD_SIZE
    per_key = QUERY_HEADS // KEY_VALUE_HEADS
    q_cols = per_key * tile
    wide = packed.shape[1] - width
    sds = jax.ShapeDtypeStruct
    lse_rows = -(-per_key * kv_local // 8) * 8
    return call(
        functools.partial(attend_kernel, n, kv_local),
        [
            sds((n, rows, width), BF16),
            sds((per_key, length, tile), BF16),
            sds((length, tile), BF16),
            sds((length, tile), BF16),
            sds((lse_rows, length), F32),
            sds((per_key, length, tile), F32),
            sds((n, rows, q_cols), BF16),
            sds((n, rows, width), BF16),
            sds((8 + chosen.shape[0], width), F32),
            sds((n,) + chosen.shape, F32),
        ],
        [
            pltpu.VMEM((width, wide), BF16), pltpu.VMEM((n, rows, q_cols), BF16),
            pltpu.VMEM((n,) + chosen.shape, F32), DMA,
        ]
        + chain_sems(n) + direct_sems(n) + direct_sems(n),
        2, "attend", 5 * 10**9, 44,
        (tokens_all, packed, cosine, sine, starts, cot, chosen), (1,),
    )


def mix_kernel(
    n, tokens_ref, att_ref, packed_ref, small_ref, hidden_ref, norms_ref, own_ref, w_s, load, s0, r0
):
    me = lax.axis_index("expert")
    q_cols = att_ref.shape[2]
    width = w_s.shape[0]
    weights = pltpu.make_async_copy(packed_ref.at[:, pl.ds(0, width)], w_s, load)
    weights.start()
    hidden = tokens_ref[...].astype(F32)
    weights.wait()
    for s in range(n):
        hidden = hidden + dot(att_ref[s], w_s[s * q_cols : (s + 1) * q_cols, :])
    hidden_ref[...] = hidden
    inverse = lax.rsqrt(jnp.mean(hidden * hidden, axis=1, keepdims=True) + EPSILON)
    norm = (hidden * inverse * small_ref[1:2, :]).astype(BF16)
    own_ref[...] = norm
    barrier_all(n, me)
    norms_ref[me] = norm
    chain = ChainGather(n, me, norms_ref, s0, r0)
    for s in range(n - 1):
        chain.step(s)
    chain.finish()


def mix(n, tokens, att, packed, small):
    rows, width = tokens.shape
    sds = jax.ShapeDtypeStruct
    return call(
        functools.partial(mix_kernel, n),
        [sds((rows, width), F32), sds((n, rows, width), BF16), sds((rows, width), BF16)],
        [pltpu.VMEM((width, width), BF16), DMA] + chain_sems(n),
        3, "mix", 2 * 10**9, 32, (tokens, att, packed, small), (2,),
    )


class ChainReduce:
    def __init__(self, n, me, parts, slots, send, recv):
        self.n, self.me, self.parts = n, me, parts
        self.slots, self.send, self.recv = slots, send, recv

    def copy(self, way, s, d, source):
        target = self.me + 1 if way == 0 else self.me - 1
        slot = d if way == 0 else jnp.where(d == target, self.n, d)
        return remote(
            source.at[d], self.slots.at[slot], self.send.at[way, s], self.recv.at[way, s], target
        )

    def far(self, way):
        return self.me if way == 0 else self.n - 1 - self.me

    def step(self, when):
        for way in (0, 1):
            far = self.far(way)
            s = when - far
            d = self.n - 1 - s if way == 0 else s
            slots = self.slots

            @pl.when(s >= 0)
            def _():
                @pl.when(far == 0)
                def _():
                    self.copy(way, s, d, self.parts).start()

                @pl.when(far > 0)
                def _():
                    self.copy(way, s, d, slots).wait_recv()
                    slots[d] = (slots[d].astype(F32) + self.parts[d].astype(F32)).astype(BF16)
                    self.copy(way, s, d, slots).start()

            if when > 0:

                @pl.when(s > 0)
                def _():
                    self.copy(way, s - 1, d, slots).wait_send()

    def finish(self, total):
        n, me = self.n, self.me
        total[...] = self.parts[me].astype(F32)
        for way in (0, 1):
            far = self.far(way)

            @pl.when(far > 0)
            def _():
                self.copy(way, n - 1 - far, me, self.slots).wait_recv()
                total[...] += self.slots[me if way == 0 else n].astype(F32)

            @pl.when(far < n - 1)
            def _():
                self.copy(way, n - 2 - far, me, self.slots).wait_send()


def rms_back(grad, rows, gain):
    inverse = lax.rsqrt(jnp.mean(rows * rows, axis=1, keepdims=True) + EPSILON)
    scaled = grad * gain
    grad_gain = jnp.sum(grad * rows * inverse, axis=0, keepdims=True)
    mean = jnp.mean(scaled * rows, axis=1, keepdims=True)
    return inverse * scaled - rows * (inverse * inverse * inverse * mean), grad_gain


def softmax_chosen(logits, chosen):
    top = jnp.max(jnp.where(chosen > 0.0, logits, -1e30), axis=0, keepdims=True)
    powers = jnp.where(chosen > 0.0, jnp.exp(jnp.where(chosen > 0.0, logits - top, 0.0)), 0.0)
    return powers / jnp.sum(powers, axis=0, keepdims=True)


def return_kernel(
    n, parts_ref, gg_ref, chosen_ref, small_ref, hidden_ref, norm_ref, cot_ref, att_ref, packed_ref,
    grad_ref, ga_ref, o_ref, extra_ref,
    w_s, slots, total, gg_s, send_ga, load, s0, r0, s1, r1, s2, r2,
):
    me = lax.axis_index("expert")
    width = w_s.shape[0]
    q_cols = ga_ref.shape[2]
    weights = pltpu.make_async_copy(packed_ref.at[:, pl.ds(0, width)], w_s, load)
    weights.start()
    barrier_all(n, me)
    chain = ChainReduce(n, me, parts_ref, slots, s0, r0)
    chain.step(0)
    gates_swap = Exchange(n, me, gg_ref, gg_s, s1, r1)
    for d in range(n):
        gates_swap.start(d)
    gg_s[me] = gg_ref[me]
    router = small_ref[8:, :].astype(BF16)
    gates = softmax_chosen(dot_t(router, norm_ref[...]), chosen_ref[...])
    gates_swap.finish()
    grad_gates = gg_s[...].reshape(gates.shape)
    middle = jnp.sum(gates * grad_gates, axis=0, keepdims=True)
    grad_logits = (gates * (grad_gates - middle)).astype(BF16)
    extra_ref[8:, :] = dot(grad_logits, norm_ref[...])
    for s in range(1, n - 1):
        chain.step(s)
    chain.finish(total)
    grad_norm = total[...] + tdot(grad_logits, router)
    grad, grad_gain = rms_back(grad_norm, hidden_ref[...], small_ref[1:2, :])
    row = lax.broadcasted_iota(jnp.int32, (8, width), 0)
    extra_ref[:8, :] = jnp.where(row == 1, grad_gain, 0.0)
    grad = cot_ref[...].astype(F32) + grad
    grad_ref[...] = grad
    proj = grad.astype(BF16)
    weights.wait()
    swap = Exchange(n, me, send_ga, ga_ref, s2, r2)
    for d in range(n):
        send_ga[d] = dot_t(proj, w_s[d * q_cols : (d + 1) * q_cols, :]).astype(BF16)
        swap.start(d)
    ga_ref[me] = send_ga[me]
    for d in range(n):
        o_ref[d * q_cols : (d + 1) * q_cols, :] = tdot(att_ref[d], proj).astype(BF16)
    swap.finish()


def give_back(n, parts, gg, chosen, small, hidden, norm, cot, att, packed):
    rows, width = cot.shape
    q_cols = att.shape[2]
    sds, vm = jax.ShapeDtypeStruct, pltpu.VMEM
    return call(
        functools.partial(return_kernel, n),
        [
            sds((rows, width), F32), sds(att.shape, BF16), sds((width, width), BF16),
            sds(small.shape, F32),
        ],
        [
            vm((width, width), BF16), vm((n + 1, rows, width), BF16),
            vm((rows, width), F32), vm(gg.shape, F32), vm((n, rows, q_cols), BF16), DMA,
        ]
        + chain_sems(n) + direct_sems(n) + direct_sems(n),
        4, "give_back", 4 * 10**9, 48,
        (parts, gg, chosen, small, hidden, norm, cot, att, packed), (8,),
    )


def attend_back_kernel(
    n, kv_local, chips, q_ref, k_ref, v_ref, lse_ref, out_ref, ga_ref, starts_ref, cos_ref,
    sin_ref, norm_ref, packed_ref, tokens_ref, small_ref, grad_ref, extra_ref, o_ref,
    input_ref, shares_ref, og_ref,
    w_s, gq_s, gk_s, gv_s, gqkv_s, ga_s, parts_s, b_slots, total, load,
    o_first, o_sums, o_second, o_total, o_send, o_got, dw_s, w_first, w_sums, w_second, w_total,
    s1, r1, s2, r2, s3, r3, s4, r4, *sems,
):
    me = lax.axis_index("expert")
    place = lax.axis_index("dp")
    per_key, length, tile = q_ref.shape
    rows = length // n
    q_cols, k_cols = per_key * tile, tile
    width, wide = w_s.shape
    used = q_cols + 2 * k_cols
    scale = HEAD_SIZE ** (-0.5)
    pieces = starts_ref.shape[1]
    weights = pltpu.make_async_copy(packed_ref.at[:, pl.ds(width, wide)], w_s, load)
    weights.start()
    barrier_plane(n, me, chips, place)
    o_sum = PairReduce(chips, place, o_ref, o_first, o_sums, o_second, sems[:4])
    o_sum.start()
    o_swap = Exchange(n, me, o_send, o_got, s2, r2)
    o_share = ChainGather(n, me, og_ref, s3, r3)
    gk_s[...] = jnp.zeros_like(gk_s)
    gv_s[...] = jnp.zeros_like(gv_s)
    lane = lax.broadcasted_iota(jnp.int32, (rows, tile), 1)
    lane_w = lax.broadcasted_iota(jnp.int32, (rows, 128), 1)
    for i in range(n):
        reach = reach_of(i, rows, length, pieces)
        part = slice(i * rows, (i + 1) * rows)
        deltas = jnp.zeros((rows, 128), F32)
        for t in range(per_key):
            for g in range(kv_local):
                at = (g * per_key + t) * HEAD_SIZE
                ga_s[t, :, g * HEAD_SIZE : (g + 1) * HEAD_SIZE] = ga_ref[i, :, at : at + HEAD_SIZE]
            product = ga_s[t].astype(F32) * out_ref[t, part, :]
            for g in range(kv_local):
                own = jnp.where(lane // HEAD_SIZE == g, product, 0.0)
                deltas = jnp.where(
                    lane_w == t * kv_local + g, jnp.sum(own, axis=1, keepdims=True), deltas
                )
        delta_s = deltas.T
        k_pos = lax.broadcasted_iota(jnp.int32, (reach, rows), 0)
        q_pos = lax.broadcasted_iota(jnp.int32, (reach, rows), 1) + i * rows
        bias = bias_rows(starts_ref, q_pos, k_pos)
        keys, values = k_ref[:reach, :], v_ref[:reach, :]
        k_lane = lax.broadcasted_iota(jnp.int32, (reach, tile), 1)
        for t in range(per_key):
            q, ga = q_ref[t, part, :], ga_s[t]
            grad_q = jnp.zeros((rows, tile), F32)
            for g in range(kv_local):
                h = t * kv_local + g
                mine = lane // HEAD_SIZE == g
                q_g = jnp.where(mine, q, jnp.zeros_like(q))
                ga_g = jnp.where(mine, ga, jnp.zeros_like(ga))
                scores = dot_t(keys, q_g) + bias
                probs = jnp.exp(scores - lse_ref[h : h + 1, part])
                grad_probs = dot_t(values, ga_g)
                grad_raw = (probs * (grad_probs - delta_s[h : h + 1, :])).astype(BF16)
                gk_s[:reach, :] += dot(grad_raw, q_g)
                gv_s[:reach, :] += dot(probs.astype(BF16), ga_g)
                key = jnp.where(k_lane // HEAD_SIZE == g, keys, jnp.zeros_like(keys))
                grad_q = grad_q + tdot(grad_raw, key)
            for g in range(kv_local):
                at = (g * per_key + t) * HEAD_SIZE
                gq_s[part, at : at + HEAD_SIZE] = (
                    grad_q[:, g * HEAD_SIZE : (g + 1) * HEAD_SIZE] * scale
                )
        if i == 0:
            o_sum.middle()
        if i == n // 2:
            o_sum.finish(o_total)
            piece = width // n
            for d in range(n):
                o_send[d] = o_total[:, d * piece : (d + 1) * piece].astype(BF16)
                o_swap.start(d)
        if i == n - 1:
            o_swap.finish()
            mine = o_send[me].astype(F32)
            for d in range(n):
                mine = mine + jnp.where(d == me, 0.0, o_got[d].astype(F32))
            og_ref[me] = mine.astype(BF16)
            o_share.step(0)
    gq_s[:, q_cols:] = gk_s[...]
    weights.wait()
    if used < gqkv_s.shape[1]:
        gqkv_s[...] = jnp.zeros_like(gqkv_s)
    gain = small_ref[:1, :]
    grad_gain = jnp.zeros_like(gain)
    for i in range(n):
        part = slice(i * rows, (i + 1) * rows)
        qk = turn(gq_s[part, :], cos_ref[part, :], -sin_ref[part, :]).astype(BF16)
        gqkv_s[part, : q_cols + k_cols] = qk
        gqkv_s[part, q_cols + k_cols : used] = gv_s[part, :].astype(BF16)
        back = dot_t(gqkv_s[part, :], w_s[:, : wide - 128])
        parts_s[i] = back.astype(BF16)
        grad_gain = grad_gain + jnp.sum(back * norm_ref[i].astype(F32), axis=0, keepdims=True)
    chain = ChainReduce(n, me, parts_s, b_slots, s1, r1)
    chain.step(0)
    norms = norm_ref[...].reshape(length, width)
    dw = tdot(norms, gqkv_s[...]).astype(BF16)
    dw_s[:, :, : wide - 128] = dw.reshape(2 * chips, -1, wide - 128)
    extra = extra_ref[...]
    row = lax.broadcasted_iota(jnp.int32, extra.shape, 0)
    extra = jnp.where(row == 0, grad_gain / gain, extra)
    extra = jnp.concatenate([extra, jnp.zeros((128 - extra.shape[0], width), F32)], axis=0)
    dw_s[:, :, wide - 128 :] = extra.T.astype(BF16).reshape(2 * chips, -1, 128)
    w_sum = PairReduce(chips, place, dw_s, w_first, w_sums, w_second, sems[4:])
    w_sum.start()
    for s in range(1, n - 1):
        o_share.step(s)
    o_share.finish()
    w_sum.middle()
    if n > 2:
        chain.step(1)
    w_sum.finish(w_total)
    shares_ref[me] = w_total[...].astype(BF16)
    w_share = ChainGather(n, me, shares_ref, s4, r4)
    w_share.step(0)
    for s in range(2, n - 1):
        chain.step(s)
    for s in range(1, n - 1):
        w_share.step(s)
    chain.finish(total)
    grad, _ = rms_back(total[...], tokens_ref[...].astype(F32), gain)
    input_ref[...] = (grad_ref[...] + grad).astype(BF16)
    w_share.finish()


def attend_back(
    n, kv_local, chips, saved, ga, starts, cosine, sine, norms, packed, tokens, small, grad, extra,
    grad_o,
):
    q, k, v, lse, out = saved
    rows, width = tokens.shape
    per_key, length, tile = q.shape
    wide = packed.shape[1] - width
    sds, vm = jax.ShapeDtypeStruct, pltpu.VMEM
    qk = (per_key + 1) * tile
    shard = width // (2 * chips)
    across, across_w = vm((chips, shard, width), BF16), vm((chips, shard, wide), BF16)
    piece = vm((n, shard, width // n), BF16)
    return call(
        functools.partial(attend_back_kernel, n, kv_local, chips),
        [
            sds((rows, width), BF16), sds((n, shard, wide), BF16),
            sds((n, shard, width // n), BF16),
        ],
        [
            vm((width, wide), BF16), vm((length, qk), F32), vm((length, tile), F32),
            vm((length, tile), F32), vm((length, wide - 128), BF16), vm((per_key, rows, tile), BF16),
            vm((n, rows, width), BF16), vm((n + 1, rows, width), BF16), vm((rows, width), F32), DMA,
            across, across, across, vm((shard, width), F32), piece, piece,
            vm((2 * chips, shard, wide), BF16), across_w, across_w, across_w,
            vm((shard, wide), F32),
        ]
        + chain_sems(n) + direct_sems(n) + chain_sems(n) + chain_sems(n)
        + pair_sems(chips) + pair_sems(chips),
        5, "attend_back", 10 * 10**9, 58,
        (q, k, v, lse, out, ga, starts, cosine, sine, norms, packed, tokens, small, grad, extra,
         grad_o.reshape(2 * chips, shard, width)),
        (10,),
    )


def expert_kernel(
    n, chosen_ref, small_ref, n2_ref, cot_ref, hidden_ref, wg_ref, wu_ref, wd_ref,
    dw_ref, gx_ref, gg_ref, output_ref,
    x_s, g_s, slope_s, silu_s, act_s, gact_s, ggp_s, gup_s, pick_s, mix_s, y_s, y_slots,
    total, gate_s, rank_s, s0, r0,
):
    me = lax.axis_index("expert")
    _, rows, width = n2_ref.shape
    local, tall, ff = act_s.shape
    cap = tall // n
    shards = wg_ref.shape[0]
    depth = ff // shards
    blocks = width // ff
    at = pl.program_id(0)
    later = jnp.maximum(at - local, 0)
    e = jnp.where(at < local, at, later // 3)
    phase = jnp.where(at < local, -1, later % 3)
    mine = me * gg_ref.shape[1] + e
    where = pl.ds(pl.multiple_of(e * cap, cap), cap)
    chain = ChainReduce(n, me, y_s, y_slots, s0, r0)

    def whole(ref):
        return ref[...].reshape(width, ff)

    def down(j):
        return wd_ref[:, 0, j * depth : (j + 1) * depth, :].reshape(ff, ff)

    def gate_column(s, pick):
        return jnp.sum(jnp.where(pick, gate_s[s, pl.ds(mine, 1), :], 0.0), axis=1, keepdims=True)

    @pl.when(at == 0)
    def _():
        barrier_all(n, me)
        before = lax.broadcasted_iota(jnp.int32, (rows, rows), 0)
        upto = jnp.where(before <= lax.broadcasted_iota(jnp.int32, (rows, rows), 1), 1.0, 0.0)
        router = small_ref[8:, :].astype(BF16)
        for s in range(n):
            chosen = chosen_ref[s]
            gate_s[s] = softmax_chosen(dot_t(router, n2_ref[s]), chosen)
            count = dot(chosen.astype(BF16), upto.astype(BF16))
            rank_s[s] = jnp.where(chosen > 0.0, count - 1.0, -1.0).astype(jnp.int32)
        gg_ref[...] = jnp.zeros_like(gg_ref)

    @pl.when(phase < 0)
    def _():
        slot = lax.broadcasted_iota(jnp.int32, (cap, rows), 0)
        cols = []
        for s in range(n):
            pick = slot == rank_s[s, pl.ds(mine, 1), :]
            hot = jnp.where(pick, 1.0, 0.0).astype(BF16)
            pick_s[s, where, :] = hot
            cols.append(gate_column(s, pick))
            x_s[s * cap : (s + 1) * cap, :] = dot(hot, n2_ref[s]).astype(BF16)
        x = x_s[...]
        gp = dot(x, whole(wg_ref))
        up = dot(x, whole(wu_ref))
        sigma = jax.nn.sigmoid(gp)
        silu = gp * sigma
        act = (silu * up).astype(BF16)
        act_s[e] = act
        silu_s[e] = silu.astype(BF16)
        slope_s[e] = (up * sigma * (1.0 + gp * (1.0 - sigma))).astype(BF16)
        for j in range(blocks):
            lanes = slice(j * ff, (j + 1) * ff)
            res = dot(act, down(j)).astype(BF16).astype(F32)
            for s in range(n):
                mix_s[s, where, lanes] = (cols[s] * res[s * cap : (s + 1) * cap, :]).astype(BF16)

    @pl.when(at == local - 1)
    def _():
        for s in range(n):
            y_s[s] = tdot(pick_s[s], mix_s[s]).astype(BF16)

    for s in range(n - 1):

        @pl.when(at == local + s * 3 * local // (n - 1))
        def _():
            chain.step(s)

    @pl.when(phase == 0)
    def _():
        for s in range(n):
            hot = pick_s[s, where, :]
            x_s[s * cap : (s + 1) * cap, :] = dot(hot, n2_ref[s]).astype(BF16)
            g_s[s * cap : (s + 1) * cap, :] = dot(hot, cot_ref[s]).astype(BF16)
        grad_act = jnp.zeros((tall, ff), F32)
        for j in range(blocks):
            grad_act = grad_act + dot_t(g_s[:, j * ff : (j + 1) * ff], down(j))
        act = act_s[e].astype(F32)
        sums = jnp.sum(act * grad_act, axis=1, keepdims=True)
        cols = []
        for s in range(n):
            pick = pick_s[s, where, :].astype(F32) > 0.5
            cols.append(gate_column(s, pick))
            part = sums[s * cap : (s + 1) * cap, :]
            gg_ref[s, pl.ds(e, 1), :] = jnp.sum(jnp.where(pick, part, 0.0), axis=0, keepdims=True)
        col = jnp.concatenate(cols, axis=0)
        grad_act = grad_act * col
        gact_s[...] = (act * col).astype(BF16)
        ggp = (grad_act * slope_s[e].astype(F32)).astype(BF16)
        ggp_s[...] = ggp
        gup_s[...] = (grad_act * silu_s[e].astype(F32)).astype(BF16)
        dw_ref[...] = tdot(x_s[...], ggp).astype(BF16).reshape(dw_ref.shape)

    @pl.when(phase == 1)
    def _():
        dw_ref[...] = tdot(x_s[...], gup_s[...]).astype(BF16).reshape(dw_ref.shape)
        grows = dot_t(ggp_s[...], whole(wg_ref)) + dot_t(gup_s[...], whole(wu_ref))
        grows = grows.astype(BF16)
        for s in range(n):
            mix_s[s, where, :] = grows[s * cap : (s + 1) * cap, :]

    @pl.when(phase == 2)
    def _():
        for j in range(blocks):
            grad = tdot(gact_s[...], g_s[:, j * ff : (j + 1) * ff]).astype(BF16)
            dw_ref[:, 0, j * depth : (j + 1) * depth, :] = grad.reshape(shards, depth, ff)

    @pl.when(at == 4 * local - 1)
    def _():
        for s in range(n):
            gx_ref[s] = tdot(pick_s[s], mix_s[s]).astype(BF16)
        chain.finish(total)
        output_ref[...] = (hidden_ref[...] + total[...]).astype(BF16)


def experts(n, chosen, small, n2, cot, hidden, w):
    _, rows, width = n2.shape
    shards, local, depth, ff = w.shape
    local = local // 3
    cap = rows * TOPK * 5 // (4 * local * n)
    tall = n * cap
    padded = chosen.shape[1] // n
    once = pl.Buffered(1)

    def const(shape):
        return pl.BlockSpec(shape, lambda i: (0,) * len(shape), pipeline_mode=once)

    def place(i):
        later = jnp.maximum(i - local, 0)
        return jnp.where(i < local, i, later // 3), later % 3

    def weight(k):
        return pl.BlockSpec((shards, 1, depth, ff), lambda i: (0, k * local + place(i)[0], 0, 0))

    def grads(i):
        later = jnp.maximum(i - local, 0)
        return (0, later % 3 * local + later // 3, 0, 0)

    sds, vm = jax.ShapeDtypeStruct, pltpu.VMEM
    saved, half = vm((local, tall, ff), BF16), vm((tall, ff), BF16)
    return pl.pallas_call(
        functools.partial(expert_kernel, n),
        grid=(4 * local,),
        in_specs=[
            const(chosen.shape), const(small.shape), const(n2.shape), const(n2.shape),
            const(hidden.shape), weight(0), weight(1), weight(2),
        ],
        out_specs=[
            pl.BlockSpec((shards, 1, depth, ff), grads),
            const(n2.shape), const((n, padded, rows)), const(hidden.shape),
        ],
        out_shape=[
            sds(w.shape, BF16), sds(n2.shape, BF16), sds((n, padded, rows), F32),
            sds(hidden.shape, BF16),
        ],
        scratch_shapes=[
            vm((tall, width), BF16), vm((tall, width), BF16), saved, saved, saved, half, half, half,
            vm((n, local * cap, rows), BF16), vm((n, local * cap, width), BF16), vm(n2.shape, BF16),
            vm((n + 1, rows, width), BF16), vm(hidden.shape, F32), vm(chosen.shape, F32), vm(chosen.shape, jnp.int32),
        ]
        + chain_sems(n),
        compiler_params=pltpu.CompilerParams(
            collective_id=6, has_side_effects=True, vmem_limit_bytes=60 * 1024 * 1024,
            dimension_semantics=("arbitrary",),
        ),
        cost_estimate=pl.CostEstimate(
            flops=40 * 10**9, transcendentals=0, bytes_accessed=60 * 10**6
        ),
        name="experts",
    )(chosen, small, n2, cot, hidden, w, w, w)


def rotary_tables(length):
    half = HEAD_SIZE // 2
    freqs = THETA ** (-(np.arange(half, dtype=np.float32) * 2.0 / HEAD_SIZE)).astype(np.float32)
    angles = np.arange(length, dtype=np.float32)[:, None] * freqs[None, :]
    cosine, sine = np.cos(angles), np.sin(angles)
    cosine = np.concatenate([cosine, cosine, cosine, cosine], axis=1)
    sine = np.concatenate([-sine, sine, -sine, sine], axis=1)
    return jnp.asarray(cosine, F32), jnp.asarray(sine, F32)


def per_device(
    tokens, attn_gain, q_weight, key_matrix, value_matrix, o_weight, ffn_gain, router_weight,
    expert_gate, expert_up, expert_down, routes, starts, cotangent,
):
    n = lax.axis_size("expert")
    member = lax.axis_index("expert")
    rows, width = tokens.shape
    length = rows * n
    kv_local = KEY_VALUE_HEADS // n
    q_cols = QUERY_HEADS // n * HEAD_SIZE
    k_cols = kv_local * HEAD_SIZE
    local, shard, ff = expert_gate.shape
    depth = expert_down.shape[1]
    blocks = width // ff
    padded = -(-local // 8) * 8

    wq = lax.dynamic_slice_in_dim(q_weight, member * q_cols, q_cols, 1)
    wk = lax.dynamic_slice_in_dim(key_matrix, member * k_cols, k_cols, 1)
    wv = lax.dynamic_slice_in_dim(value_matrix, member * k_cols, k_cols, 1)
    wide = width // 2
    used = q_cols + 2 * k_cols
    router = jnp.pad(
        router_weight.reshape(shard, n, local), ((0, 0), (0, 0), (0, padded - local))
    ).reshape(shard, n * padded)
    gains = jnp.stack([attn_gain, ffn_gain], axis=1)
    gap = jnp.zeros((shard, wide - 128 - used), BF16)
    packed = jnp.concatenate(
        [
            o_weight, wq, wk, wv, gap, jnp.pad(gains, ((0, 0), (0, 6))), router,
            jnp.zeros((shard, 120 - n * padded), BF16),
        ],
        axis=1,
    )
    packed = lax.all_gather(packed, "dp").reshape(width, -1)
    down_rows = expert_down.reshape(local, depth, blocks, ff).transpose(0, 2, 1, 3)
    stacked = jnp.concatenate(
        [expert_gate, expert_up, down_rows.reshape(local, shard, ff)], axis=0
    )
    experts_w = lax.all_gather(stacked, "dp")

    hot = routes[:, :, None] == jnp.arange(n * local, dtype=jnp.int32)
    chosen = jnp.any(hot, axis=1).astype(F32).T.reshape(n, local, rows)
    chosen = jnp.pad(chosen, ((0, 0), (0, padded - local), (0, 0))).reshape(n * padded, rows)
    cosine, sine = rotary_tables(length)
    chips = lax.axis_size("dp") // 2

    tokens_all = gather_tokens(n, tokens)
    norms, q, k, v, lse, out, att, cots, small, chosen_all = attend(
        n, kv_local, tokens_all, packed, cosine, sine, starts, cotangent, chosen
    )
    hidden, twos, two = mix(n, tokens, att, packed, small)
    grad_experts, back, gg, output = experts(n, chosen_all, small, twos, cots, hidden, experts_w)
    expert_grads = lax.psum_scatter(grad_experts, "dp", scatter_dimension=0)
    grad_hidden, ga, grad_o, extra = give_back(
        n, back, gg, chosen, small, hidden, two, cotangent, att, packed
    )
    input_grad, shares, o_grad = attend_back(
        n, kv_local, chips, (q, k, v, lse, out), ga, starts, cosine, sine, norms, packed, tokens,
        small, grad_hidden, extra, grad_o,
    )
    expert_grads = expert_grads.astype(F32)
    gate_grad, up_grad = expert_grads[:local], expert_grads[local : 2 * local]
    down_grad = expert_grads[2 * local :].reshape(local, blocks, depth, ff)
    down_grad = down_grad.transpose(0, 2, 1, 3).reshape(local, depth, width)
    o_grad = o_grad.astype(F32).transpose(1, 0, 2).reshape(shard, width)
    shares = shares.astype(F32)
    q_grad = shares[:, :, :q_cols].transpose(1, 0, 2).reshape(shard, -1)
    k_grad = shares[:, :, q_cols : q_cols + k_cols].transpose(1, 0, 2).reshape(shard, -1)
    v_grad = shares[:, :, q_cols + k_cols : used].transpose(1, 0, 2).reshape(shard, -1)
    rest = jnp.sum(shares[:, :, wide - 128 :], axis=0)
    router_grad = rest[:, 8 : 8 + n * padded].reshape(shard, n, padded)[:, :, :local]
    return (
        output, input_grad, rest[:, 0], q_grad, k_grad, v_grad, o_grad, rest[:, 1],
        router_grad.reshape(shard, n * local), gate_grad, up_grad, down_grad,
    )


def solution(mesh):
    rows, split, expert = P(("dp", "expert"), None), P("dp", None), P("expert", "dp", None)
    return jax.shard_map(
        per_device,
        mesh=mesh,
        in_specs=(
            rows, P("dp"), split, split, split, split, P("dp"), split,
            expert, expert, expert, rows, split, rows,
        ),
        out_specs=(
            rows, rows, P("dp"), split, split, split, split, P("dp"), split,
            expert, expert, expert,
        ),
        check_vma=False,
    )
```

```python
import functools

import jax
import jax.numpy as jnp
import numpy as np
from jax import lax
from jax.experimental import pallas as pl
from jax.experimental.pallas import tpu as pltpu
from jax.sharding import PartitionSpec as P

MODEL_WIDTH = 1536
QUERY_HEADS = 24
KEY_VALUE_HEADS = 8
HEAD_SIZE = 64
TOPK = 8
PIECE_LEN = 256
EPSILON = 1e-05
THETA = 10000.0
BF16 = jnp.bfloat16
F32 = jnp.float32


def dot(left, right, dims=((1,), (0,))):
    return lax.dot_general(left, right, (dims, ((), ())), preferred_element_type=F32)


def dot_t(left, right):
    return dot(left, right, ((1,), (1,)))


def tdot(left, right):
    return dot(left, right, ((0,), (0,)))


DMA = pltpu.SemaphoreType.DMA
MESH = pl.DeviceIdType.MESH


def barrier_all(n, me):
    barrier = pltpu.get_barrier_semaphore()
    for d in range(n):

        @pl.when(d != me)
        def _():
            pl.semaphore_signal(barrier, inc=1, device_id={"expert": d}, device_id_type=MESH)

    pl.semaphore_wait(barrier, n - 1)


def barrier_plane(n, me, chips, place):
    barrier = pltpu.get_barrier_semaphore()
    core, chip = place % 2, place // 2
    for d in range(n):

        @pl.when(d != me)
        def _():
            pl.semaphore_signal(barrier, inc=1, device_id={"expert": d}, device_id_type=MESH)

    pl.semaphore_signal(
        barrier, inc=1, device_id={"dp": place + 1 - 2 * core}, device_id_type=MESH
    )
    for c in range(chips):

        @pl.when(c != chip)
        def _():
            pl.semaphore_signal(
                barrier, inc=1, device_id={"dp": 2 * c + core}, device_id_type=MESH
            )

    pl.semaphore_wait(barrier, n - 1 + chips)


def remote(src, dst, send, recv, target, axis="expert"):
    return pltpu.make_async_remote_copy(
        src_ref=src, dst_ref=dst, send_sem=send, recv_sem=recv,
        device_id={axis: target}, device_id_type=MESH,
    )


class ChainGather:
    def __init__(self, n, me, slots, send, recv):
        self.n, self.me, self.slots, self.send, self.recv = n, me, slots, send, recv

    def copy(self, way, s, block, target):
        ref = self.slots.at[block]
        return remote(ref, ref, self.send.at[way, s], self.recv.at[way, s], target)

    def right(self, s):
        return self.copy(0, s, self.me - s, self.me + 1)

    def left(self, s):
        return self.copy(1, s, self.me + s, self.me - 1)

    def arrived(self, s):
        n, me = self.n, self.me

        @pl.when(me - 1 - s >= 0)
        def _():
            self.copy(0, s, me - 1 - s, me).wait_recv()

        @pl.when(me + 1 + s < n)
        def _():
            self.copy(1, s, me + 1 + s, me).wait_recv()

    def step(self, s):
        n, me = self.n, self.me
        if s >= 1:
            self.arrived(s - 1)

        @pl.when((me - s >= 0) & (me + 1 < n))
        def _():
            self.right(s).start()

        @pl.when((me + s < n) & (me > 0))
        def _():
            self.left(s).start()

    def finish(self):
        n, me = self.n, self.me
        self.arrived(n - 2)
        for s in range(n - 1):

            @pl.when((me - s >= 0) & (me + 1 < n))
            def _():
                self.right(s).wait_send()

            @pl.when((me + s < n) & (me > 0))
            def _():
                self.left(s).wait_send()


class Exchange:
    def __init__(self, n, me, source, slots, send, recv):
        self.n, self.me, self.source, self.slots = n, me, source, slots
        self.send, self.recv = send, recv

    def start(self, d):
        me = self.me

        @pl.when(d != me)
        def _():
            remote(
                self.source.at[d], self.slots.at[me], self.send.at[d], self.recv.at[me], d
            ).start()

    def finish(self):
        me = self.me
        for d in range(self.n):

            @pl.when(d != me)
            def _():
                desc = remote(
                    self.source.at[d], self.slots.at[d], self.send.at[d], self.recv.at[d], d
                )
                desc.wait_send()
                desc.wait_recv()


class PairReduce:
    def __init__(self, chips, place, parts, first, sums, second, near_sems, across_sems):
        self.chips, self.core, self.chip = chips, place % 2, place // 2
        self.partner = place + 1 - 2 * self.core
        self.parts, self.first, self.sums, self.second = parts, first, sums, second
        self.near_sems, self.across_sems = near_sems, across_sems

    def near(self, c):
        s, r = self.near_sems
        source = self.parts.at[2 * c + 1 - self.core]
        return remote(source, self.first.at[c], s.at[c], r.at[c], self.partner, "dp")

    def across(self, c, slot):
        s, r = self.across_sems
        return remote(
            self.sums.at[c], self.second.at[slot], s.at[c], r.at[slot], 2 * c + self.core, "dp"
        )

    def pair(self):
        for c in range(self.chips):
            self.near(c).start()

    def add(self):
        for c in range(self.chips):
            self.near(c).wait_recv()
            mine = self.parts[2 * c + self.core].astype(F32)
            self.sums[c] = (mine + self.first[c].astype(F32)).astype(BF16)

    def pair_sent(self):
        for c in range(self.chips):
            self.near(c).wait_send()

    def spread(self):
        for c in range(self.chips):

            @pl.when(c != self.chip)
            def _():
                self.across(c, self.chip).start()

    def finish(self, total):
        total[...] = self.sums[self.chip].astype(F32)
        for c in range(self.chips):

            @pl.when(c != self.chip)
            def _():
                self.across(c, self.chip).wait_send()
                self.across(c, c).wait_recv()
                total[...] += self.second[c].astype(F32)


def chain_sems(n):
    return [pltpu.SemaphoreType.DMA((2, n - 1)), pltpu.SemaphoreType.DMA((2, n - 1))]


def direct_sems(n):
    return [pltpu.SemaphoreType.DMA((n,)), pltpu.SemaphoreType.DMA((n,))]


def call(kernel, outs, scratch, ident, name, micros, mib, args, far=()):
    vmem = pl.BlockSpec(memory_space=pltpu.VMEM)
    smem, anywhere = pl.BlockSpec(memory_space=pltpu.SMEM), pl.BlockSpec(memory_space=pl.ANY)
    nbytes = sum(a.size * a.dtype.itemsize for a in args)
    return pl.pallas_call(
        kernel,
        in_specs=[
            anywhere if j in far else smem if a.dtype == jnp.int32 else vmem
            for j, a in enumerate(args)
        ],
        out_specs=[vmem] * len(outs),
        out_shape=outs,
        scratch_shapes=scratch,
        compiler_params=pltpu.CompilerParams(
            collective_id=ident, has_side_effects=True, vmem_limit_bytes=mib * 1024 * 1024
        ),
        cost_estimate=pl.CostEstimate(
            flops=micros * 10**9, transcendentals=0, bytes_accessed=nbytes
        ),
        name=name,
    )(*args)


def gather_kernel(
    n, tokens_ref, q_ref, k_ref, v_ref, gate_ref, up_ref, down_ref, all_ref, heads_ref, stack_ref,
    s0, r0,
):
    me = lax.axis_index("expert")
    barrier_all(n, me)
    all_ref[me] = tokens_ref[...]
    chain = ChainGather(n, me, all_ref, s0, r0)
    chain.step(0)
    local, depth, _ = down_ref.shape
    ff = gate_ref.shape[2]
    stack_ref[:local] = gate_ref[...]
    stack_ref[local : 2 * local] = up_ref[...]
    for j in range(down_ref.shape[2] // ff):
        stack_ref[2 * local :, j * depth : (j + 1) * depth, :] = down_ref[
            :, :, j * ff : (j + 1) * ff
        ]
    cols = heads_ref.shape[1] // n
    at = 0
    if cols * n > q_ref.shape[1] + 2 * k_ref.shape[1]:
        heads_ref[...] = jnp.zeros_like(heads_ref)
    for ref in (q_ref, k_ref, v_ref):
        part = ref.shape[1] // n
        for z in range(n):
            heads_ref[:, z * cols + at : z * cols + at + part] = ref[:, z * part : (z + 1) * part]
        at += part
    for s in range(1, n - 1):
        chain.step(s)
    chain.finish()


def gather_tokens(n, cols, tokens, wq, wk, wv, gate, up, down):
    rows, width = tokens.shape
    local, shard, ff = gate.shape
    sds = jax.ShapeDtypeStruct
    return call(
        functools.partial(gather_kernel, n),
        [
            sds((n, rows, width), BF16), sds((shard, n * cols), BF16),
            sds((3 * local, shard, ff), BF16),
        ],
        chain_sems(n), 1, "gather_tokens", 60, 24, (tokens, wq, wk, wv, gate, up, down),
    )


def turn(x, cosine, sine):
    half = HEAD_SIZE // 2
    tiles = []
    for c in range(0, x.shape[1], 128):
        tile = x[:, c : c + 128]
        lane = lax.broadcasted_iota(jnp.int32, tile.shape, 1) % HEAD_SIZE
        other = jnp.where(lane < half, pltpu.roll(tile, 128 - half, 1), pltpu.roll(tile, half, 1))
        tiles.append(tile * cosine + other * sine)
    return jnp.concatenate(tiles, axis=1)


def bias_rows(starts_ref, q_pos, k_pos):
    seen = k_pos <= q_pos
    for k in range(starts_ref.shape[1]):
        a = starts_ref[0, k]
        q_in = (q_pos >= a) & (q_pos < a + PIECE_LEN)
        k_in = (k_pos >= a) & (k_pos < a + PIECE_LEN)
        seen = seen | (q_in & k_in)
    return jnp.where(seen, 0.0, -1e30)


def reach_of(block, rows, length, pieces):
    span = length // pieces
    return min(length, -(-((block + 1) * rows) // span) * span)


def attend_kernel(
    n, kv_local, tokens_ref, packed_ref, cos_ref, sin_ref, starts_ref, cot_ref,
    chosen_ref, norm_ref, q_ref, k_ref, v_ref, lse_ref, out_ref, att_ref, cots_ref, small_ref,
    every_ref, w_s, send_att, send_chosen, load, s0, r0, s1, r1, s2, r2,
):
    me = lax.axis_index("expert")
    per_key, length, tile = q_ref.shape
    rows = length // n
    q_cols, k_cols = per_key * tile, tile
    width, wide = w_s.shape
    weights = pltpu.make_async_copy(packed_ref.at[:, pl.ds(width, wide)], w_s, load)
    weights.start()
    barrier_all(n, me)
    cots_ref[me] = cot_ref[:, : cots_ref.shape[2]]
    chain = ChainGather(n, me, cots_ref, s0, r0)
    chain.step(0)
    swap = Exchange(n, me, send_att, att_ref, s1, r1)
    choice = Exchange(n, me, send_chosen, every_ref, s2, r2)
    every_ref[me] = chosen_ref[...]
    for d in range(n):
        send_chosen[d] = chosen_ref[...]
        choice.start(d)
    pieces = starts_ref.shape[1]
    weights.wait()
    small = w_s[:, wide - 128 :].astype(F32).T
    small_ref[...] = small[: small_ref.shape[0], :]
    gain = small[:1, :]
    lane = lax.broadcasted_iota(jnp.int32, (rows, tile), 1)
    lane_w = lax.broadcasted_iota(jnp.int32, (rows, 128), 1)
    for i in range(n):
        part = slice(i * rows, (i + 1) * rows)
        x = tokens_ref[i].astype(F32)
        inverse = lax.rsqrt(jnp.mean(x * x, axis=1, keepdims=True) + EPSILON)
        norm = (x * inverse * gain).astype(BF16)
        norm_ref[i] = norm
        qkv = dot(norm, w_s[:, : wide - 128])
        qk = turn(qkv[:, : q_cols + k_cols], cos_ref[part, :], sin_ref[part, :]).astype(BF16)
        v_ref[part, :] = qkv[:, q_cols + k_cols : q_cols + 2 * k_cols].astype(BF16)
        k_ref[part, :] = qk[:, q_cols:]
        q = (qk[:, :q_cols].astype(F32) * HEAD_SIZE ** (-0.5)).astype(BF16)
        for t in range(per_key):
            for g in range(kv_local):
                at = (g * per_key + t) * HEAD_SIZE
                q_ref[t, part, g * HEAD_SIZE : (g + 1) * HEAD_SIZE] = q[:, at : at + HEAD_SIZE]
    if n > 2:
        chain.step(1)
    for i in range(n):
        reach = reach_of(i, rows, length, pieces)
        part = slice(i * rows, (i + 1) * rows)
        q_pos = lax.broadcasted_iota(jnp.int32, (rows, reach), 0) + i * rows
        k_pos = lax.broadcasted_iota(jnp.int32, (rows, reach), 1)
        bias = bias_rows(starts_ref, q_pos, k_pos)
        keys, values = k_ref[:reach, :], v_ref[:reach, :]
        k_lane = lax.broadcasted_iota(jnp.int32, (reach, tile), 1)

        def head(t, logs):
            q = q_ref[t, part, :]
            total = jnp.zeros((rows, tile), F32)
            for g in range(kv_local):
                mine = lane // HEAD_SIZE == g
                scores = dot_t(jnp.where(mine, q, jnp.zeros_like(q)), keys) + bias
                top = jnp.max(scores, axis=1, keepdims=True)
                powers = jnp.exp(scores - top)
                norm = jnp.sum(powers, axis=1, keepdims=True)
                value = jnp.where(k_lane // HEAD_SIZE == g, values, jnp.zeros_like(values))
                total = total + dot(powers.astype(BF16), value) * (1.0 / norm)
                logs = jnp.where(lane_w == t * kv_local + g, top + jnp.log(norm), logs)
            out_ref[t, part, :] = total
            return logs

        logs = lax.fori_loop(0, per_key, head, jnp.zeros((rows, 128), F32))
        lse_ref[:, part] = logs.T[: lse_ref.shape[0], :]
        for t in range(per_key):
            for g in range(kv_local):
                at = (g * per_key + t) * HEAD_SIZE
                send_att[i, :, at : at + HEAD_SIZE] = out_ref[
                    t, part, g * HEAD_SIZE : (g + 1) * HEAD_SIZE
                ].astype(BF16)
        swap.start(i)
        if i + 2 < n - 1:
            chain.step(i + 2)
    att_ref[me] = send_att[me]
    choice.finish()
    chain.finish()
    swap.finish()


def attend(n, kv_local, tokens_all, packed, cosine, sine, starts, cot, chosen):
    rows, width = cot.shape
    length = n * rows
    tile = kv_local * HEAD_SIZE
    per_key = QUERY_HEADS // KEY_VALUE_HEADS
    q_cols = per_key * tile
    wide = packed.shape[1] - width
    sds = jax.ShapeDtypeStruct
    lse_rows = -(-per_key * kv_local // 8) * 8
    return call(
        functools.partial(attend_kernel, n, kv_local),
        [
            sds((n, rows, width), BF16),
            sds((per_key, length, tile), BF16),
            sds((length, tile), BF16),
            sds((length, tile), BF16),
            sds((lse_rows, length), F32),
            sds((per_key, length, tile), F32),
            sds((n, rows, q_cols), BF16),
            sds((n, rows, width // 2), BF16),
            sds((8 + chosen.shape[0], width), F32),
            sds((n,) + chosen.shape, F32),
        ],
        [
            pltpu.VMEM((width, wide), BF16), pltpu.VMEM((n, rows, q_cols), BF16),
            pltpu.VMEM((n,) + chosen.shape, F32), DMA,
        ]
        + chain_sems(n) + direct_sems(n) + direct_sems(n),
        2, "attend", 80, 44,
        (tokens_all, packed, cosine, sine, starts, cot, chosen), (1,),
    )


def mix_kernel(
    n, tokens_ref, att_ref, packed_ref, small_ref, hidden_ref, norms_ref, own_ref, w_s, load, s0, r0
):
    me = lax.axis_index("expert")
    q_cols = att_ref.shape[2]
    width = w_s.shape[0]
    weights = pltpu.make_async_copy(packed_ref.at[:, pl.ds(0, width)], w_s, load)
    weights.start()
    hidden = tokens_ref[...].astype(F32)
    weights.wait()
    for s in range(n):
        hidden = hidden + dot(att_ref[s], w_s[s * q_cols : (s + 1) * q_cols, :])
    hidden_ref[...] = hidden
    inverse = lax.rsqrt(jnp.mean(hidden * hidden, axis=1, keepdims=True) + EPSILON)
    norm = (hidden * inverse * small_ref[1:2, :]).astype(BF16)
    own_ref[...] = norm
    barrier_all(n, me)
    norms_ref[me] = norm
    chain = ChainGather(n, me, norms_ref, s0, r0)
    for s in range(n - 1):
        chain.step(s)
    chain.finish()


def mix(n, tokens, att, packed, small):
    rows, width = tokens.shape
    sds = jax.ShapeDtypeStruct
    return call(
        functools.partial(mix_kernel, n),
        [sds((rows, width), F32), sds((n, rows, width), BF16), sds((rows, width), BF16)],
        [pltpu.VMEM((width, width), BF16), DMA] + chain_sems(n),
        3, "mix", 60, 32, (tokens, att, packed, small), (2,),
    )


class ChainReduce:
    def __init__(self, n, me, parts, slots, send, recv):
        self.n, self.me, self.parts = n, me, parts
        self.slots, self.send, self.recv = slots, send, recv

    def copy(self, way, s, d, source):
        target = self.me + 1 if way == 0 else self.me - 1
        slot = d if way == 0 else jnp.where(d == target, self.n, d)
        return remote(
            source.at[d], self.slots.at[slot], self.send.at[way, s], self.recv.at[way, s], target
        )

    def far(self, way):
        return self.me if way == 0 else self.n - 1 - self.me

    def step(self, when):
        for way in (0, 1):
            far = self.far(way)
            s = when - far
            d = self.n - 1 - s if way == 0 else s
            slots = self.slots

            @pl.when(s >= 0)
            def _():
                @pl.when(far == 0)
                def _():
                    self.copy(way, s, d, self.parts).start()

                @pl.when(far > 0)
                def _():
                    self.copy(way, s, d, slots).wait_recv()
                    slots[d] = (slots[d].astype(F32) + self.parts[d].astype(F32)).astype(BF16)
                    self.copy(way, s, d, slots).start()

            if when > 0:

                @pl.when(s > 0)
                def _():
                    self.copy(way, s - 1, d, slots).wait_send()

    def finish(self, total):
        n, me = self.n, self.me
        total[...] = self.parts[me].astype(F32)
        for way in (0, 1):
            far = self.far(way)

            @pl.when(far > 0)
            def _():
                self.copy(way, n - 1 - far, me, self.slots).wait_recv()
                total[...] += self.slots[me if way == 0 else n].astype(F32)

            @pl.when(far < n - 1)
            def _():
                self.copy(way, n - 2 - far, me, self.slots).wait_send()


def rms_back(grad, rows, gain):
    inverse = lax.rsqrt(jnp.mean(rows * rows, axis=1, keepdims=True) + EPSILON)
    scaled = grad * gain
    grad_gain = jnp.sum(grad * rows * inverse, axis=0, keepdims=True)
    mean = jnp.mean(scaled * rows, axis=1, keepdims=True)
    return inverse * scaled - rows * (inverse * inverse * inverse * mean), grad_gain


def softmax_chosen(logits, chosen):
    top = jnp.max(jnp.where(chosen > 0.0, logits, -1e30), axis=0, keepdims=True)
    powers = jnp.where(chosen > 0.0, jnp.exp(jnp.where(chosen > 0.0, logits - top, 0.0)), 0.0)
    return powers / jnp.sum(powers, axis=0, keepdims=True)


def return_kernel(
    n, parts_ref, gg_ref, chosen_ref, small_ref, hidden_ref, norm_ref, cot_ref, att_ref, packed_ref,
    grad_ref, ga_ref, o_ref, extra_ref,
    w_s, slots, total, gg_s, send_ga, o_parts, o_first, load, s0, r0, s1, r1, s2, r2, *near,
):
    me = lax.axis_index("expert")
    place = lax.axis_index("dp")
    chips = o_ref.shape[0]
    width = w_s.shape[0]
    q_cols = ga_ref.shape[2]
    weights = pltpu.make_async_copy(packed_ref.at[:, pl.ds(0, width)], w_s, load)
    weights.start()
    barrier_plane(n, me, chips, place)
    chain = ChainReduce(n, me, parts_ref, slots, s0, r0)
    chain.step(0)
    gates_swap = Exchange(n, me, gg_ref, gg_s, s1, r1)
    for d in range(n):
        gates_swap.start(d)
    gg_s[me] = gg_ref[me]
    router = small_ref[8:, :].astype(BF16)
    gates = softmax_chosen(dot_t(router, norm_ref[...]), chosen_ref[...])
    gates_swap.finish()
    grad_gates = gg_s[...].reshape(gates.shape)
    middle = jnp.sum(gates * grad_gates, axis=0, keepdims=True)
    grad_logits = (gates * (grad_gates - middle)).astype(BF16)
    extra_ref[8:, :] = dot(grad_logits, norm_ref[...])
    for s in range(1, n - 1):
        chain.step(s)
    chain.finish(total)
    grad_norm = total[...] + tdot(grad_logits, router)
    grad, grad_gain = rms_back(grad_norm, hidden_ref[...], small_ref[1:2, :])
    row = lax.broadcasted_iota(jnp.int32, (8, width), 0)
    extra_ref[:8, :] = jnp.where(row == 1, grad_gain, 0.0)
    grad = cot_ref[...].astype(F32) + grad
    grad_ref[...] = grad
    proj = grad.astype(BF16)
    weights.wait()
    swap = Exchange(n, me, send_ga, ga_ref, s2, r2)
    for d in range(n):
        send_ga[d] = dot_t(proj, w_s[d * q_cols : (d + 1) * q_cols, :]).astype(BF16)
        swap.start(d)
    ga_ref[me] = send_ga[me]
    shard = o_parts.shape[1]
    for d in range(n):
        grad_o = tdot(att_ref[d], proj).astype(BF16)
        o_parts[d * q_cols // shard : (d + 1) * q_cols // shard] = grad_o.reshape(-1, shard, width)
    o_sum = PairReduce(chips, place, o_parts, o_first, o_ref, None, near, None)
    o_sum.pair()
    o_sum.add()
    o_sum.pair_sent()
    swap.finish()


def give_back(n, chips, parts, gg, chosen, small, hidden, norm, cot, att, packed):
    rows, width = cot.shape
    q_cols = att.shape[2]
    shard = width // (2 * chips)
    sds, vm = jax.ShapeDtypeStruct, pltpu.VMEM
    return call(
        functools.partial(return_kernel, n),
        [
            sds((rows, width), F32), sds(att.shape, BF16), sds((chips, shard, width), BF16),
            sds(small.shape, F32),
        ],
        [
            vm((width, width), BF16), vm((n + 1, rows, width), BF16),
            vm((rows, width), F32), vm(gg.shape, F32), vm((n, rows, q_cols), BF16),
            vm((2 * chips, shard, width), BF16), vm((chips, shard, width), BF16), DMA,
        ]
        + chain_sems(n) + direct_sems(n) + direct_sems(n) + direct_sems(chips),
        4, "give_back", 80, 48,
        (parts, gg, chosen, small, hidden, norm, cot, att, packed), (8,),
    )


def attend_back_kernel(
    n, kv_local, q_ref, k_ref, v_ref, lse_ref, out_ref, ga_ref, starts_ref, cos_ref,
    sin_ref, norm_ref, all_ref, tokens_ref, small_ref, grad_ref, extra_ref, o_ref,
    input_ref, shares_ref, og_ref,
    w_s, gq_s, gk_s, gv_s, gqkv_s, ga_s, q_send, q_got, kv_send, kv_got, load,
    o_second, o_total, o_send, o_got, dw_s, w_first, w_sums, w_second, w_total,
    s0, r0, s1, r1, s2, r2, s3, r3, s4, r4, *sems,
):
    me = lax.axis_index("expert")
    place = lax.axis_index("dp")
    per_key, length, tile = q_ref.shape
    chips, shard, _ = o_ref.shape
    rows = length // n
    q_cols, k_cols = per_key * tile, tile
    width = w_s.shape[0]
    cols = w_s.shape[1] // n
    scale = HEAD_SIZE ** (-0.5)
    pieces = starts_ref.shape[1]
    weights = pltpu.make_async_copy(all_ref, w_s, load)
    weights.start()
    barrier_plane(n, me, chips, place)
    o_sum = PairReduce(chips, place, None, None, o_ref, o_second, None, sems[:2])
    o_sum.spread()
    q_swap = Exchange(n, me, q_send, q_got, s0, r0)
    kv_swap = Exchange(n, me, kv_send, kv_got, s1, r1)
    o_swap = Exchange(n, me, o_send, o_got, s2, r2)
    o_share = ChainGather(n, me, og_ref, s3, r3)
    w_share = ChainGather(n, me, shares_ref, s4, r4)
    gq_s[...] = jnp.zeros_like(gq_s)
    gqkv_s[...] = jnp.zeros_like(gqkv_s)
    gk_s[...] = jnp.zeros_like(gk_s)
    gv_s[...] = jnp.zeros_like(gv_s)
    lane = lax.broadcasted_iota(jnp.int32, (rows, tile), 1)
    lane_w = lax.broadcasted_iota(jnp.int32, (rows, 128), 1)
    for i in range(n):
        reach = reach_of(i, rows, length, pieces)
        part = slice(i * rows, (i + 1) * rows)
        deltas = jnp.zeros((rows, 128), F32)
        for t in range(per_key):
            for g in range(kv_local):
                at = (g * per_key + t) * HEAD_SIZE
                ga_s[t, :, g * HEAD_SIZE : (g + 1) * HEAD_SIZE] = ga_ref[i, :, at : at + HEAD_SIZE]
            product = ga_s[t].astype(F32) * out_ref[t, part, :]
            for g in range(kv_local):
                own = jnp.where(lane // HEAD_SIZE == g, product, 0.0)
                deltas = jnp.where(
                    lane_w == t * kv_local + g, jnp.sum(own, axis=1, keepdims=True), deltas
                )
        delta_s = deltas.T
        k_pos = lax.broadcasted_iota(jnp.int32, (reach, rows), 0)
        q_pos = lax.broadcasted_iota(jnp.int32, (reach, rows), 1) + i * rows
        bias = bias_rows(starts_ref, q_pos, k_pos)
        keys, values = k_ref[:reach, :], v_ref[:reach, :]
        k_lane = lax.broadcasted_iota(jnp.int32, (reach, tile), 1)
        for t in range(per_key):
            q, ga = q_ref[t, part, :], ga_s[t]
            grad_q = jnp.zeros((rows, tile), F32)
            for g in range(kv_local):
                h = t * kv_local + g
                mine = lane // HEAD_SIZE == g
                q_g = jnp.where(mine, q, jnp.zeros_like(q))
                ga_g = jnp.where(mine, ga, jnp.zeros_like(ga))
                scores = dot_t(keys, q_g) + bias
                probs = jnp.exp(scores - lse_ref[h : h + 1, part])
                grad_probs = dot_t(values, ga_g)
                grad_raw = (probs * (grad_probs - delta_s[h : h + 1, :])).astype(BF16)
                gk_s[:reach, :tile] += dot(grad_raw, q_g)
                gv_s[:reach, :] += dot(probs.astype(BF16), ga_g)
                key = jnp.where(k_lane // HEAD_SIZE == g, keys, jnp.zeros_like(keys))
                grad_q = grad_q + tdot(grad_raw, key)
            for g in range(kv_local):
                at = (g * per_key + t) * HEAD_SIZE
                gq_s[:, at : at + HEAD_SIZE] = (
                    grad_q[:, g * HEAD_SIZE : (g + 1) * HEAD_SIZE] * scale
                )
        turned = turn(gq_s[...], cos_ref[part, :], -sin_ref[part, :])[:, :q_cols].astype(BF16)
        gqkv_s[part, :q_cols] = turned
        q_send[i] = turned
        q_swap.start(i)
    for i in range(n):
        part = slice(i * rows, (i + 1) * rows)
        turned = turn(gk_s[part, :], cos_ref[part, :], -sin_ref[part, :])[:, :k_cols].astype(BF16)
        kv_send[i, :, :k_cols] = turned
        kv_send[i, :, k_cols:] = gv_s[part, :].astype(BF16)
        kv_swap.start(i)
        gqkv_s[part, q_cols : q_cols + 2 * k_cols] = kv_send[i]
    weights.wait()
    norms = norm_ref[...].reshape(length, width)
    dw = tdot(norms, gqkv_s[...])
    own = w_s[:, pl.ds(pl.multiple_of(me * cols, 128), cols)].astype(F32)
    grad_gain = jnp.sum(dw * own, axis=1, keepdims=True)
    dw_s[:, :, :cols] = dw.astype(BF16).reshape(2 * chips, shard, cols)
    extra = extra_ref[...]
    extra = jnp.concatenate([extra, jnp.zeros((128 - extra.shape[0], width), F32)], axis=0).T
    lane_e = lax.broadcasted_iota(jnp.int32, extra.shape, 1)
    extra = jnp.where(lane_e == 0, grad_gain, extra)
    dw_s[:, :, cols:] = extra.astype(BF16).reshape(2 * chips, shard, 128)
    w_sum = PairReduce(chips, place, dw_s, w_first, w_sums, w_second, sems[2:4], sems[4:])
    w_sum.pair()
    o_sum.finish(o_total)
    piece = width // n
    for d in range(n):
        o_send[d] = o_total[:, d * piece : (d + 1) * piece].astype(BF16)
        o_swap.start(d)
    w_sum.add()
    w_sum.spread()
    q_got[me] = q_send[me]
    kv_got[me] = kv_send[me]
    q_swap.finish()
    kv_swap.finish()
    grad_norm = jnp.zeros((rows, width), F32)
    for z in range(n):
        grad_norm = grad_norm + dot_t(q_got[z], w_s[:, z * cols : z * cols + q_cols])
        grad_norm = grad_norm + dot_t(
            kv_got[z], w_s[:, z * cols + q_cols : z * cols + q_cols + 2 * k_cols]
        )
    grad, _ = rms_back(grad_norm, tokens_ref[...].astype(F32), small_ref[:1, :])
    input_ref[...] = (grad_ref[...] + grad).astype(BF16)
    o_swap.finish()
    mine = o_send[me].astype(F32)
    for d in range(n):
        mine = mine + jnp.where(d == me, 0.0, o_got[d].astype(F32))
    og_ref[me] = mine.astype(BF16)
    o_share.step(0)
    w_sum.pair_sent()
    w_sum.finish(w_total)
    shares_ref[me] = w_total[...].astype(BF16)
    w_share.step(0)
    for s in range(1, n - 1):
        o_share.step(s)
        w_share.step(s)
    o_share.finish()
    w_share.finish()


def attend_back(
    n, kv_local, saved, ga, starts, cosine, sine, norms, w_all, tokens, small, grad, extra, sums_o
):
    q, k, v, lse, out = saved
    rows, width = tokens.shape
    per_key, length, tile = q.shape
    chips, shard, _ = sums_o.shape
    cols = w_all.shape[1] // n
    wide = cols + 128
    sds, vm = jax.ShapeDtypeStruct, pltpu.VMEM
    q_cols = per_key * tile
    across_w = vm((chips, shard, wide), BF16)
    piece = vm((n, shard, width // n), BF16)
    q_block, kv_block = vm((n, rows, q_cols), BF16), vm((n, rows, 2 * tile), BF16)
    return call(
        functools.partial(attend_back_kernel, n, kv_local),
        [
            sds((rows, width), BF16), sds((n, shard, wide), BF16),
            sds((n, shard, width // n), BF16),
        ],
        [
            vm(w_all.shape, BF16), vm((rows, -(-q_cols // 128) * 128), F32), vm((length, 128), F32),
            vm((length, tile), F32), vm((length, cols), BF16), vm((per_key, rows, tile), BF16),
            q_block, q_block, kv_block, kv_block, DMA,
            vm((chips, shard, width), BF16), vm((shard, width), F32), piece, piece,
            vm((2 * chips, shard, wide), BF16), across_w, across_w, across_w,
            vm((shard, wide), F32),
        ]
        + direct_sems(n) + direct_sems(n) + direct_sems(n) + chain_sems(n) + chain_sems(n)
        + direct_sems(chips) + direct_sems(chips) + direct_sems(chips),
        5, "attend_back", 90, 56,
        (q, k, v, lse, out, ga, starts, cosine, sine, norms, w_all, tokens, small, grad, extra,
         sums_o),
        (10,),
    )


def expert_kernel(
    n, chosen_ref, small_ref, n2_ref, cots_ref, cot_ref, hidden_ref, wg_ref, wu_ref, wd_ref,
    dw_ref, gx_ref, gg_ref, output_ref,
    x_s, g_s, slope_s, silu_s, act_s, gact_s, ggp_s, gup_s, pick_s, mix_s, y_s, y_slots,
    total, gate_s, rank_s, rest_s, s0, r0, s1, r1,
):
    me = lax.axis_index("expert")
    _, rows, width = n2_ref.shape
    local, tall, ff = act_s.shape
    cap = tall // n
    shards = wg_ref.shape[0]
    depth = ff // shards
    blocks = width // ff
    at = pl.program_id(0)
    later = jnp.maximum(at - local, 0)
    e = jnp.where(at < local, at, later // 3)
    phase = jnp.where(at < local, -1, later % 3)
    mine = me * gg_ref.shape[1] + e
    where = pl.ds(pl.multiple_of(e * cap, cap), cap)
    chain = ChainReduce(n, me, y_s, y_slots, s0, r0)
    more = ChainGather(n, me, rest_s, s1, r1)
    half = cots_ref.shape[2]

    def whole(ref):
        return ref[...].reshape(width, ff)

    def down(j):
        return wd_ref[:, 0, j * depth : (j + 1) * depth, :].reshape(ff, ff)

    def gate_column(s, pick):
        return jnp.sum(jnp.where(pick, gate_s[s, pl.ds(mine, 1), :], 0.0), axis=1, keepdims=True)

    @pl.when(at == 0)
    def _():
        barrier_all(n, me)
        rest_s[me] = cot_ref[:, half:]
        more.step(0)
        before = lax.broadcasted_iota(jnp.int32, (rows, rows), 0)
        upto = jnp.where(before <= lax.broadcasted_iota(jnp.int32, (rows, rows), 1), 1.0, 0.0)
        router = small_ref[8:, :].astype(BF16)
        for s in range(n):
            chosen = chosen_ref[s]
            gate_s[s] = softmax_chosen(dot_t(router, n2_ref[s]), chosen)
            count = dot(chosen.astype(BF16), upto.astype(BF16))
            rank_s[s] = jnp.where(chosen > 0.0, count - 1.0, -1.0).astype(jnp.int32)
        gg_ref[...] = jnp.zeros_like(gg_ref)

    for s in range(1, n - 1):

        @pl.when(at == min((s * local + n - 2) // (n - 1), local - 1))
        def _():
            more.step(s)

    @pl.when(phase < 0)
    def _():
        slot = lax.broadcasted_iota(jnp.int32, (cap, rows), 0)
        cols = []
        for s in range(n):
            pick = slot == rank_s[s, pl.ds(mine, 1), :]
            hot = jnp.where(pick, 1.0, 0.0).astype(BF16)
            pick_s[s, where, :] = hot
            cols.append(gate_column(s, pick))
            x_s[s * cap : (s + 1) * cap, :] = dot(hot, n2_ref[s]).astype(BF16)
        x = x_s[...]
        gp = dot(x, whole(wg_ref))
        up = dot(x, whole(wu_ref))
        sigma = jax.nn.sigmoid(gp)
        silu = gp * sigma
        act = (silu * up).astype(BF16)
        act_s[e] = act
        silu_s[e] = silu.astype(BF16)
        slope_s[e] = (up * sigma * (1.0 + gp * (1.0 - sigma))).astype(BF16)
        for j in range(blocks):
            lanes = slice(j * ff, (j + 1) * ff)
            res = dot(act, down(j)).astype(BF16).astype(F32)
            for s in range(n):
                mix_s[s, where, lanes] = (cols[s] * res[s * cap : (s + 1) * cap, :]).astype(BF16)

    @pl.when(at == local - 1)
    def _():
        for s in range(n):
            y_s[s] = tdot(pick_s[s], mix_s[s]).astype(BF16)

    for s in range(n - 1):

        @pl.when(at == local + s * 3 * local // (n - 1))
        def _():
            chain.step(s)

    @pl.when(at == local)
    def _():
        more.finish()

    @pl.when(phase == 0)
    def _():
        for s in range(n):
            hot = pick_s[s, where, :]
            x_s[s * cap : (s + 1) * cap, :] = dot(hot, n2_ref[s]).astype(BF16)
            g_s[s * cap : (s + 1) * cap, :half] = dot(hot, cots_ref[s]).astype(BF16)
            g_s[s * cap : (s + 1) * cap, half:] = dot(hot, rest_s[s]).astype(BF16)
        grad_act = jnp.zeros((tall, ff), F32)
        for j in range(blocks):
            grad_act = grad_act + dot_t(g_s[:, j * ff : (j + 1) * ff], down(j))
        act = act_s[e].astype(F32)
        sums = jnp.sum(act * grad_act, axis=1, keepdims=True)
        cols = []
        for s in range(n):
            pick = pick_s[s, where, :].astype(F32) > 0.5
            cols.append(gate_column(s, pick))
            part = sums[s * cap : (s + 1) * cap, :]
            gg_ref[s, pl.ds(e, 1), :] = jnp.sum(jnp.where(pick, part, 0.0), axis=0, keepdims=True)
        col = jnp.concatenate(cols, axis=0)
        grad_act = grad_act * col
        gact_s[...] = (act * col).astype(BF16)
        ggp = (grad_act * slope_s[e].astype(F32)).astype(BF16)
        ggp_s[...] = ggp
        gup_s[...] = (grad_act * silu_s[e].astype(F32)).astype(BF16)
        dw_ref[...] = tdot(x_s[...], ggp).astype(BF16).reshape(dw_ref.shape)

    @pl.when(phase == 1)
    def _():
        dw_ref[...] = tdot(x_s[...], gup_s[...]).astype(BF16).reshape(dw_ref.shape)
        grows = dot_t(ggp_s[...], whole(wg_ref)) + dot_t(gup_s[...], whole(wu_ref))
        grows = grows.astype(BF16)
        for s in range(n):
            mix_s[s, where, :] = grows[s * cap : (s + 1) * cap, :]

    @pl.when(phase == 2)
    def _():
        for j in range(blocks):
            grad = tdot(gact_s[...], g_s[:, j * ff : (j + 1) * ff]).astype(BF16)
            dw_ref[:, 0, j * depth : (j + 1) * depth, :] = grad.reshape(shards, depth, ff)

    @pl.when(at == 4 * local - 1)
    def _():
        for s in range(n):
            gx_ref[s] = tdot(pick_s[s], mix_s[s]).astype(BF16)
        chain.finish(total)
        output_ref[...] = (hidden_ref[...] + total[...]).astype(BF16)


def experts(n, chosen, small, n2, cots, cot, hidden, w):
    _, rows, width = n2.shape
    shards, local, depth, ff = w.shape
    local = local // 3
    cap = rows * TOPK * 5 // (4 * local * n)
    tall = n * cap
    padded = chosen.shape[1] // n
    once = pl.Buffered(1)

    def const(shape):
        return pl.BlockSpec(shape, lambda i: (0,) * len(shape), pipeline_mode=once)

    def place(i):
        later = jnp.maximum(i - local, 0)
        return jnp.where(i < local, i, later // 3), later % 3

    def weight(k):
        return pl.BlockSpec((shards, 1, depth, ff), lambda i: (0, k * local + place(i)[0], 0, 0))

    def grads(i):
        later = jnp.maximum(i - local, 0)
        return (0, later % 3 * local + later // 3, 0, 0)

    sds, vm = jax.ShapeDtypeStruct, pltpu.VMEM
    saved, half = vm((local, tall, ff), BF16), vm((tall, ff), BF16)
    return pl.pallas_call(
        functools.partial(expert_kernel, n),
        grid=(4 * local,),
        in_specs=[
            const(chosen.shape), const(small.shape), const(n2.shape), const(cots.shape),
            const(cot.shape), const(hidden.shape), weight(0), weight(1), weight(2),
        ],
        out_specs=[
            pl.BlockSpec((shards, 1, depth, ff), grads),
            const(n2.shape), const((n, padded, rows)), const(hidden.shape),
        ],
        out_shape=[
            sds(w.shape, BF16), sds(n2.shape, BF16), sds((n, padded, rows), F32),
            sds(hidden.shape, BF16),
        ],
        scratch_shapes=[
            vm((tall, width), BF16), vm((tall, width), BF16), saved, saved, saved, half, half, half,
            vm((n, local * cap, rows), BF16), vm((n, local * cap, width), BF16), vm(n2.shape, BF16),
            vm((n + 1, rows, width), BF16), vm(hidden.shape, F32), vm(chosen.shape, F32), vm(chosen.shape, jnp.int32),
            vm((n, rows, width - cots.shape[2]), BF16),
        ]
        + chain_sems(n) + chain_sems(n),
        compiler_params=pltpu.CompilerParams(
            collective_id=6, has_side_effects=True, vmem_limit_bytes=60 * 1024 * 1024,
            dimension_semantics=("arbitrary",),
        ),
        cost_estimate=pl.CostEstimate(
            flops=95 * 10**9, transcendentals=0, bytes_accessed=60 * 10**6
        ),
        name="experts",
    )(chosen, small, n2, cots, cot, hidden, w, w, w)


def finish_kernel(
    n, shares_ref, pieces_ref, sums_ref, y_ref, grad_ref, q_ref, k_ref, v_ref, o_ref, small_ref,
    gate_ref, up_ref, down_ref, output_ref, input_ref,
):
    q_cols, k_cols = q_ref.shape[1] // n, k_ref.shape[1] // n
    piece = pieces_ref.shape[2]
    cols = shares_ref.shape[2] - 128
    small = jnp.zeros(small_ref.shape, F32)
    for z in range(n):
        at = 0
        for ref, part in ((q_ref, q_cols), (k_ref, k_cols), (v_ref, k_cols)):
            ref[:, z * part : (z + 1) * part] = shares_ref[z, :, at : at + part].astype(F32)
            at += part
        small = small + shares_ref[z, :, cols:].astype(F32)
        o_ref[:, z * piece : (z + 1) * piece] = pieces_ref[z].astype(F32)
    small_ref[...] = small
    local, depth, _ = down_ref.shape
    ff = gate_ref.shape[2]
    gate_ref[...] = sums_ref[:local].astype(F32)
    up_ref[...] = sums_ref[local : 2 * local].astype(F32)
    for j in range(down_ref.shape[2] // ff):
        down_ref[:, :, j * ff : (j + 1) * ff] = sums_ref[
            2 * local :, j * depth : (j + 1) * depth, :
        ].astype(F32)
    output_ref[...] = y_ref[...]
    input_ref[...] = grad_ref[...]


def finish(n, k_width, depth, shares, pieces, sums, y, grad):
    _, shard, _ = shares.shape
    width = y.shape[1]
    local, ff = sums.shape[0] // 3, sums.shape[2]
    sds = jax.ShapeDtypeStruct
    square, narrow, expert = (
        sds((shard, width), F32), sds((shard, k_width), F32), sds((local, shard, ff), F32)
    )
    vmem = pl.BlockSpec(memory_space=pltpu.VMEM)
    return pl.pallas_call(
        functools.partial(finish_kernel, n),
        in_specs=[vmem] * 5,
        out_specs=[vmem] * 10,
        out_shape=[
            square, narrow, narrow, square, sds((shard, 128), F32), expert, expert,
            sds((local, depth, width), F32), sds(y.shape, BF16), sds(y.shape, BF16),
        ],
        compiler_params=pltpu.CompilerParams(vmem_limit_bytes=40 * 1024 * 1024),
        name="finish",
    )(shares, pieces, sums, y, grad)


def rotary_tables(length):
    half = HEAD_SIZE // 2
    freqs = THETA ** (-(np.arange(half, dtype=np.float32) * 2.0 / HEAD_SIZE)).astype(np.float32)
    angles = np.arange(length, dtype=np.float32)[:, None] * freqs[None, :]
    cosine, sine = np.cos(angles), np.sin(angles)
    cosine = np.concatenate([cosine, cosine, cosine, cosine], axis=1)
    sine = np.concatenate([-sine, sine, -sine, sine], axis=1)
    return jnp.asarray(cosine, F32), jnp.asarray(sine, F32)


def per_device(
    tokens, attn_gain, q_weight, key_matrix, value_matrix, o_weight, ffn_gain, router_weight,
    expert_gate, expert_up, expert_down, routes, starts, cotangent,
):
    n = lax.axis_size("expert")
    member = lax.axis_index("expert")
    rows, width = tokens.shape
    length = rows * n
    kv_local = KEY_VALUE_HEADS // n
    q_cols = QUERY_HEADS // n * HEAD_SIZE
    k_cols = kv_local * HEAD_SIZE
    local, shard, _ = expert_gate.shape
    padded = -(-local // 8) * 8

    wq = lax.dynamic_slice_in_dim(q_weight, member * q_cols, q_cols, 1)
    wk = lax.dynamic_slice_in_dim(key_matrix, member * k_cols, k_cols, 1)
    wv = lax.dynamic_slice_in_dim(value_matrix, member * k_cols, k_cols, 1)
    wide = width // 2
    used = q_cols + 2 * k_cols
    router = jnp.pad(
        router_weight.reshape(shard, n, local), ((0, 0), (0, 0), (0, padded - local))
    ).reshape(shard, n * padded)
    gains = jnp.stack([attn_gain, ffn_gain], axis=1)
    gap = jnp.zeros((shard, wide - 128 - used), BF16)
    packed = jnp.concatenate(
        [
            o_weight, wq, wk, wv, gap, jnp.pad(gains, ((0, 0), (0, 6))), router,
            jnp.zeros((shard, 120 - n * padded), BF16),
        ],
        axis=1,
    )
    packed = lax.all_gather(packed, "dp").reshape(width, -1)
    hot = routes[:, :, None] == jnp.arange(n * local, dtype=jnp.int32)
    chosen = jnp.any(hot, axis=1).astype(F32).T.reshape(n, local, rows)
    chosen = jnp.pad(chosen, ((0, 0), (0, padded - local), (0, 0))).reshape(n * padded, rows)
    cosine, sine = rotary_tables(length)
    chips = lax.axis_size("dp") // 2

    cols = -(-used // 128) * 128
    tokens_all, w_all, stacked = gather_tokens(
        n, cols, tokens, q_weight, key_matrix, value_matrix, expert_gate, expert_up, expert_down
    )
    experts_w = lax.all_gather(stacked, "dp")
    norms, q, k, v, lse, out, att, cots, small, chosen_all = attend(
        n, kv_local, tokens_all, packed, cosine, sine, starts, cotangent, chosen
    )
    w_all, att = lax.optimization_barrier((w_all, att))
    w_all = lax.all_gather(w_all, "dp").reshape(width, n * cols)
    hidden, twos, two = mix(n, tokens, att, packed, small)
    grad_experts, back, gg, output = experts(
        n, chosen_all, small, twos, cots, cotangent, hidden, experts_w
    )
    expert_grads = lax.psum_scatter(grad_experts, "dp", scatter_dimension=0)
    grad_hidden, ga, sums_o, extra = give_back(
        n, chips, back, gg, chosen, small, hidden, two, cotangent, att, packed
    )
    input_grad, shares, o_grad = attend_back(
        n, kv_local, (q, k, v, lse, out), ga, starts, cosine, sine, norms, w_all, tokens,
        small, grad_hidden, extra, sums_o,
    )
    q_grad, k_grad, v_grad, o_grad, rest, gate_grad, up_grad, down_grad, output, input_grad = finish(
        n, key_matrix.shape[1], expert_down.shape[1], shares, o_grad, expert_grads, output, input_grad
    )
    router_grad = rest[:, 8 : 8 + n * padded].reshape(shard, n, padded)[:, :, :local]
    return (
        output, input_grad, rest[:, 0] / attn_gain.astype(F32), q_grad, k_grad, v_grad, o_grad,
        rest[:, 1], router_grad.reshape(shard, n * local), gate_grad, up_grad, down_grad,
    )


def solution(mesh):
    rows, split, expert = P(("dp", "expert"), None), P("dp", None), P("expert", "dp", None)
    return jax.shard_map(
        per_device,
        mesh=mesh,
        in_specs=(
            rows, P("dp"), split, split, split, split, P("dp"), split,
            expert, expert, expert, rows, split, rows,
        ),
        out_specs=(
            rows, rows, P("dp"), split, split, split, split, P("dp"), split,
            expert, expert, expert,
        ),
        check_vma=False,
    )
```

```python
import functools

import jax
import jax.numpy as jnp
import numpy as np
from jax import lax
from jax.experimental import pallas as pl
from jax.experimental.pallas import tpu as pltpu
from jax.sharding import PartitionSpec as P

MODEL_WIDTH = 1536
QUERY_HEADS = 24
KEY_VALUE_HEADS = 8
HEAD_SIZE = 64
TOPK = 8
PIECE_LEN = 256
EPSILON = 1e-05
THETA = 10000.0
BF16 = jnp.bfloat16
F32 = jnp.float32


def dot(left, right, dims=((1,), (0,))):
    return lax.dot_general(left, right, (dims, ((), ())), preferred_element_type=F32)


def dot_t(left, right):
    return dot(left, right, ((1,), (1,)))


def tdot(left, right):
    return dot(left, right, ((0,), (0,)))


DMA = pltpu.SemaphoreType.DMA
MESH = pl.DeviceIdType.MESH
LIMIT = 60 * 1024 * 1024


def barrier_all(n, me):
    barrier = pltpu.get_barrier_semaphore()
    for d in range(n):

        @pl.when(d != me)
        def _():
            pl.semaphore_signal(barrier, inc=1, device_id={"expert": d}, device_id_type=MESH)

    pl.semaphore_wait(barrier, n - 1)


def barrier_plane(n, me, chips, place):
    barrier = pltpu.get_barrier_semaphore()
    core, chip = place % 2, place // 2
    for d in range(n):

        @pl.when(d != me)
        def _():
            pl.semaphore_signal(barrier, inc=1, device_id={"expert": d}, device_id_type=MESH)

    pl.semaphore_signal(
        barrier, inc=1, device_id={"dp": place + 1 - 2 * core}, device_id_type=MESH
    )
    for c in range(chips):

        @pl.when(c != chip)
        def _():
            pl.semaphore_signal(
                barrier, inc=1, device_id={"dp": 2 * c + core}, device_id_type=MESH
            )

    pl.semaphore_wait(barrier, n - 1 + chips)


def remote(src, dst, send, recv, target, axis="expert"):
    return pltpu.make_async_remote_copy(
        src_ref=src, dst_ref=dst, send_sem=send, recv_sem=recv,
        device_id={axis: target}, device_id_type=MESH,
    )


class ChainGather:
    def __init__(self, n, me, slots, send, recv):
        self.n, self.me, self.slots, self.send, self.recv = n, me, slots, send, recv

    def copy(self, way, s, block, target):
        ref = self.slots.at[block]
        return remote(ref, ref, self.send.at[way, s], self.recv.at[way, s], target)

    def right(self, s):
        return self.copy(0, s, self.me - s, self.me + 1)

    def left(self, s):
        return self.copy(1, s, self.me + s, self.me - 1)

    def arrived(self, s):
        n, me = self.n, self.me

        @pl.when(me - 1 - s >= 0)
        def _():
            self.copy(0, s, me - 1 - s, me).wait_recv()

        @pl.when(me + 1 + s < n)
        def _():
            self.copy(1, s, me + 1 + s, me).wait_recv()

    def step(self, s):
        n, me = self.n, self.me
        if s >= 1:
            self.arrived(s - 1)

        @pl.when((me - s >= 0) & (me + 1 < n))
        def _():
            self.right(s).start()

        @pl.when((me + s < n) & (me > 0))
        def _():
            self.left(s).start()

    def finish(self):
        n, me = self.n, self.me
        self.arrived(n - 2)
        for s in range(n - 1):

            @pl.when((me - s >= 0) & (me + 1 < n))
            def _():
                self.right(s).wait_send()

            @pl.when((me + s < n) & (me > 0))
            def _():
                self.left(s).wait_send()


class Exchange:
    def __init__(self, n, me, source, slots, send, recv):
        self.n, self.me, self.source, self.slots = n, me, source, slots
        self.send, self.recv = send, recv

    def start(self, d):
        me = self.me

        @pl.when(d != me)
        def _():
            remote(
                self.source.at[d], self.slots.at[me], self.send.at[d], self.recv.at[me], d
            ).start()

    def finish(self):
        me = self.me
        for d in range(self.n):

            @pl.when(d != me)
            def _():
                desc = remote(
                    self.source.at[d], self.slots.at[d], self.send.at[d], self.recv.at[d], d
                )
                desc.wait_send()
                desc.wait_recv()


class PairReduce:
    def __init__(self, chips, place, parts, first, sums, second, near_sems, across_sems):
        self.chips, self.core, self.chip = chips, place % 2, place // 2
        self.partner = place + 1 - 2 * self.core
        self.parts, self.first, self.sums, self.second = parts, first, sums, second
        self.near_sems, self.across_sems = near_sems, across_sems

    def near(self, c):
        s, r = self.near_sems
        source = self.parts.at[2 * c + 1 - self.core]
        return remote(source, self.first.at[c], s.at[c], r.at[c], self.partner, "dp")

    def across(self, c, slot):
        s, r = self.across_sems
        return remote(
            self.sums.at[c], self.second.at[slot], s.at[c], r.at[slot], 2 * c + self.core, "dp"
        )

    def pair(self):
        for c in range(self.chips):
            self.near(c).start()

    def add(self):
        for c in range(self.chips):
            self.near(c).wait_recv()
            mine = self.parts[2 * c + self.core].astype(F32)
            self.sums[c] = (mine + self.first[c].astype(F32)).astype(BF16)

    def pair_sent(self):
        for c in range(self.chips):
            self.near(c).wait_send()

    def spread(self):
        for c in range(self.chips):

            @pl.when(c != self.chip)
            def _():
                self.across(c, self.chip).start()

    def finish(self, total):
        total[...] = self.sums[self.chip].astype(F32)
        for c in range(self.chips):

            @pl.when(c != self.chip)
            def _():
                self.across(c, self.chip).wait_send()
                self.across(c, c).wait_recv()
                total[...] += self.second[c].astype(F32)


def chain_sems(n):
    return [pltpu.SemaphoreType.DMA((2, n - 1)), pltpu.SemaphoreType.DMA((2, n - 1))]


def direct_sems(n):
    return [pltpu.SemaphoreType.DMA((n,)), pltpu.SemaphoreType.DMA((n,))]


def call(kernel, outs, scratch, ident, name, micros, args, far=(), keep=()):
    vmem, hbm = pl.BlockSpec(memory_space=pltpu.VMEM), pl.BlockSpec(memory_space=pltpu.HBM)
    smem = pl.BlockSpec(memory_space=pltpu.SMEM)
    nbytes = sum(a.size * a.dtype.itemsize for a in args)
    first, count = len(args), len(outs)

    def body(*refs):
        inside, results, rest = refs[:first], list(refs[first : first + count]), refs[first + count :]
        stages, rest = rest[: len(keep)], rest[len(keep) :]
        copies = {}
        if keep:
            for j, k in enumerate(keep):
                copies[k] = pltpu.make_async_copy(stages[j], results[k], rest[0].at[j])
                results[k] = stages[j]
            rest = rest[1:]

        def save(*which):
            for k in which:
                copies[k].start()

        kernel(*inside, *results, *rest, **(dict(save=save) if keep else {}))
        for k in keep:
            copies[k].wait()

    kept = [pltpu.VMEM(outs[k].shape, outs[k].dtype) for k in keep]
    return pl.pallas_call(
        body,
        in_specs=[
            hbm if j in far else smem if a.dtype == jnp.int32 else vmem for j, a in enumerate(args)
        ],
        out_specs=[hbm if k in keep else vmem for k in range(count)],
        out_shape=outs,
        scratch_shapes=kept + ([pltpu.SemaphoreType.DMA((len(keep),))] if keep else []) + scratch,
        compiler_params=pltpu.CompilerParams(
            collective_id=ident, has_side_effects=True, vmem_limit_bytes=LIMIT
        ),
        cost_estimate=pl.CostEstimate(
            flops=micros * 10**9, transcendentals=0, bytes_accessed=nbytes
        ),
        name=name,
    )(*args)


def stack_kernel(gate_ref, up_ref, down_ref, stack_ref):
    local, depth, width = down_ref.shape
    ff = gate_ref.shape[2]
    stack_ref[:local] = gate_ref[...]
    stack_ref[local : 2 * local] = up_ref[...]
    for j in range(width // ff):
        stack_ref[2 * local :, j * depth : (j + 1) * depth, :] = down_ref[
            :, :, j * ff : (j + 1) * ff
        ]


def stack(gate, up, down):
    local, shard, ff = gate.shape
    vmem = pl.BlockSpec(memory_space=pltpu.VMEM)
    return pl.pallas_call(
        stack_kernel,
        in_specs=[vmem] * 3,
        out_specs=vmem,
        out_shape=jax.ShapeDtypeStruct((3 * local, shard, ff), BF16),
        compiler_params=pltpu.CompilerParams(vmem_limit_bytes=LIMIT),
        cost_estimate=pl.CostEstimate(flops=3 * 10**9, transcendentals=0, bytes_accessed=6 * 10**6),
        name="stack",
    )(gate, up, down)


class PlaneGather:
    def __init__(self, chips, place, slots, sems):
        self.chips, self.core, self.chip, self.place = chips, place % 2, place // 2, place
        self.partner = place + 1 - 2 * self.core
        self.slots, self.sems = slots, sems

    def across(self, c, block):
        s, r, _, _ = self.sems
        ref = self.slots.at[block]
        return remote(ref, ref, s.at[c], r.at[block // 2], 2 * c + self.core, "dp")

    def near(self, block):
        _, _, s, r = self.sems
        ref = self.slots.at[block]
        return remote(ref, ref, s.at[block // 2], r.at[block // 2], self.partner, "dp")

    def start(self):
        self.near(self.place).start()
        for c in range(self.chips):

            @pl.when(c != self.chip)
            def _():
                self.across(c, self.place).start()

    def forward(self):
        for c in range(self.chips):

            @pl.when(c != self.chip)
            def _():
                block = 2 * c + self.core
                self.across(c, block).wait_recv()
                self.near(block).start()

    def finish(self):
        for c in range(self.chips):
            self.near(2 * c + self.core).wait_send()
            self.near(2 * c + 1 - self.core).wait_recv()

            @pl.when(c != self.chip)
            def _():
                self.across(c, self.place).wait_send()


def gather_kernel(
    n, tokens_ref, q_ref, k_ref, v_ref, o_ref, all_ref, heads_ref, o_all_ref, load, s0, r0, *sems, save
):
    me = lax.axis_index("expert")
    place = lax.axis_index("dp")
    chips = o_all_ref.shape[0] // 2
    rows = pltpu.make_async_copy(tokens_ref, all_ref.at[me], load.at[0])
    own = pltpu.make_async_copy(o_ref, o_all_ref.at[place], load.at[1])
    rows.start()
    own.start()
    barrier_plane(n, me, chips, place)
    chain = ChainGather(n, me, all_ref, s0, r0)
    weights = PlaneGather(chips, place, o_all_ref, sems)
    rows.wait()
    chain.step(0)
    own.wait()
    weights.start()
    cols = heads_ref.shape[1] // n
    at = 0
    if cols * n > q_ref.shape[1] + 2 * k_ref.shape[1]:
        heads_ref[...] = jnp.zeros_like(heads_ref)
    for ref in (q_ref, k_ref, v_ref):
        part = ref.shape[1] // n
        for z in range(n):
            heads_ref[:, z * cols + at : z * cols + at + part] = ref[:, z * part : (z + 1) * part]
        at += part
    save(1)
    for s in range(1, n - 1):
        chain.step(s)
    weights.forward()
    weights.finish()
    save(2)
    chain.finish()
    save(0)


def gather_tokens(n, cols, tokens, wq, wk, wv, wo):
    rows, width = tokens.shape
    shard = wq.shape[0]
    chips = width // shard // 2
    sds = jax.ShapeDtypeStruct
    return call(
        functools.partial(gather_kernel, n),
        [
            sds((n, rows, width), BF16), sds((shard, n * cols), BF16),
            sds((2 * chips, shard, width), BF16),
        ],
        [pltpu.SemaphoreType.DMA((2,))] + chain_sems(n) + direct_sems(chips) + direct_sems(chips),
        1, "gather_tokens", 60, (tokens, wq, wk, wv, wo), (0, 4), (0, 1, 2),
    )


def turn(x, cosine, sine):
    half = HEAD_SIZE // 2
    tiles = []
    for c in range(0, x.shape[1], 128):
        tile = x[:, c : c + 128]
        lane = lax.broadcasted_iota(jnp.int32, tile.shape, 1) % HEAD_SIZE
        other = jnp.where(lane < half, pltpu.roll(tile, 128 - half, 1), pltpu.roll(tile, half, 1))
        tiles.append(tile * cosine + other * sine)
    return jnp.concatenate(tiles, axis=1)


def bias_rows(starts_ref, q_pos, k_pos):
    seen = k_pos <= q_pos
    for k in range(starts_ref.shape[1]):
        a = starts_ref[0, k]
        q_in = (q_pos >= a) & (q_pos < a + PIECE_LEN)
        k_in = (k_pos >= a) & (k_pos < a + PIECE_LEN)
        seen = seen | (q_in & k_in)
    return jnp.where(seen, 0.0, -1e30)


def reach_of(block, rows, length, pieces):
    span = length // pieces
    return min(length, -(-((block + 1) * rows) // span) * span)


def attend_kernel(
    n, kv_local, tokens_ref, packed_ref, cos_ref, sin_ref, starts_ref, cot_ref,
    chosen_ref, norm_ref, q_ref, k_ref, v_ref, lse_ref, out_ref, att_ref, cots_ref, small_ref,
    every_ref, w_s, send_att, send_chosen, load, s0, r0, s1, r1, s2, r2, *, save,
):
    me = lax.axis_index("expert")
    per_key, length, tile = q_ref.shape
    rows = length // n
    q_cols, k_cols = per_key * tile, tile
    width, wide = w_s.shape
    weights = pltpu.make_async_copy(packed_ref, w_s, load)
    weights.start()
    barrier_all(n, me)
    cots_ref[me] = cot_ref[:, : cots_ref.shape[2]]
    chain = ChainGather(n, me, cots_ref, s0, r0)
    chain.step(0)
    swap = Exchange(n, me, send_att, att_ref, s1, r1)
    choice = Exchange(n, me, send_chosen, every_ref, s2, r2)
    every_ref[me] = chosen_ref[...]
    for d in range(n):
        send_chosen[d] = chosen_ref[...]
        choice.start(d)
    pieces = starts_ref.shape[1]
    weights.wait()
    small = w_s[:, wide - 128 :].astype(F32).T
    small_ref[...] = small[: small_ref.shape[0], :]
    save(8)
    gain = small[:1, :]
    lane = lax.broadcasted_iota(jnp.int32, (rows, tile), 1)
    lane_w = lax.broadcasted_iota(jnp.int32, (rows, 128), 1)
    for i in range(n):
        part = slice(i * rows, (i + 1) * rows)
        x = tokens_ref[i].astype(F32)
        inverse = lax.rsqrt(jnp.mean(x * x, axis=1, keepdims=True) + EPSILON)
        norm = (x * inverse * gain).astype(BF16)
        norm_ref[i] = norm
        qkv = dot(norm, w_s[:, : wide - 128])
        qk = turn(qkv[:, : q_cols + k_cols], cos_ref[part, :], sin_ref[part, :]).astype(BF16)
        v_ref[part, :] = qkv[:, q_cols + k_cols : q_cols + 2 * k_cols].astype(BF16)
        k_ref[part, :] = qk[:, q_cols:]
        q = (qk[:, :q_cols].astype(F32) * HEAD_SIZE ** (-0.5)).astype(BF16)
        for t in range(per_key):
            for g in range(kv_local):
                at = (g * per_key + t) * HEAD_SIZE
                q_ref[t, part, g * HEAD_SIZE : (g + 1) * HEAD_SIZE] = q[:, at : at + HEAD_SIZE]
    save(0, 1, 2, 3)
    if n > 2:
        chain.step(1)
    for i in range(n):
        reach = reach_of(i, rows, length, pieces)
        part = slice(i * rows, (i + 1) * rows)
        q_pos = lax.broadcasted_iota(jnp.int32, (rows, reach), 0) + i * rows
        k_pos = lax.broadcasted_iota(jnp.int32, (rows, reach), 1)
        bias = bias_rows(starts_ref, q_pos, k_pos)
        keys, values = k_ref[:reach, :], v_ref[:reach, :]
        k_lane = lax.broadcasted_iota(jnp.int32, (reach, tile), 1)

        def head(t, logs):
            q = q_ref[t, part, :]
            total = jnp.zeros((rows, tile), F32)
            for g in range(kv_local):
                mine = lane // HEAD_SIZE == g
                scores = dot_t(jnp.where(mine, q, jnp.zeros_like(q)), keys) + bias
                top = jnp.max(scores, axis=1, keepdims=True)
                powers = jnp.exp(scores - top)
                norm = jnp.sum(powers, axis=1, keepdims=True)
                value = jnp.where(k_lane // HEAD_SIZE == g, values, jnp.zeros_like(values))
                total = total + dot(powers.astype(BF16), value) * (1.0 / norm)
                logs = jnp.where(lane_w == t * kv_local + g, top + jnp.log(norm), logs)
            out_ref[t, part, :] = total
            return logs

        logs = lax.fori_loop(0, per_key, head, jnp.zeros((rows, 128), F32))
        lse_ref[:, part] = logs.T[: lse_ref.shape[0], :]
        for t in range(per_key):
            for g in range(kv_local):
                at = (g * per_key + t) * HEAD_SIZE
                send_att[i, :, at : at + HEAD_SIZE] = out_ref[
                    t, part, g * HEAD_SIZE : (g + 1) * HEAD_SIZE
                ].astype(BF16)
        swap.start(i)
        if i + 2 < n - 1:
            chain.step(i + 2)
    save(4, 5)
    att_ref[me] = send_att[me]
    choice.finish()
    chain.finish()
    save(7, 9)
    swap.finish()


def attend(n, kv_local, tokens_all, packed, cosine, sine, starts, cot, chosen):
    rows, width = cot.shape
    length = n * rows
    tile = kv_local * HEAD_SIZE
    per_key = QUERY_HEADS // KEY_VALUE_HEADS
    q_cols = per_key * tile
    wide = packed.shape[1]
    sds = jax.ShapeDtypeStruct
    lse_rows = -(-per_key * kv_local // 8) * 8
    return call(
        functools.partial(attend_kernel, n, kv_local),
        [
            sds((n, rows, width), BF16),
            sds((per_key, length, tile), BF16),
            sds((length, tile), BF16),
            sds((length, tile), BF16),
            sds((lse_rows, length), F32),
            sds((per_key, length, tile), F32),
            sds((n, rows, q_cols), BF16),
            sds((n, rows, width // 2), BF16),
            sds((8 + chosen.shape[0], width), F32),
            sds((n,) + chosen.shape, F32),
        ],
        [
            pltpu.VMEM((width, wide), BF16), pltpu.VMEM((n, rows, q_cols), BF16),
            pltpu.VMEM((n,) + chosen.shape, F32), DMA,
        ]
        + chain_sems(n) + direct_sems(n) + direct_sems(n),
        2, "attend", 80,
        (tokens_all, packed, cosine, sine, starts, cot, chosen), (1,),
        (0, 1, 2, 3, 4, 5, 7, 8, 9),
    )


def mix_kernel(
    n, tokens_ref, att_ref, packed_ref, small_ref, hidden_ref, norms_ref, own_ref, w_s, load, s0, r0, *, save
):
    me = lax.axis_index("expert")
    q_cols = att_ref.shape[2]
    width = w_s.shape[0]
    weights = pltpu.make_async_copy(packed_ref, w_s, load)
    weights.start()
    hidden = tokens_ref[...].astype(F32)
    weights.wait()
    for s in range(n):
        hidden = hidden + dot(att_ref[s], w_s[s * q_cols : (s + 1) * q_cols, :])
    hidden_ref[...] = hidden
    inverse = lax.rsqrt(jnp.mean(hidden * hidden, axis=1, keepdims=True) + EPSILON)
    norm = (hidden * inverse * small_ref[1:2, :]).astype(BF16)
    own_ref[...] = norm
    barrier_all(n, me)
    norms_ref[me] = norm
    chain = ChainGather(n, me, norms_ref, s0, r0)
    chain.step(0)
    save(0, 2)
    for s in range(1, n - 1):
        chain.step(s)
    chain.finish()
    save(1)


def mix(n, tokens, att, w_o, small):
    rows, width = tokens.shape
    sds = jax.ShapeDtypeStruct
    return call(
        functools.partial(mix_kernel, n),
        [sds((rows, width), F32), sds((n, rows, width), BF16), sds((rows, width), BF16)],
        [pltpu.VMEM((width, width), BF16), DMA] + chain_sems(n),
        3, "mix", 60, (tokens, att, w_o, small), (2,), (0, 1, 2),
    )


class ChainReduce:
    def __init__(self, n, me, parts, slots, send, recv):
        self.n, self.me, self.parts = n, me, parts
        self.slots, self.send, self.recv = slots, send, recv

    def copy(self, way, s, d, source):
        target = self.me + 1 if way == 0 else self.me - 1
        slot = d if way == 0 else jnp.where(d == target, self.n, d)
        return remote(
            source.at[d], self.slots.at[slot], self.send.at[way, s], self.recv.at[way, s], target
        )

    def far(self, way):
        return self.me if way == 0 else self.n - 1 - self.me

    def step(self, when):
        for way in (0, 1):
            far = self.far(way)
            s = when - far
            d = self.n - 1 - s if way == 0 else s
            slots = self.slots

            @pl.when(s >= 0)
            def _():
                @pl.when(far == 0)
                def _():
                    self.copy(way, s, d, self.parts).start()

                @pl.when(far > 0)
                def _():
                    self.copy(way, s, d, slots).wait_recv()
                    slots[d] = (slots[d].astype(F32) + self.parts[d].astype(F32)).astype(BF16)
                    self.copy(way, s, d, slots).start()

            if when > 0:

                @pl.when(s > 0)
                def _():
                    self.copy(way, s - 1, d, slots).wait_send()

    def finish(self, total):
        n, me = self.n, self.me
        total[...] = self.parts[me].astype(F32)
        for way in (0, 1):
            far = self.far(way)

            @pl.when(far > 0)
            def _():
                self.copy(way, n - 1 - far, me, self.slots).wait_recv()
                total[...] += self.slots[me if way == 0 else n].astype(F32)

            @pl.when(far < n - 1)
            def _():
                self.copy(way, n - 2 - far, me, self.slots).wait_send()


def rms_back(grad, rows, gain):
    inverse = lax.rsqrt(jnp.mean(rows * rows, axis=1, keepdims=True) + EPSILON)
    scaled = grad * gain
    grad_gain = jnp.sum(grad * rows * inverse, axis=0, keepdims=True)
    mean = jnp.mean(scaled * rows, axis=1, keepdims=True)
    return inverse * scaled - rows * (inverse * inverse * inverse * mean), grad_gain


def softmax_chosen(logits, chosen):
    top = jnp.max(jnp.where(chosen > 0.0, logits, -1e30), axis=0, keepdims=True)
    powers = jnp.where(chosen > 0.0, jnp.exp(jnp.where(chosen > 0.0, logits - top, 0.0)), 0.0)
    return powers / jnp.sum(powers, axis=0, keepdims=True)


def return_kernel(
    n, parts_ref, gg_ref, chosen_ref, small_ref, hidden_ref, norm_ref, cot_ref, att_ref, packed_ref,
    grad_ref, ga_ref, o_ref, extra_ref,
    w_s, slots, total, gg_s, send_ga, o_parts, o_first, load, s0, r0, s1, r1, s2, r2, *near, save,
):
    me = lax.axis_index("expert")
    place = lax.axis_index("dp")
    chips = o_ref.shape[0]
    width = w_s.shape[0]
    q_cols = ga_ref.shape[2]
    weights = pltpu.make_async_copy(packed_ref, w_s, load)
    weights.start()
    barrier_plane(n, me, chips, place)
    chain = ChainReduce(n, me, parts_ref, slots, s0, r0)
    chain.step(0)
    gates_swap = Exchange(n, me, gg_ref, gg_s, s1, r1)
    for d in range(n):
        gates_swap.start(d)
    gg_s[me] = gg_ref[me]
    router = small_ref[8:, :].astype(BF16)
    gates = softmax_chosen(dot_t(router, norm_ref[...]), chosen_ref[...])
    gates_swap.finish()
    grad_gates = gg_s[...].reshape(gates.shape)
    middle = jnp.sum(gates * grad_gates, axis=0, keepdims=True)
    grad_logits = (gates * (grad_gates - middle)).astype(BF16)
    extra_ref[8:, :] = dot(grad_logits, norm_ref[...])
    for s in range(1, n - 1):
        chain.step(s)
    chain.finish(total)
    grad_norm = total[...] + tdot(grad_logits, router)
    grad, grad_gain = rms_back(grad_norm, hidden_ref[...], small_ref[1:2, :])
    row = lax.broadcasted_iota(jnp.int32, (8, width), 0)
    extra_ref[:8, :] = jnp.where(row == 1, grad_gain, 0.0)
    grad = cot_ref[...].astype(F32) + grad
    grad_ref[...] = grad
    save(0, 3)
    proj = grad.astype(BF16)
    weights.wait()
    swap = Exchange(n, me, send_ga, ga_ref, s2, r2)
    for d in range(n):
        send_ga[d] = dot_t(proj, w_s[d * q_cols : (d + 1) * q_cols, :]).astype(BF16)
        swap.start(d)
    ga_ref[me] = send_ga[me]
    shard = o_parts.shape[1]
    for d in range(n):
        grad_o = tdot(att_ref[d], proj).astype(BF16)
        o_parts[d * q_cols // shard : (d + 1) * q_cols // shard] = grad_o.reshape(-1, shard, width)
    o_sum = PairReduce(chips, place, o_parts, o_first, o_ref, None, near, None)
    o_sum.pair()
    o_sum.add()
    save(2)
    o_sum.pair_sent()
    swap.finish()
    save(1)


def give_back(n, chips, parts, gg, chosen, small, hidden, norm, cot, att, w_o):
    rows, width = cot.shape
    q_cols = att.shape[2]
    shard = width // (2 * chips)
    sds, vm = jax.ShapeDtypeStruct, pltpu.VMEM
    return call(
        functools.partial(return_kernel, n),
        [
            sds((rows, width), F32), sds(att.shape, BF16), sds((chips, shard, width), BF16),
            sds(small.shape, F32),
        ],
        [
            vm((width, width), BF16), vm((n + 1, rows, width), BF16),
            vm((rows, width), F32), vm(gg.shape, F32), vm((n, rows, q_cols), BF16),
            vm((2 * chips, shard, width), BF16), vm((chips, shard, width), BF16), DMA,
        ]
        + chain_sems(n) + direct_sems(n) + direct_sems(n) + direct_sems(chips),
        4, "give_back", 80,
        (parts, gg, chosen, small, hidden, norm, cot, att, w_o), (8,), (0, 1, 2, 3),
    )


def attend_back_kernel(
    n, kv_local, q_ref, k_ref, v_ref, lse_ref, out_ref, ga_ref, starts_ref, cos_ref,
    sin_ref, norm_ref, all_ref, tokens_ref, small_ref, grad_ref, extra_ref, o_ref,
    input_ref, shares_ref, og_ref,
    w_s, gq_s, gk_s, gv_s, gqkv_s, ga_s, q_send, q_got, kv_send, kv_got, load,
    o_second, o_total, o_send, o_got, dw_s, w_first, w_sums, w_second, w_total,
    s0, r0, s1, r1, s2, r2, s3, r3, s4, r4, *sems,
):
    me = lax.axis_index("expert")
    place = lax.axis_index("dp")
    per_key, length, tile = q_ref.shape
    chips, shard, _ = o_ref.shape
    rows = length // n
    q_cols, k_cols = per_key * tile, tile
    width = w_s.shape[0]
    cols = w_s.shape[1] // n
    scale = HEAD_SIZE ** (-0.5)
    pieces = starts_ref.shape[1]
    weights = pltpu.make_async_copy(all_ref, w_s, load)
    weights.start()
    barrier_plane(n, me, chips, place)
    o_sum = PairReduce(chips, place, None, None, o_ref, o_second, None, sems[:2])
    o_sum.spread()
    q_swap = Exchange(n, me, q_send, q_got, s0, r0)
    kv_swap = Exchange(n, me, kv_send, kv_got, s1, r1)
    o_swap = Exchange(n, me, o_send, o_got, s2, r2)
    o_share = ChainGather(n, me, og_ref, s3, r3)
    w_share = ChainGather(n, me, shares_ref, s4, r4)
    gq_s[...] = jnp.zeros_like(gq_s)
    gqkv_s[...] = jnp.zeros_like(gqkv_s)
    gk_s[...] = jnp.zeros_like(gk_s)
    gv_s[...] = jnp.zeros_like(gv_s)
    lane = lax.broadcasted_iota(jnp.int32, (rows, tile), 1)
    lane_w = lax.broadcasted_iota(jnp.int32, (rows, 128), 1)
    for i in range(n):
        reach = reach_of(i, rows, length, pieces)
        part = slice(i * rows, (i + 1) * rows)
        deltas = jnp.zeros((rows, 128), F32)
        for t in range(per_key):
            for g in range(kv_local):
                at = (g * per_key + t) * HEAD_SIZE
                ga_s[t, :, g * HEAD_SIZE : (g + 1) * HEAD_SIZE] = ga_ref[i, :, at : at + HEAD_SIZE]
            product = ga_s[t].astype(F32) * out_ref[t, part, :]
            for g in range(kv_local):
                own = jnp.where(lane // HEAD_SIZE == g, product, 0.0)
                deltas = jnp.where(
                    lane_w == t * kv_local + g, jnp.sum(own, axis=1, keepdims=True), deltas
                )
        delta_s = deltas.T
        k_pos = lax.broadcasted_iota(jnp.int32, (reach, rows), 0)
        q_pos = lax.broadcasted_iota(jnp.int32, (reach, rows), 1) + i * rows
        bias = bias_rows(starts_ref, q_pos, k_pos)
        keys, values = k_ref[:reach, :], v_ref[:reach, :]
        k_lane = lax.broadcasted_iota(jnp.int32, (reach, tile), 1)
        for t in range(per_key):
            q, ga = q_ref[t, part, :], ga_s[t]
            grad_q = jnp.zeros((rows, tile), F32)
            for g in range(kv_local):
                h = t * kv_local + g
                mine = lane // HEAD_SIZE == g
                q_g = jnp.where(mine, q, jnp.zeros_like(q))
                ga_g = jnp.where(mine, ga, jnp.zeros_like(ga))
                scores = dot_t(keys, q_g) + bias
                probs = jnp.exp(scores - lse_ref[h : h + 1, part])
                grad_probs = dot_t(values, ga_g)
                grad_raw = (probs * (grad_probs - delta_s[h : h + 1, :])).astype(BF16)
                gk_s[:reach, :tile] += dot(grad_raw, q_g)
                gv_s[:reach, :] += dot(probs.astype(BF16), ga_g)
                key = jnp.where(k_lane // HEAD_SIZE == g, keys, jnp.zeros_like(keys))
                grad_q = grad_q + tdot(grad_raw, key)
            for g in range(kv_local):
                at = (g * per_key + t) * HEAD_SIZE
                gq_s[:, at : at + HEAD_SIZE] = (
                    grad_q[:, g * HEAD_SIZE : (g + 1) * HEAD_SIZE] * scale
                )
        turned = turn(gq_s[...], cos_ref[part, :], -sin_ref[part, :])[:, :q_cols].astype(BF16)
        gqkv_s[part, :q_cols] = turned
        q_send[i] = turned
        q_swap.start(i)
    for i in range(n):
        part = slice(i * rows, (i + 1) * rows)
        turned = turn(gk_s[part, :], cos_ref[part, :], -sin_ref[part, :])[:, :k_cols].astype(BF16)
        kv_send[i, :, :k_cols] = turned
        kv_send[i, :, k_cols:] = gv_s[part, :].astype(BF16)
        kv_swap.start(i)
        gqkv_s[part, q_cols : q_cols + 2 * k_cols] = kv_send[i]
    weights.wait()
    norms = norm_ref[...].reshape(length, width)
    dw = tdot(norms, gqkv_s[...])
    own = w_s[:, pl.ds(pl.multiple_of(me * cols, 128), cols)].astype(F32)
    grad_gain = jnp.sum(dw * own, axis=1, keepdims=True)
    dw_s[:, :, :cols] = dw.astype(BF16).reshape(2 * chips, shard, cols)
    extra = extra_ref[...]
    extra = jnp.concatenate([extra, jnp.zeros((128 - extra.shape[0], width), F32)], axis=0).T
    lane_e = lax.broadcasted_iota(jnp.int32, extra.shape, 1)
    extra = jnp.where(lane_e == 0, grad_gain, extra)
    dw_s[:, :, cols:] = extra.astype(BF16).reshape(2 * chips, shard, 128)
    w_sum = PairReduce(chips, place, dw_s, w_first, w_sums, w_second, sems[2:4], sems[4:])
    w_sum.pair()
    o_sum.finish(o_total)
    piece = width // n
    for d in range(n):
        o_send[d] = o_total[:, d * piece : (d + 1) * piece].astype(BF16)
        o_swap.start(d)
    w_sum.add()
    w_sum.spread()
    q_got[me] = q_send[me]
    kv_got[me] = kv_send[me]
    q_swap.finish()
    kv_swap.finish()
    grad_norm = jnp.zeros((rows, width), F32)
    for z in range(n):
        grad_norm = grad_norm + dot_t(q_got[z], w_s[:, z * cols : z * cols + q_cols])
        grad_norm = grad_norm + dot_t(
            kv_got[z], w_s[:, z * cols + q_cols : z * cols + q_cols + 2 * k_cols]
        )
    grad, _ = rms_back(grad_norm, tokens_ref[...].astype(F32), small_ref[:1, :])
    input_ref[...] = (grad_ref[...] + grad).astype(BF16)
    o_swap.finish()
    mine = o_send[me].astype(F32)
    for d in range(n):
        mine = mine + jnp.where(d == me, 0.0, o_got[d].astype(F32))
    og_ref[me] = mine.astype(BF16)
    o_share.step(0)
    w_sum.pair_sent()
    w_sum.finish(w_total)
    shares_ref[me] = w_total[...].astype(BF16)
    w_share.step(0)
    for s in range(1, n - 1):
        o_share.step(s)
        w_share.step(s)
    o_share.finish()
    w_share.finish()


def attend_back(
    n, kv_local, saved, ga, starts, cosine, sine, norms, w_all, tokens, small, grad, extra, sums_o
):
    q, k, v, lse, out = saved
    rows, width = tokens.shape
    per_key, length, tile = q.shape
    chips, shard, _ = sums_o.shape
    cols = w_all.shape[1] // n
    wide = cols + 128
    sds, vm = jax.ShapeDtypeStruct, pltpu.VMEM
    q_cols = per_key * tile
    across_w = vm((chips, shard, wide), BF16)
    piece = vm((n, shard, width // n), BF16)
    q_block, kv_block = vm((n, rows, q_cols), BF16), vm((n, rows, 2 * tile), BF16)
    return call(
        functools.partial(attend_back_kernel, n, kv_local),
        [
            sds((rows, width), BF16), sds((n, shard, wide), BF16),
            sds((n, shard, width // n), BF16),
        ],
        [
            vm(w_all.shape, BF16), vm((rows, -(-q_cols // 128) * 128), F32), vm((length, 128), F32),
            vm((length, tile), F32), vm((length, cols), BF16), vm((per_key, rows, tile), BF16),
            q_block, q_block, kv_block, kv_block, DMA,
            vm((chips, shard, width), BF16), vm((shard, width), F32), piece, piece,
            vm((2 * chips, shard, wide), BF16), across_w, across_w, across_w,
            vm((shard, wide), F32),
        ]
        + direct_sems(n) + direct_sems(n) + direct_sems(n) + chain_sems(n) + chain_sems(n)
        + direct_sems(chips) + direct_sems(chips) + direct_sems(chips),
        5, "attend_back", 90,
        (q, k, v, lse, out, ga, starts, cosine, sine, norms, w_all, tokens, small, grad, extra,
         sums_o),
        (10,),
    )


def expert_kernel(
    n, chosen_ref, small_ref, n2_ref, cots_ref, cot_ref, hidden_ref, wg_ref, wu_ref, wd_ref,
    dw_ref, gx_ref, gg_ref, output_ref,
    x_s, g_s, slope_s, silu_s, act_s, gact_s, ggp_s, gup_s, pick_s, mix_s, y_s, y_slots,
    total, gate_s, rank_s, rest_s, s0, r0, s1, r1,
):
    me = lax.axis_index("expert")
    _, rows, width = n2_ref.shape
    local, tall, ff = act_s.shape
    cap = tall // n
    shards = wg_ref.shape[0]
    depth = ff // shards
    blocks = width // ff
    at = pl.program_id(0)
    later = jnp.maximum(at - local, 0)
    e = jnp.where(at < local, at, later // 3)
    phase = jnp.where(at < local, -1, later % 3)
    mine = me * gg_ref.shape[1] + e
    where = pl.ds(pl.multiple_of(e * cap, cap), cap)
    chain = ChainReduce(n, me, y_s, y_slots, s0, r0)
    more = ChainGather(n, me, rest_s, s1, r1)
    half = cots_ref.shape[2]

    def whole(ref):
        return ref[...].reshape(width, ff)

    def down(j):
        return wd_ref[:, 0, j * depth : (j + 1) * depth, :].reshape(ff, ff)

    def gate_column(s, pick):
        return jnp.sum(jnp.where(pick, gate_s[s, pl.ds(mine, 1), :], 0.0), axis=1, keepdims=True)

    @pl.when(at == 0)
    def _():
        barrier_all(n, me)
        rest_s[me] = cot_ref[:, half:]
        more.step(0)
        before = lax.broadcasted_iota(jnp.int32, (rows, rows), 0)
        upto = jnp.where(before <= lax.broadcasted_iota(jnp.int32, (rows, rows), 1), 1.0, 0.0)
        router = small_ref[8:, :].astype(BF16)
        for s in range(n):
            chosen = chosen_ref[s]
            gate_s[s] = softmax_chosen(dot_t(router, n2_ref[s]), chosen)
            count = dot(chosen.astype(BF16), upto.astype(BF16))
            rank_s[s] = jnp.where(chosen > 0.0, count - 1.0, -1.0).astype(jnp.int32)
        gg_ref[...] = jnp.zeros_like(gg_ref)

    for s in range(1, n - 1):

        @pl.when(at == min((s * local + n - 2) // (n - 1), local - 1))
        def _():
            more.step(s)

    @pl.when(phase < 0)
    def _():
        slot = lax.broadcasted_iota(jnp.int32, (cap, rows), 0)
        cols = []
        for s in range(n):
            pick = slot == rank_s[s, pl.ds(mine, 1), :]
            hot = jnp.where(pick, 1.0, 0.0).astype(BF16)
            pick_s[s, where, :] = hot
            cols.append(gate_column(s, pick))
            x_s[s * cap : (s + 1) * cap, :] = dot(hot, n2_ref[s]).astype(BF16)
        x = x_s[...]
        gp = dot(x, whole(wg_ref))
        up = dot(x, whole(wu_ref))
        sigma = jax.nn.sigmoid(gp)
        silu = gp * sigma
        act = (silu * up).astype(BF16)
        act_s[e] = act
        silu_s[e] = silu.astype(BF16)
        slope_s[e] = (up * sigma * (1.0 + gp * (1.0 - sigma))).astype(BF16)
        for j in range(blocks):
            lanes = slice(j * ff, (j + 1) * ff)
            res = dot(act, down(j)).astype(BF16).astype(F32)
            for s in range(n):
                mix_s[s, where, lanes] = (cols[s] * res[s * cap : (s + 1) * cap, :]).astype(BF16)

    @pl.when(at == local - 1)
    def _():
        for s in range(n):
            y_s[s] = tdot(pick_s[s], mix_s[s]).astype(BF16)

    for s in range(n - 1):

        @pl.when(at == local + s * 3 * local // (n - 1))
        def _():
            chain.step(s)

    @pl.when(at == local)
    def _():
        more.finish()

    @pl.when(phase == 0)
    def _():
        for s in range(n):
            hot = pick_s[s, where, :]
            x_s[s * cap : (s + 1) * cap, :] = dot(hot, n2_ref[s]).astype(BF16)
            g_s[s * cap : (s + 1) * cap, :half] = dot(hot, cots_ref[s]).astype(BF16)
            g_s[s * cap : (s + 1) * cap, half:] = dot(hot, rest_s[s]).astype(BF16)
        grad_act = jnp.zeros((tall, ff), F32)
        for j in range(blocks):
            grad_act = grad_act + dot_t(g_s[:, j * ff : (j + 1) * ff], down(j))
        act = act_s[e].astype(F32)
        sums = jnp.sum(act * grad_act, axis=1, keepdims=True)
        cols = []
        for s in range(n):
            pick = pick_s[s, where, :].astype(F32) > 0.5
            cols.append(gate_column(s, pick))
            part = sums[s * cap : (s + 1) * cap, :]
            gg_ref[s, pl.ds(e, 1), :] = jnp.sum(jnp.where(pick, part, 0.0), axis=0, keepdims=True)
        col = jnp.concatenate(cols, axis=0)
        grad_act = grad_act * col
        gact_s[...] = (act * col).astype(BF16)
        ggp = (grad_act * slope_s[e].astype(F32)).astype(BF16)
        ggp_s[...] = ggp
        gup_s[...] = (grad_act * silu_s[e].astype(F32)).astype(BF16)
        dw_ref[...] = tdot(x_s[...], ggp).astype(BF16).reshape(dw_ref.shape)

    @pl.when(phase == 1)
    def _():
        dw_ref[...] = tdot(x_s[...], gup_s[...]).astype(BF16).reshape(dw_ref.shape)
        grows = dot_t(ggp_s[...], whole(wg_ref)) + dot_t(gup_s[...], whole(wu_ref))
        grows = grows.astype(BF16)
        for s in range(n):
            mix_s[s, where, :] = grows[s * cap : (s + 1) * cap, :]

    @pl.when(phase == 2)
    def _():
        for j in range(blocks):
            grad = tdot(gact_s[...], g_s[:, j * ff : (j + 1) * ff]).astype(BF16)
            dw_ref[:, 0, j * depth : (j + 1) * depth, :] = grad.reshape(shards, depth, ff)

    @pl.when(at == 4 * local - 1)
    def _():
        for s in range(n):
            gx_ref[s] = tdot(pick_s[s], mix_s[s]).astype(BF16)
        chain.finish(total)
        output_ref[...] = (hidden_ref[...] + total[...]).astype(BF16)


def experts(n, chosen, small, n2, cots, cot, hidden, w):
    _, rows, width = n2.shape
    shards, local, depth, ff = w.shape
    local = local // 3
    cap = rows * TOPK * 5 // (4 * local * n)
    tall = n * cap
    padded = chosen.shape[1] // n
    once = pl.Buffered(1)

    def const(shape):
        return pl.BlockSpec(shape, lambda i: (0,) * len(shape), pipeline_mode=once)

    def place(i):
        later = jnp.maximum(i - local, 0)
        return jnp.where(i < local, i, later // 3), later % 3

    def weight(k):
        return pl.BlockSpec((shards, 1, depth, ff), lambda i: (0, k * local + place(i)[0], 0, 0))

    def grads(i):
        later = jnp.maximum(i - local, 0)
        return (0, later % 3 * local + later // 3, 0, 0)

    sds, vm = jax.ShapeDtypeStruct, pltpu.VMEM
    saved, half = vm((local, tall, ff), BF16), vm((tall, ff), BF16)
    return pl.pallas_call(
        functools.partial(expert_kernel, n),
        grid=(4 * local,),
        in_specs=[
            const(chosen.shape), const(small.shape), const(n2.shape), const(cots.shape),
            const(cot.shape), const(hidden.shape), weight(0), weight(1), weight(2),
        ],
        out_specs=[
            pl.BlockSpec((shards, 1, depth, ff), grads),
            const(n2.shape), const((n, padded, rows)), const(hidden.shape),
        ],
        out_shape=[
            sds(w.shape, BF16), sds(n2.shape, BF16), sds((n, padded, rows), F32),
            sds(hidden.shape, BF16),
        ],
        scratch_shapes=[
            vm((tall, width), BF16), vm((tall, width), BF16), saved, saved, saved, half, half, half,
            vm((n, local * cap, rows), BF16), vm((n, local * cap, width), BF16), vm(n2.shape, BF16),
            vm((n + 1, rows, width), BF16), vm(hidden.shape, F32), vm(chosen.shape, F32), vm(chosen.shape, jnp.int32),
            vm((n, rows, width - cots.shape[2]), BF16),
        ]
        + chain_sems(n) + chain_sems(n),
        compiler_params=pltpu.CompilerParams(
            collective_id=6, has_side_effects=True, vmem_limit_bytes=LIMIT,
            dimension_semantics=("arbitrary",),
        ),
        cost_estimate=pl.CostEstimate(
            flops=95 * 10**9, transcendentals=0, bytes_accessed=60 * 10**6
        ),
        name="experts",
    )(chosen, small, n2, cots, cot, hidden, w, w, w)


def finish_kernel(
    n, shares_far, pieces_far, sums_far, y_far, grad_far, q_ref, k_ref, v_ref, o_ref, small_ref,
    gate_ref, up_ref, down_ref, output_ref, input_ref, shares_ref, pieces_ref, sums_ref, sems,
):
    copies = [
        pltpu.make_async_copy(source, target, sems.at[j])
        for j, (source, target) in enumerate(
            (
                (shares_far, shares_ref), (pieces_far, pieces_ref), (sums_far, sums_ref),
                (y_far, output_ref), (grad_far, input_ref),
            )
        )
    ]
    for copy in copies:
        copy.start()
    for copy in copies:
        copy.wait()
    q_cols, k_cols = q_ref.shape[1] // n, k_ref.shape[1] // n
    piece = pieces_ref.shape[2]
    cols = shares_ref.shape[2] - 128
    small = jnp.zeros(small_ref.shape, F32)
    for z in range(n):
        at = 0
        for ref, part in ((q_ref, q_cols), (k_ref, k_cols), (v_ref, k_cols)):
            ref[:, z * part : (z + 1) * part] = shares_ref[z, :, at : at + part].astype(F32)
            at += part
        small = small + shares_ref[z, :, cols:].astype(F32)
        o_ref[:, z * piece : (z + 1) * piece] = pieces_ref[z].astype(F32)
    small_ref[...] = small
    local, depth, _ = down_ref.shape
    ff = gate_ref.shape[2]
    gate_ref[...] = sums_ref[:local].astype(F32)
    up_ref[...] = sums_ref[local : 2 * local].astype(F32)
    for j in range(down_ref.shape[2] // ff):
        down_ref[:, :, j * ff : (j + 1) * ff] = sums_ref[
            2 * local :, j * depth : (j + 1) * depth, :
        ].astype(F32)


def finish(n, k_width, depth, shares, pieces, sums, y, grad):
    _, shard, _ = shares.shape
    width = y.shape[1]
    local, ff = sums.shape[0] // 3, sums.shape[2]
    sds = jax.ShapeDtypeStruct
    square, narrow, expert = (
        sds((shard, width), F32), sds((shard, k_width), F32), sds((local, shard, ff), F32)
    )
    vmem, hbm = pl.BlockSpec(memory_space=pltpu.VMEM), pl.BlockSpec(memory_space=pltpu.HBM)
    return pl.pallas_call(
        functools.partial(finish_kernel, n),
        in_specs=[hbm] * 5,
        out_specs=[vmem] * 10,
        scratch_shapes=[
            pltpu.VMEM(a.shape, BF16) for a in (shares, pieces, sums)
        ] + [pltpu.SemaphoreType.DMA((5,))],
        out_shape=[
            square, narrow, narrow, square, sds((shard, 128), F32), expert, expert,
            sds((local, depth, width), F32), sds(y.shape, BF16), sds(y.shape, BF16),
        ],
        compiler_params=pltpu.CompilerParams(vmem_limit_bytes=LIMIT),
        name="finish",
    )(shares, pieces, sums, y, grad)


def rotary_tables(length):
    half = HEAD_SIZE // 2
    freqs = THETA ** (-(np.arange(half, dtype=np.float32) * 2.0 / HEAD_SIZE)).astype(np.float32)
    angles = np.arange(length, dtype=np.float32)[:, None] * freqs[None, :]
    cosine, sine = np.cos(angles), np.sin(angles)
    cosine = np.concatenate([cosine, cosine, cosine, cosine], axis=1)
    sine = np.concatenate([-sine, sine, -sine, sine], axis=1)
    return jnp.asarray(cosine, F32), jnp.asarray(sine, F32)


def per_device(
    tokens, attn_gain, q_weight, key_matrix, value_matrix, o_weight, ffn_gain, router_weight,
    expert_gate, expert_up, expert_down, routes, starts, cotangent,
):
    n = lax.axis_size("expert")
    member = lax.axis_index("expert")
    rows, width = tokens.shape
    length = rows * n
    kv_local = KEY_VALUE_HEADS // n
    q_cols = QUERY_HEADS // n * HEAD_SIZE
    k_cols = kv_local * HEAD_SIZE
    local, shard, _ = expert_gate.shape
    padded = -(-local // 8) * 8

    wq = lax.dynamic_slice_in_dim(q_weight, member * q_cols, q_cols, 1)
    wk = lax.dynamic_slice_in_dim(key_matrix, member * k_cols, k_cols, 1)
    wv = lax.dynamic_slice_in_dim(value_matrix, member * k_cols, k_cols, 1)
    wide = width // 2
    used = q_cols + 2 * k_cols
    router = jnp.pad(
        router_weight.reshape(shard, n, local), ((0, 0), (0, 0), (0, padded - local))
    ).reshape(shard, n * padded)
    gains = jnp.stack([attn_gain, ffn_gain], axis=1)
    gap = jnp.zeros((shard, wide - 128 - used), BF16)
    packed = jnp.concatenate(
        [
            wq, wk, wv, gap, jnp.pad(gains, ((0, 0), (0, 6))), router,
            jnp.zeros((shard, 120 - n * padded), BF16),
        ],
        axis=1,
    )
    packed = lax.all_gather(packed, "dp").reshape(width, -1)
    hot = routes[:, :, None] == jnp.arange(n * local, dtype=jnp.int32)
    chosen = jnp.any(hot, axis=1).astype(F32).T.reshape(n, local, rows)
    chosen = jnp.pad(chosen, ((0, 0), (0, padded - local), (0, 0))).reshape(n * padded, rows)
    cosine, sine = rotary_tables(length)
    chips = lax.axis_size("dp") // 2

    cols = -(-used // 128) * 128
    stacked = stack(expert_gate, expert_up, expert_down)
    experts_w = lax.all_gather(stacked, "dp")
    tokens_all, w_all, w_o = gather_tokens(
        n, cols, tokens, q_weight, key_matrix, value_matrix, o_weight
    )
    w_o = w_o.reshape(width, width)
    norms, q, k, v, lse, out, att, cots, small, chosen_all = attend(
        n, kv_local, tokens_all, packed, cosine, sine, starts, cotangent, chosen
    )
    w_all, att = lax.optimization_barrier((w_all, att))
    w_all = lax.all_gather(w_all, "dp").reshape(width, n * cols)
    hidden, twos, two = mix(n, tokens, att, w_o, small)
    grad_experts, back, gg, output = experts(
        n, chosen_all, small, twos, cots, cotangent, hidden, experts_w
    )
    expert_grads = lax.psum_scatter(grad_experts, "dp", scatter_dimension=0)
    grad_hidden, ga, sums_o, extra = give_back(
        n, chips, back, gg, chosen, small, hidden, two, cotangent, att, w_o
    )
    input_grad, shares, o_grad = attend_back(
        n, kv_local, (q, k, v, lse, out), ga, starts, cosine, sine, norms, w_all, tokens,
        small, grad_hidden, extra, sums_o,
    )
    q_grad, k_grad, v_grad, o_grad, rest, gate_grad, up_grad, down_grad, output, input_grad = finish(
        n, key_matrix.shape[1], expert_down.shape[1], shares, o_grad, expert_grads, output, input_grad
    )
    router_grad = rest[:, 8 : 8 + n * padded].reshape(shard, n, padded)[:, :, :local]
    return (
        output, input_grad, rest[:, 0] / attn_gain.astype(F32), q_grad, k_grad, v_grad, o_grad,
        rest[:, 1], router_grad.reshape(shard, n * local), gate_grad, up_grad, down_grad,
    )


def solution(mesh):
    rows, split, expert = P(("dp", "expert"), None), P("dp", None), P("expert", "dp", None)
    return jax.shard_map(
        per_device,
        mesh=mesh,
        in_specs=(
            rows, P("dp"), split, split, split, split, P("dp"), split,
            expert, expert, expert, rows, split, rows,
        ),
        out_specs=(
            rows, rows, P("dp"), split, split, split, split, P("dp"), split,
            expert, expert, expert,
        ),
        check_vma=False,
    )
```

```python
import functools

import jax
import jax.numpy as jnp
import numpy as np
from jax import lax
from jax.experimental import pallas as pl
from jax.experimental.pallas import tpu as pltpu
from jax.sharding import PartitionSpec as P

MODEL_WIDTH = 1536
QUERY_HEADS = 24
KEY_VALUE_HEADS = 8
HEAD_SIZE = 64
TOPK = 8
PIECE_LEN = 256
EPSILON = 1e-05
THETA = 10000.0
BF16 = jnp.bfloat16
F32 = jnp.float32


def dot(left, right, dims=((1,), (0,))):
    return lax.dot_general(left, right, (dims, ((), ())), preferred_element_type=F32)


def dot_t(left, right):
    return dot(left, right, ((1,), (1,)))


def tdot(left, right):
    return dot(left, right, ((0,), (0,)))


DMA = pltpu.SemaphoreType.DMA
MESH = pl.DeviceIdType.MESH
LIMIT = 60 * 1024 * 1024


def barrier_all(n, me):
    barrier = pltpu.get_barrier_semaphore()
    for d in range(n):

        @pl.when(d != me)
        def _():
            pl.semaphore_signal(barrier, inc=1, device_id={"expert": d}, device_id_type=MESH)

    pl.semaphore_wait(barrier, n - 1)


def barrier_plane(n, me, chips, place):
    barrier = pltpu.get_barrier_semaphore()
    core, chip = place % 2, place // 2
    for d in range(n):

        @pl.when(d != me)
        def _():
            pl.semaphore_signal(barrier, inc=1, device_id={"expert": d}, device_id_type=MESH)

    pl.semaphore_signal(
        barrier, inc=1, device_id={"dp": place + 1 - 2 * core}, device_id_type=MESH
    )
    for c in range(chips):

        @pl.when(c != chip)
        def _():
            pl.semaphore_signal(
                barrier, inc=1, device_id={"dp": 2 * c + core}, device_id_type=MESH
            )

    pl.semaphore_wait(barrier, n - 1 + chips)


def remote(src, dst, send, recv, target, axis="expert"):
    return pltpu.make_async_remote_copy(
        src_ref=src, dst_ref=dst, send_sem=send, recv_sem=recv,
        device_id={axis: target}, device_id_type=MESH,
    )


class ChainGather:
    def __init__(self, n, me, slots, send, recv):
        self.n, self.me, self.slots, self.send, self.recv = n, me, slots, send, recv

    def copy(self, way, s, block, target):
        ref = self.slots.at[block]
        return remote(ref, ref, self.send.at[way, s], self.recv.at[way, s], target)

    def right(self, s):
        return self.copy(0, s, self.me - s, self.me + 1)

    def left(self, s):
        return self.copy(1, s, self.me + s, self.me - 1)

    def arrived(self, s):
        n, me = self.n, self.me

        @pl.when(me - 1 - s >= 0)
        def _():
            self.copy(0, s, me - 1 - s, me).wait_recv()

        @pl.when(me + 1 + s < n)
        def _():
            self.copy(1, s, me + 1 + s, me).wait_recv()

    def step(self, s):
        n, me = self.n, self.me
        if s >= 1:
            self.arrived(s - 1)

        @pl.when((me - s >= 0) & (me + 1 < n))
        def _():
            self.right(s).start()

        @pl.when((me + s < n) & (me > 0))
        def _():
            self.left(s).start()

    def finish(self):
        n, me = self.n, self.me
        self.arrived(n - 2)
        for s in range(n - 1):

            @pl.when((me - s >= 0) & (me + 1 < n))
            def _():
                self.right(s).wait_send()

            @pl.when((me + s < n) & (me > 0))
            def _():
                self.left(s).wait_send()


class Exchange:
    def __init__(self, n, me, source, slots, send, recv):
        self.n, self.me, self.source, self.slots = n, me, source, slots
        self.send, self.recv = send, recv

    def start(self, d):
        me = self.me

        @pl.when(d != me)
        def _():
            remote(
                self.source.at[d], self.slots.at[me], self.send.at[d], self.recv.at[me], d
            ).start()

    def finish(self):
        me = self.me
        for d in range(self.n):

            @pl.when(d != me)
            def _():
                desc = remote(
                    self.source.at[d], self.slots.at[d], self.send.at[d], self.recv.at[d], d
                )
                desc.wait_send()
                desc.wait_recv()


class PairReduce:
    def __init__(self, chips, place, parts, first, sums, second, near_sems, across_sems):
        self.chips, self.core, self.chip = chips, place % 2, place // 2
        self.partner = place + 1 - 2 * self.core
        self.parts, self.first, self.sums, self.second = parts, first, sums, second
        self.near_sems, self.across_sems = near_sems, across_sems

    def near(self, c):
        s, r = self.near_sems
        source = self.parts.at[2 * c + 1 - self.core]
        return remote(source, self.first.at[c], s.at[c], r.at[c], self.partner, "dp")

    def across(self, c, slot):
        s, r = self.across_sems
        return remote(
            self.sums.at[c], self.second.at[slot], s.at[c], r.at[slot], 2 * c + self.core, "dp"
        )

    def pair(self):
        for c in range(self.chips):
            self.near(c).start()

    def add(self):
        for c in range(self.chips):
            self.near(c).wait_recv()
            mine = self.parts[2 * c + self.core].astype(F32)
            self.sums[c] = (mine + self.first[c].astype(F32)).astype(BF16)

    def pair_sent(self):
        for c in range(self.chips):
            self.near(c).wait_send()

    def spread(self):
        for c in range(self.chips):

            @pl.when(c != self.chip)
            def _():
                self.across(c, self.chip).start()

    def finish(self, total):
        total[...] = self.sums[self.chip].astype(F32)
        for c in range(self.chips):

            @pl.when(c != self.chip)
            def _():
                self.across(c, self.chip).wait_send()
                self.across(c, c).wait_recv()
                total[...] += self.second[c].astype(F32)


def chain_sems(n):
    return [pltpu.SemaphoreType.DMA((2, n - 1)), pltpu.SemaphoreType.DMA((2, n - 1))]


def direct_sems(n):
    return [pltpu.SemaphoreType.DMA((n,)), pltpu.SemaphoreType.DMA((n,))]


def call(kernel, outs, scratch, ident, name, micros, args, far=(), keep=()):
    vmem, hbm = pl.BlockSpec(memory_space=pltpu.VMEM), pl.BlockSpec(memory_space=pltpu.HBM)
    smem = pl.BlockSpec(memory_space=pltpu.SMEM)
    nbytes = sum(a.size * a.dtype.itemsize for a in args)
    first, count = len(args), len(outs)

    def body(*refs):
        inside, results, rest = refs[:first], list(refs[first : first + count]), refs[first + count :]
        stages, rest = rest[: len(keep)], rest[len(keep) :]
        copies = {}
        if keep:
            for j, k in enumerate(keep):
                copies[k] = pltpu.make_async_copy(stages[j], results[k], rest[0].at[j])
                results[k] = stages[j]
            rest = rest[1:]

        def save(*which):
            for k in which:
                copies[k].start()

        kernel(*inside, *results, *rest, **(dict(save=save) if keep else {}))
        for k in keep:
            copies[k].wait()

    kept = [pltpu.VMEM(outs[k].shape, outs[k].dtype) for k in keep]
    return pl.pallas_call(
        body,
        in_specs=[
            hbm if j in far else smem if a.dtype == jnp.int32 else vmem for j, a in enumerate(args)
        ],
        out_specs=[hbm if k in keep else vmem for k in range(count)],
        out_shape=outs,
        scratch_shapes=kept + ([pltpu.SemaphoreType.DMA((len(keep),))] if keep else []) + scratch,
        compiler_params=pltpu.CompilerParams(
            collective_id=ident, has_side_effects=True, vmem_limit_bytes=LIMIT
        ),
        cost_estimate=pl.CostEstimate(
            flops=micros * 10**9, transcendentals=0, bytes_accessed=nbytes
        ),
        name=name,
    )(*args)


def stack_kernel(
    n, me_ref, gate_ref, up_ref, down_ref, q_ref, k_ref, v_ref, first_ref, second_ref, router_ref,
    stack_ref, packed_ref,
):
    local, depth, width = down_ref.shape
    ff = gate_ref.shape[2]
    stack_ref[:local] = gate_ref[...]
    stack_ref[local : 2 * local] = up_ref[...]
    for j in range(width // ff):
        stack_ref[2 * local :, j * depth : (j + 1) * depth, :] = down_ref[
            :, :, j * ff : (j + 1) * ff
        ]
    shard, wide = packed_ref.shape
    at = 0
    for ref in (q_ref, k_ref, v_ref):
        part = ref.shape[1] // n
        mine = ref[:, :part]
        for z in range(1, n):
            mine = jnp.where(me_ref[0] == z, ref[:, z * part : (z + 1) * part], mine)
        packed_ref[:, at : at + part] = mine
        at += part
    small = wide - 128
    if at < small:
        packed_ref[:, at:small] = jnp.zeros((shard, small - at), BF16)
    tall = -(-shard // 128) * 128
    gains = jnp.concatenate([first_ref[...], second_ref[...]], axis=0).astype(F32)
    gains = jnp.concatenate([gains, jnp.zeros((2, tall - shard), F32)], axis=1)
    gains = jnp.concatenate([gains, jnp.zeros((126, tall), F32)], axis=0)
    packed_ref[:, small:] = gains.T[:shard, :].astype(BF16)
    padded = -(-local // 8) * 8
    for z in range(n):
        lane = small + 8 + z * padded
        packed_ref[:, lane : lane + local] = router_ref[:, z * local : (z + 1) * local]


def stack(n, member, wide, gate, up, down, wq, wk, wv, first, second, router):
    local, shard, ff = gate.shape
    vmem = pl.BlockSpec(memory_space=pltpu.VMEM)
    return pl.pallas_call(
        functools.partial(stack_kernel, n),
        in_specs=[pl.BlockSpec(memory_space=pltpu.SMEM)] + [vmem] * 9,
        out_specs=[vmem] * 2,
        out_shape=[
            jax.ShapeDtypeStruct((3 * local, shard, ff), BF16),
            jax.ShapeDtypeStruct((shard, wide), BF16),
        ],
        compiler_params=pltpu.CompilerParams(vmem_limit_bytes=LIMIT),
        cost_estimate=pl.CostEstimate(flops=4 * 10**9, transcendentals=0, bytes_accessed=8 * 10**6),
        name="stack",
    )(
        member.astype(jnp.int32)[None], gate, up, down, wq, wk, wv, first[None], second[None],
        router,
    )


class PlaneGather:
    def __init__(self, chips, place, slots, sems):
        self.chips, self.core, self.chip, self.place = chips, place % 2, place // 2, place
        self.partner = place + 1 - 2 * self.core
        self.slots, self.sems = slots, sems

    def across(self, c, block):
        s, r, _, _ = self.sems
        ref = self.slots.at[block]
        return remote(ref, ref, s.at[c], r.at[block // 2], 2 * c + self.core, "dp")

    def near(self, block):
        _, _, s, r = self.sems
        ref = self.slots.at[block]
        return remote(ref, ref, s.at[block // 2], r.at[block // 2], self.partner, "dp")

    def start(self):
        self.near(self.place).start()
        for c in range(self.chips):

            @pl.when(c != self.chip)
            def _():
                self.across(c, self.place).start()

    def forward(self):
        for c in range(self.chips):

            @pl.when(c != self.chip)
            def _():
                block = 2 * c + self.core
                self.across(c, block).wait_recv()
                self.near(block).start()

    def finish(self):
        for c in range(self.chips):
            self.near(2 * c + self.core).wait_send()
            self.near(2 * c + 1 - self.core).wait_recv()

            @pl.when(c != self.chip)
            def _():
                self.across(c, self.place).wait_send()


def gather_kernel(
    n, tokens_ref, q_ref, k_ref, v_ref, o_ref, all_ref, heads_ref, o_all_ref, load, s0, r0, *sems, save
):
    me = lax.axis_index("expert")
    place = lax.axis_index("dp")
    chips = o_all_ref.shape[0] // 2
    rows = pltpu.make_async_copy(tokens_ref, all_ref.at[me], load.at[0])
    own = pltpu.make_async_copy(o_ref, o_all_ref.at[place], load.at[1])
    rows.start()
    own.start()
    barrier_plane(n, me, chips, place)
    chain = ChainGather(n, me, all_ref, s0, r0)
    weights = PlaneGather(chips, place, o_all_ref, sems)
    rows.wait()
    chain.step(0)
    own.wait()
    weights.start()
    cols = heads_ref.shape[1] // n
    at = 0
    if cols * n > q_ref.shape[1] + 2 * k_ref.shape[1]:
        heads_ref[...] = jnp.zeros_like(heads_ref)
    for ref in (q_ref, k_ref, v_ref):
        part = ref.shape[1] // n
        for z in range(n):
            heads_ref[:, z * cols + at : z * cols + at + part] = ref[:, z * part : (z + 1) * part]
        at += part
    save(1)
    for s in range(1, n - 1):
        chain.step(s)
    weights.forward()
    weights.finish()
    save(2)
    chain.finish()
    save(0)


def gather_tokens(n, cols, tokens, wq, wk, wv, wo):
    rows, width = tokens.shape
    shard = wq.shape[0]
    chips = width // shard // 2
    sds = jax.ShapeDtypeStruct
    return call(
        functools.partial(gather_kernel, n),
        [
            sds((n, rows, width), BF16), sds((shard, n * cols), BF16),
            sds((2 * chips, shard, width), BF16),
        ],
        [pltpu.SemaphoreType.DMA((2,))] + chain_sems(n) + direct_sems(chips) + direct_sems(chips),
        1, "gather_tokens", 60, (tokens, wq, wk, wv, wo), (0, 4), (0, 1, 2),
    )


def turn(x, cosine, sine):
    half = HEAD_SIZE // 2
    tiles = []
    for c in range(0, x.shape[1], 128):
        tile = x[:, c : c + 128]
        lane = lax.broadcasted_iota(jnp.int32, tile.shape, 1) % HEAD_SIZE
        other = jnp.where(lane < half, pltpu.roll(tile, 128 - half, 1), pltpu.roll(tile, half, 1))
        tiles.append(tile * cosine + other * sine)
    return jnp.concatenate(tiles, axis=1)


def bias_rows(starts_ref, q_pos, k_pos):
    seen = k_pos <= q_pos
    for k in range(starts_ref.shape[1]):
        a = starts_ref[0, k]
        q_in = (q_pos >= a) & (q_pos < a + PIECE_LEN)
        k_in = (k_pos >= a) & (k_pos < a + PIECE_LEN)
        seen = seen | (q_in & k_in)
    return jnp.where(seen, 0.0, -1e30)


def reach_of(block, rows, length, pieces):
    span = length // pieces
    return min(length, -(-((block + 1) * rows) // span) * span)


def attend_kernel(
    n, kv_local, tokens_ref, packed_ref, cos_ref, sin_ref, starts_ref, cot_ref,
    chosen_ref, norm_ref, q_ref, k_ref, v_ref, lse_ref, out_ref, att_ref, cots_ref, small_ref,
    every_ref, w_s, send_att, send_chosen, load, s0, r0, s1, r1, s2, r2, *, save,
):
    me = lax.axis_index("expert")
    per_key, length, tile = q_ref.shape
    rows = length // n
    q_cols, k_cols = per_key * tile, tile
    width, wide = w_s.shape
    weights = pltpu.make_async_copy(packed_ref, w_s, load)
    weights.start()
    barrier_all(n, me)
    cots_ref[me] = cot_ref[:, : cots_ref.shape[2]]
    chain = ChainGather(n, me, cots_ref, s0, r0)
    chain.step(0)
    swap = Exchange(n, me, send_att, att_ref, s1, r1)
    choice = Exchange(n, me, send_chosen, every_ref, s2, r2)
    every_ref[me] = chosen_ref[...]
    for d in range(n):
        send_chosen[d] = chosen_ref[...]
        choice.start(d)
    pieces = starts_ref.shape[1]
    weights.wait()
    small = w_s[:, wide - 128 :].astype(F32).T
    small_ref[...] = small[: small_ref.shape[0], :]
    save(8)
    gain = small[:1, :]
    lane = lax.broadcasted_iota(jnp.int32, (rows, tile), 1)
    lane_w = lax.broadcasted_iota(jnp.int32, (rows, 128), 1)
    for i in range(n):
        part = slice(i * rows, (i + 1) * rows)
        x = tokens_ref[i].astype(F32)
        inverse = lax.rsqrt(jnp.mean(x * x, axis=1, keepdims=True) + EPSILON)
        norm = (x * inverse * gain).astype(BF16)
        norm_ref[i] = norm
        qkv = dot(norm, w_s[:, : wide - 128])
        qk = turn(qkv[:, : q_cols + k_cols], cos_ref[part, :], sin_ref[part, :]).astype(BF16)
        v_ref[part, :] = qkv[:, q_cols + k_cols : q_cols + 2 * k_cols].astype(BF16)
        k_ref[part, :] = qk[:, q_cols:]
        q = (qk[:, :q_cols].astype(F32) * HEAD_SIZE ** (-0.5)).astype(BF16)
        for t in range(per_key):
            for g in range(kv_local):
                at = (g * per_key + t) * HEAD_SIZE
                q_ref[t, part, g * HEAD_SIZE : (g + 1) * HEAD_SIZE] = q[:, at : at + HEAD_SIZE]
    save(0, 1, 2, 3)
    if n > 2:
        chain.step(1)
    for i in range(n):
        reach = reach_of(i, rows, length, pieces)
        part = slice(i * rows, (i + 1) * rows)
        q_pos = lax.broadcasted_iota(jnp.int32, (rows, reach), 0) + i * rows
        k_pos = lax.broadcasted_iota(jnp.int32, (rows, reach), 1)
        bias = bias_rows(starts_ref, q_pos, k_pos)
        keys, values = k_ref[:reach, :], v_ref[:reach, :]
        k_lane = lax.broadcasted_iota(jnp.int32, (reach, tile), 1)

        def head(t, logs):
            q = q_ref[t, part, :]
            total = jnp.zeros((rows, tile), F32)
            for g in range(kv_local):
                mine = lane // HEAD_SIZE == g
                scores = dot_t(jnp.where(mine, q, jnp.zeros_like(q)), keys) + bias
                top = jnp.max(scores, axis=1, keepdims=True)
                powers = jnp.exp(scores - top)
                norm = jnp.sum(powers, axis=1, keepdims=True)
                value = jnp.where(k_lane // HEAD_SIZE == g, values, jnp.zeros_like(values))
                total = total + dot(powers.astype(BF16), value) * (1.0 / norm)
                logs = jnp.where(lane_w == t * kv_local + g, top + jnp.log(norm), logs)
            out_ref[t, part, :] = total
            return logs

        logs = lax.fori_loop(0, per_key, head, jnp.zeros((rows, 128), F32))
        lse_ref[:, part] = logs.T[: lse_ref.shape[0], :]
        for t in range(per_key):
            for g in range(kv_local):
                at = (g * per_key + t) * HEAD_SIZE
                send_att[i, :, at : at + HEAD_SIZE] = out_ref[
                    t, part, g * HEAD_SIZE : (g + 1) * HEAD_SIZE
                ].astype(BF16)
        swap.start(i)
        if i + 2 < n - 1:
            chain.step(i + 2)
    save(4, 5)
    att_ref[me] = send_att[me]
    choice.finish()
    chain.finish()
    save(7, 9)
    swap.finish()


def attend(n, kv_local, tokens_all, packed, cosine, sine, starts, cot, chosen):
    rows, width = cot.shape
    length = n * rows
    tile = kv_local * HEAD_SIZE
    per_key = QUERY_HEADS // KEY_VALUE_HEADS
    q_cols = per_key * tile
    wide = packed.shape[1]
    sds = jax.ShapeDtypeStruct
    lse_rows = -(-per_key * kv_local // 8) * 8
    return call(
        functools.partial(attend_kernel, n, kv_local),
        [
            sds((n, rows, width), BF16),
            sds((per_key, length, tile), BF16),
            sds((length, tile), BF16),
            sds((length, tile), BF16),
            sds((lse_rows, length), F32),
            sds((per_key, length, tile), F32),
            sds((n, rows, q_cols), BF16),
            sds((n, rows, width // 2), BF16),
            sds((8 + chosen.shape[0], width), F32),
            sds((n,) + chosen.shape, F32),
        ],
        [
            pltpu.VMEM((width, wide), BF16), pltpu.VMEM((n, rows, q_cols), BF16),
            pltpu.VMEM((n,) + chosen.shape, F32), DMA,
        ]
        + chain_sems(n) + direct_sems(n) + direct_sems(n),
        2, "attend", 80,
        (tokens_all, packed, cosine, sine, starts, cot, chosen), (1,),
        (0, 1, 2, 3, 4, 5, 7, 8, 9),
    )


def mix_kernel(
    n, tokens_ref, att_ref, packed_ref, small_ref, hidden_ref, norms_ref, own_ref, w_s, load, s0, r0, *, save
):
    me = lax.axis_index("expert")
    q_cols = att_ref.shape[2]
    width = w_s.shape[0]
    weights = pltpu.make_async_copy(packed_ref, w_s, load)
    weights.start()
    hidden = tokens_ref[...].astype(F32)
    weights.wait()
    for s in range(n):
        hidden = hidden + dot(att_ref[s], w_s[s * q_cols : (s + 1) * q_cols, :])
    hidden_ref[...] = hidden
    inverse = lax.rsqrt(jnp.mean(hidden * hidden, axis=1, keepdims=True) + EPSILON)
    norm = (hidden * inverse * small_ref[1:2, :]).astype(BF16)
    own_ref[...] = norm
    barrier_all(n, me)
    norms_ref[me] = norm
    chain = ChainGather(n, me, norms_ref, s0, r0)
    chain.step(0)
    save(0, 2)
    for s in range(1, n - 1):
        chain.step(s)
    chain.finish()
    save(1)


def mix(n, tokens, att, w_o, small):
    rows, width = tokens.shape
    sds = jax.ShapeDtypeStruct
    return call(
        functools.partial(mix_kernel, n),
        [sds((rows, width), F32), sds((n, rows, width), BF16), sds((rows, width), BF16)],
        [pltpu.VMEM((width, width), BF16), DMA] + chain_sems(n),
        3, "mix", 60, (tokens, att, w_o, small), (2,), (0, 1, 2),
    )


class ChainReduce:
    def __init__(self, n, me, parts, slots, send, recv):
        self.n, self.me, self.parts = n, me, parts
        self.slots, self.send, self.recv = slots, send, recv

    def copy(self, way, s, d, source):
        target = self.me + 1 if way == 0 else self.me - 1
        slot = d if way == 0 else jnp.where(d == target, self.n, d)
        return remote(
            source.at[d], self.slots.at[slot], self.send.at[way, s], self.recv.at[way, s], target
        )

    def far(self, way):
        return self.me if way == 0 else self.n - 1 - self.me

    def step(self, when):
        for way in (0, 1):
            far = self.far(way)
            s = when - far
            d = self.n - 1 - s if way == 0 else s
            slots = self.slots

            @pl.when(s >= 0)
            def _():
                @pl.when(far == 0)
                def _():
                    self.copy(way, s, d, self.parts).start()

                @pl.when(far > 0)
                def _():
                    self.copy(way, s, d, slots).wait_recv()
                    slots[d] = (slots[d].astype(F32) + self.parts[d].astype(F32)).astype(BF16)
                    self.copy(way, s, d, slots).start()

            if when > 0:

                @pl.when(s > 0)
                def _():
                    self.copy(way, s - 1, d, slots).wait_send()

    def finish(self, total, onto=False):
        n, me = self.n, self.me
        mine = self.parts[me].astype(F32)
        total[...] = total[...] + mine if onto else mine
        for way in (0, 1):
            far = self.far(way)

            @pl.when(far > 0)
            def _():
                self.copy(way, n - 1 - far, me, self.slots).wait_recv()
                total[...] += self.slots[me if way == 0 else n].astype(F32)

            @pl.when(far < n - 1)
            def _():
                self.copy(way, n - 2 - far, me, self.slots).wait_send()


def rms_back(grad, rows, gain):
    inverse = lax.rsqrt(jnp.mean(rows * rows, axis=1, keepdims=True) + EPSILON)
    scaled = grad * gain
    grad_gain = jnp.sum(grad * rows * inverse, axis=0, keepdims=True)
    mean = jnp.mean(scaled * rows, axis=1, keepdims=True)
    return inverse * scaled - rows * (inverse * inverse * inverse * mean), grad_gain


def softmax_chosen(logits, chosen):
    top = jnp.max(jnp.where(chosen > 0.0, logits, -1e30), axis=0, keepdims=True)
    powers = jnp.where(chosen > 0.0, jnp.exp(jnp.where(chosen > 0.0, logits - top, 0.0)), 0.0)
    return powers / jnp.sum(powers, axis=0, keepdims=True)


def return_kernel(
    n, parts_ref, gg_ref, chosen_ref, small_ref, hidden_ref, norm_ref, cot_ref, att_ref, packed_ref,
    grad_ref, ga_ref, o_ref, extra_ref,
    w_s, slots, total, gg_s, send_ga, o_parts, o_first, load, s0, r0, s1, r1, s2, r2, *near, save,
):
    me = lax.axis_index("expert")
    place = lax.axis_index("dp")
    chips = o_ref.shape[0]
    width = w_s.shape[0]
    q_cols = ga_ref.shape[2]
    weights = pltpu.make_async_copy(packed_ref, w_s, load)
    weights.start()
    barrier_plane(n, me, chips, place)
    chain = ChainReduce(n, me, parts_ref, slots, s0, r0)
    chain.step(0)
    gates_swap = Exchange(n, me, gg_ref, gg_s, s1, r1)
    for d in range(n):
        gates_swap.start(d)
    gg_s[me] = gg_ref[me]
    router = small_ref[8:, :].astype(BF16)
    gates = softmax_chosen(dot_t(router, norm_ref[...]), chosen_ref[...])
    gates_swap.finish()
    grad_gates = gg_s[...].reshape(gates.shape)
    middle = jnp.sum(gates * grad_gates, axis=0, keepdims=True)
    grad_logits = (gates * (grad_gates - middle)).astype(BF16)
    extra_ref[8:, :] = dot(grad_logits, norm_ref[...])
    for s in range(1, n - 1):
        chain.step(s)
    chain.finish(total)
    grad_norm = total[...] + tdot(grad_logits, router)
    grad, grad_gain = rms_back(grad_norm, hidden_ref[...], small_ref[1:2, :])
    row = lax.broadcasted_iota(jnp.int32, (8, width), 0)
    extra_ref[:8, :] = jnp.where(row == 1, grad_gain, 0.0)
    grad = cot_ref[...].astype(F32) + grad
    grad_ref[...] = grad
    save(0, 3)
    proj = grad.astype(BF16)
    weights.wait()
    swap = Exchange(n, me, send_ga, ga_ref, s2, r2)
    for d in range(n):
        send_ga[d] = dot_t(proj, w_s[d * q_cols : (d + 1) * q_cols, :]).astype(BF16)
        swap.start(d)
    ga_ref[me] = send_ga[me]
    shard = o_parts.shape[1]
    for d in range(n):
        grad_o = tdot(att_ref[d], proj).astype(BF16)
        o_parts[d * q_cols // shard : (d + 1) * q_cols // shard] = grad_o.reshape(-1, shard, width)
    o_sum = PairReduce(chips, place, o_parts, o_first, o_ref, None, near, None)
    o_sum.pair()
    o_sum.add()
    save(2)
    o_sum.pair_sent()
    swap.finish()
    save(1)


def give_back(n, chips, parts, gg, chosen, small, hidden, norm, cot, att, w_o):
    rows, width = cot.shape
    q_cols = att.shape[2]
    shard = width // (2 * chips)
    sds, vm = jax.ShapeDtypeStruct, pltpu.VMEM
    return call(
        functools.partial(return_kernel, n),
        [
            sds((rows, width), F32), sds(att.shape, BF16), sds((chips, shard, width), BF16),
            sds(small.shape, F32),
        ],
        [
            vm((width, width), BF16), vm((n + 1, rows, width), BF16),
            vm((rows, width), F32), vm(gg.shape, F32), vm((n, rows, q_cols), BF16),
            vm((2 * chips, shard, width), BF16), vm((chips, shard, width), BF16), DMA,
        ]
        + chain_sems(n) + direct_sems(n) + direct_sems(n) + direct_sems(chips),
        4, "give_back", 80,
        (parts, gg, chosen, small, hidden, norm, cot, att, w_o), (8,), (0, 1, 2, 3),
    )


def attend_back_kernel(
    n, kv_local, q_ref, k_ref, v_ref, lse_ref, out_ref, ga_ref, starts_ref, cos_ref,
    sin_ref, norm_ref, all_ref, tokens_ref, small_ref, grad_ref, extra_ref, o_ref,
    input_ref, shares_ref, og_ref,
    w_s, gq_s, gk_s, gv_s, gqkv_s, ga_s, q_send, q_got, kv_send, kv_got, load,
    norm_s, tokens_s, grad_s, extra_s, o_second, o_total, o_send, o_got, dw_s, w_first, w_sums, w_second, w_total,
    s0, r0, s1, r1, s2, r2, s3, r3, s4, r4, *sems,
):
    me = lax.axis_index("expert")
    place = lax.axis_index("dp")
    per_key, length, tile = q_ref.shape
    chips, shard, _ = o_ref.shape
    rows = length // n
    q_cols, k_cols = per_key * tile, tile
    width = w_s.shape[0]
    cols = w_s.shape[1] // n
    scale = HEAD_SIZE ** (-0.5)
    pieces = starts_ref.shape[1]
    late = [
        pltpu.make_async_copy(source, target, load.at[j])
        for j, (source, target) in enumerate(
            (
                (all_ref, w_s), (norm_ref, norm_s), (tokens_ref, tokens_s), (grad_ref, grad_s),
                (extra_ref, extra_s),
            )
        )
    ]
    for copy in late:
        copy.start()
    barrier_plane(n, me, chips, place)
    o_sum = PairReduce(chips, place, None, None, o_ref, o_second, None, sems[:2])
    o_sum.spread()
    q_swap = Exchange(n, me, q_send, q_got, s0, r0)
    kv_swap = Exchange(n, me, kv_send, kv_got, s1, r1)
    o_swap = Exchange(n, me, o_send, o_got, s2, r2)
    o_share = ChainGather(n, me, og_ref, s3, r3)
    w_share = ChainGather(n, me, shares_ref, s4, r4)
    gq_s[...] = jnp.zeros_like(gq_s)
    gqkv_s[...] = jnp.zeros_like(gqkv_s)
    gk_s[...] = jnp.zeros_like(gk_s)
    gv_s[...] = jnp.zeros_like(gv_s)
    lane = lax.broadcasted_iota(jnp.int32, (rows, tile), 1)
    lane_w = lax.broadcasted_iota(jnp.int32, (rows, 128), 1)
    for i in range(n):
        reach = reach_of(i, rows, length, pieces)
        part = slice(i * rows, (i + 1) * rows)
        deltas = jnp.zeros((rows, 128), F32)
        for t in range(per_key):
            for g in range(kv_local):
                at = (g * per_key + t) * HEAD_SIZE
                ga_s[t, :, g * HEAD_SIZE : (g + 1) * HEAD_SIZE] = ga_ref[i, :, at : at + HEAD_SIZE]
            product = ga_s[t].astype(F32) * out_ref[t, part, :]
            for g in range(kv_local):
                own = jnp.where(lane // HEAD_SIZE == g, product, 0.0)
                deltas = jnp.where(
                    lane_w == t * kv_local + g, jnp.sum(own, axis=1, keepdims=True), deltas
                )
        delta_s = deltas.T
        k_pos = lax.broadcasted_iota(jnp.int32, (reach, rows), 0)
        q_pos = lax.broadcasted_iota(jnp.int32, (reach, rows), 1) + i * rows
        bias = bias_rows(starts_ref, q_pos, k_pos)
        keys, values = k_ref[:reach, :], v_ref[:reach, :]
        k_lane = lax.broadcasted_iota(jnp.int32, (reach, tile), 1)
        for t in range(per_key):
            q, ga = q_ref[t, part, :], ga_s[t]
            grad_q = jnp.zeros((rows, tile), F32)
            for g in range(kv_local):
                h = t * kv_local + g
                mine = lane // HEAD_SIZE == g
                q_g = jnp.where(mine, q, jnp.zeros_like(q))
                ga_g = jnp.where(mine, ga, jnp.zeros_like(ga))
                scores = dot_t(keys, q_g) + bias
                probs = jnp.exp(scores - lse_ref[h : h + 1, part])
                grad_probs = dot_t(values, ga_g)
                grad_raw = (probs * (grad_probs - delta_s[h : h + 1, :])).astype(BF16)
                gk_s[:reach, :tile] += dot(grad_raw, q_g)
                gv_s[:reach, :] += dot(probs.astype(BF16), ga_g)
                key = jnp.where(k_lane // HEAD_SIZE == g, keys, jnp.zeros_like(keys))
                grad_q = grad_q + tdot(grad_raw, key)
            for g in range(kv_local):
                at = (g * per_key + t) * HEAD_SIZE
                gq_s[:, at : at + HEAD_SIZE] = (
                    grad_q[:, g * HEAD_SIZE : (g + 1) * HEAD_SIZE] * scale
                )
        turned = turn(gq_s[...], cos_ref[part, :], -sin_ref[part, :])[:, :q_cols].astype(BF16)
        gqkv_s[part, :q_cols] = turned
        q_send[i] = turned
        q_swap.start(i)
    for i in range(n):
        part = slice(i * rows, (i + 1) * rows)
        turned = turn(gk_s[part, :], cos_ref[part, :], -sin_ref[part, :])[:, :k_cols].astype(BF16)
        kv_send[i, :, :k_cols] = turned
        kv_send[i, :, k_cols:] = gv_s[part, :].astype(BF16)
        kv_swap.start(i)
        gqkv_s[part, q_cols : q_cols + 2 * k_cols] = kv_send[i]
    for copy in late:
        copy.wait()
    norms = norm_s[...].reshape(length, width)
    dw = tdot(norms, gqkv_s[...])
    own = w_s[:, pl.ds(pl.multiple_of(me * cols, 128), cols)].astype(F32)
    grad_gain = jnp.sum(dw * own, axis=1, keepdims=True)
    dw_s[:, :, :cols] = dw.astype(BF16).reshape(2 * chips, shard, cols)
    extra = extra_s[...]
    extra = jnp.concatenate([extra, jnp.zeros((128 - extra.shape[0], width), F32)], axis=0).T
    lane_e = lax.broadcasted_iota(jnp.int32, extra.shape, 1)
    extra = jnp.where(lane_e == 0, grad_gain, extra)
    dw_s[:, :, cols:] = extra.astype(BF16).reshape(2 * chips, shard, 128)
    w_sum = PairReduce(chips, place, dw_s, w_first, w_sums, w_second, sems[2:4], sems[4:])
    w_sum.pair()
    w_sum.add()
    w_sum.spread()
    o_sum.finish(o_total)
    piece = width // n
    for d in range(n):
        o_send[d] = o_total[:, d * piece : (d + 1) * piece].astype(BF16)
        o_swap.start(d)
    q_got[me] = q_send[me]
    kv_got[me] = kv_send[me]
    q_swap.finish()
    kv_swap.finish()
    grad_norm = jnp.zeros((rows, width), F32)
    for z in range(n):
        grad_norm = grad_norm + dot_t(q_got[z], w_s[:, z * cols : z * cols + q_cols])
        grad_norm = grad_norm + dot_t(
            kv_got[z], w_s[:, z * cols + q_cols : z * cols + q_cols + 2 * k_cols]
        )
    grad, _ = rms_back(grad_norm, tokens_s[...].astype(F32), small_ref[:1, :])
    input_ref[...] = (grad_s[...] + grad).astype(BF16)
    o_swap.finish()
    mine = o_send[me].astype(F32)
    for d in range(n):
        mine = mine + jnp.where(d == me, 0.0, o_got[d].astype(F32))
    og_ref[me] = mine.astype(BF16)
    o_share.step(0)
    w_sum.pair_sent()
    w_sum.finish(w_total)
    shares_ref[me] = w_total[...].astype(BF16)
    w_share.step(0)
    for s in range(1, n - 1):
        o_share.step(s)
        w_share.step(s)
    o_share.finish()
    w_share.finish()


def attend_back(
    n, kv_local, saved, ga, starts, cosine, sine, norms, w_all, tokens, small, grad, extra, sums_o
):
    q, k, v, lse, out = saved
    rows, width = tokens.shape
    per_key, length, tile = q.shape
    chips, shard, _ = sums_o.shape
    cols = w_all.shape[1] // n
    wide = cols + 128
    sds, vm = jax.ShapeDtypeStruct, pltpu.VMEM
    q_cols = per_key * tile
    across_w = vm((chips, shard, wide), BF16)
    piece = vm((n, shard, width // n), BF16)
    q_block, kv_block = vm((n, rows, q_cols), BF16), vm((n, rows, 2 * tile), BF16)
    return call(
        functools.partial(attend_back_kernel, n, kv_local),
        [
            sds((rows, width), BF16), sds((n, shard, wide), BF16),
            sds((n, shard, width // n), BF16),
        ],
        [
            vm(w_all.shape, BF16), vm((rows, -(-q_cols // 128) * 128), F32), vm((length, 128), F32),
            vm((length, tile), F32), vm((length, cols), BF16), vm((per_key, rows, tile), BF16),
            q_block, q_block, kv_block, kv_block, pltpu.SemaphoreType.DMA((5,)),
            vm(norms.shape, BF16), vm(tokens.shape, BF16), vm(grad.shape, F32), vm(extra.shape, F32),
            vm((chips, shard, width), BF16), vm((shard, width), F32), piece, piece,
            vm((2 * chips, shard, wide), BF16), across_w, across_w, across_w,
            vm((shard, wide), F32),
        ]
        + direct_sems(n) + direct_sems(n) + direct_sems(n) + chain_sems(n) + chain_sems(n)
        + direct_sems(chips) + direct_sems(chips) + direct_sems(chips),
        5, "attend_back", 90,
        (q, k, v, lse, out, ga, starts, cosine, sine, norms, w_all, tokens, small, grad, extra,
         sums_o),
        (9, 10, 11, 13, 14),
    )


def expert_kernel(
    n, chips, chosen_ref, small_ref, n2_ref, cots_ref, cot_ref, hidden_ref, wg_ref, wu_ref, wd_ref,
    dw_ref, gx_ref, gg_ref, output_ref, gate_ref,
    x_s, g_s, slope_s, silu_s, act_s, gact_s, ggp_s, gup_s, pick_s, mix_s, y_s, y_slots,
    total, gate_s, rank_s, rest_s, d_parts, d_first, d_sums, d_second, d_total, d_stage,
    load, pair_free, across_free, s0, r0, s1, r1, *sems,
):
    me = lax.axis_index("expert")
    place = lax.axis_index("dp")
    _, rows, width = n2_ref.shape
    local, tall, ff = act_s.shape
    cap = tall // n
    shards = wg_ref.shape[0]
    depth = ff // shards
    blocks = width // ff
    at = pl.program_id(0)
    later = jnp.maximum(at - local, 0)
    e = jnp.where(at < local, at, later // 3)
    phase = jnp.where(at < local, -1, later % 3)
    mine = me * gg_ref.shape[1] + e
    where = pl.ds(pl.multiple_of(e * cap, cap), cap)
    chain = ChainReduce(n, me, y_s, y_slots, s0, r0)
    more = ChainGather(n, me, rest_s, s1, r1)
    half = cots_ref.shape[2]
    last = local - 1
    skip = last - gate_ref.shape[0]
    spread = PairReduce(chips, place, d_parts, d_first, d_sums, d_second, sems[:2], sems[2:])
    begun = pltpu.make_async_copy(hidden_ref, total, load.at[0])
    ended = pltpu.make_async_copy(y_s, gx_ref, load.at[1])

    def gate_out(of):
        return pltpu.make_async_copy(d_stage, gate_ref.at[of - skip], load.at[2])

    def gate_done(of):
        spread.finish(d_total)

        @pl.when(of > skip)
        def _():
            gate_out(of - 1).wait()

        d_stage[...] = d_total[...].astype(BF16)
        gate_out(of).start()

    def whole(ref):
        return ref[...].reshape(width, ff)

    def down(j):
        return wd_ref[:, 0, j * depth : (j + 1) * depth, :].reshape(ff, ff)

    def gate_column(s, pick):
        return jnp.sum(jnp.where(pick, gate_s[s, pl.ds(mine, 1), :], 0.0), axis=1, keepdims=True)

    @pl.when(at == 0)
    def _():
        barrier_plane(n, me, chips, place)
        begun.start()
        rest_s[me] = cot_ref[:, half:]
        more.step(0)
        before = lax.broadcasted_iota(jnp.int32, (rows, rows), 0)
        upto = jnp.where(before <= lax.broadcasted_iota(jnp.int32, (rows, rows), 1), 1.0, 0.0)
        router = small_ref[8:, :].astype(BF16)
        for s in range(n):
            chosen = chosen_ref[s]
            gate_s[s] = softmax_chosen(dot_t(router, n2_ref[s]), chosen)
            count = dot(chosen.astype(BF16), upto.astype(BF16))
            rank_s[s] = jnp.where(chosen > 0.0, count - 1.0, -1.0).astype(jnp.int32)
        gg_ref[...] = jnp.zeros_like(gg_ref)

    for s in range(1, n - 1):

        @pl.when(at == min((s * local + n - 2) // (n - 1), local - 1))
        def _():
            more.step(s)

    @pl.when(phase < 0)
    def _():
        slot = lax.broadcasted_iota(jnp.int32, (cap, rows), 0)
        cols = []
        for s in range(n):
            pick = slot == rank_s[s, pl.ds(mine, 1), :]
            hot = jnp.where(pick, 1.0, 0.0).astype(BF16)
            pick_s[s, where, :] = hot
            cols.append(gate_column(s, pick))
            x_s[s * cap : (s + 1) * cap, :] = dot(hot, n2_ref[s]).astype(BF16)
        x = x_s[...]
        gp = dot(x, whole(wg_ref))
        up = dot(x, whole(wu_ref))
        sigma = jax.nn.sigmoid(gp)
        silu = gp * sigma
        act = (silu * up).astype(BF16)
        act_s[e] = act
        silu_s[e] = silu.astype(BF16)
        slope_s[e] = (up * sigma * (1.0 + gp * (1.0 - sigma))).astype(BF16)
        for j in range(blocks):
            lanes = slice(j * ff, (j + 1) * ff)
            res = dot(act, down(j)).astype(BF16).astype(F32)
            for s in range(n):
                mix_s[s, where, lanes] = (cols[s] * res[s * cap : (s + 1) * cap, :]).astype(BF16)

    @pl.when(at == local - 1)
    def _():
        for s in range(n):
            y_s[s] = tdot(pick_s[s], mix_s[s]).astype(BF16)

    for s in range(n - 1):

        @pl.when(at == local + s * 3 * local // (n - 1))
        def _():
            chain.step(s)

    @pl.when(at == local)
    def _():
        more.finish()

    @pl.when(phase == 0)
    def _():
        for s in range(n):
            hot = pick_s[s, where, :]
            x_s[s * cap : (s + 1) * cap, :] = dot(hot, n2_ref[s]).astype(BF16)
            g_s[s * cap : (s + 1) * cap, :half] = dot(hot, cots_ref[s]).astype(BF16)
            g_s[s * cap : (s + 1) * cap, half:] = dot(hot, rest_s[s]).astype(BF16)
        grad_act = jnp.zeros((tall, ff), F32)
        for j in range(blocks):
            grad_act = grad_act + dot_t(g_s[:, j * ff : (j + 1) * ff], down(j))
        act = act_s[e].astype(F32)
        sums = jnp.sum(act * grad_act, axis=1, keepdims=True)
        cols = []
        for s in range(n):
            pick = pick_s[s, where, :].astype(F32) > 0.5
            cols.append(gate_column(s, pick))
            part = sums[s * cap : (s + 1) * cap, :]
            gg_ref[s, pl.ds(e, 1), :] = jnp.sum(jnp.where(pick, part, 0.0), axis=0, keepdims=True)
        col = jnp.concatenate(cols, axis=0)
        grad_act = grad_act * col
        gact_s[...] = (act * col).astype(BF16)
        ggp = (grad_act * slope_s[e].astype(F32)).astype(BF16)
        ggp_s[...] = ggp
        gup_s[...] = (grad_act * silu_s[e].astype(F32)).astype(BF16)
        grad = tdot(x_s[...], ggp).astype(BF16)

        @pl.when((e < skip) | (e == last))
        def _():
            dw_ref[...] = grad.reshape(dw_ref.shape)

        @pl.when((e > skip) & (e < last))
        def _():
            pl.semaphore_wait(pair_free, 1)
            spread.pair_sent()

        @pl.when((e >= skip) & (e < last))
        def _():
            d_parts[...] = grad.reshape(d_parts.shape)
            spread.pair()

    @pl.when(phase == 1)
    def _():
        dw_ref[...] = tdot(x_s[...], gup_s[...]).astype(BF16).reshape(dw_ref.shape)
        grows = dot_t(ggp_s[...], whole(wg_ref)) + dot_t(gup_s[...], whole(wu_ref))
        grows = grows.astype(BF16)
        for s in range(n):
            mix_s[s, where, :] = grows[s * cap : (s + 1) * cap, :]

        @pl.when(e > skip)
        def _():
            gate_done(e - 1)

        @pl.when((e > skip) & (e < last))
        def _():
            for c in range(chips):

                @pl.when(c != spread.chip)
                def _():
                    pl.semaphore_signal(
                        across_free, inc=1, device_id={"dp": 2 * c + spread.core},
                        device_id_type=MESH,
                    )

            pl.semaphore_wait(across_free, chips - 1)

        @pl.when((e >= skip) & (e < last))
        def _():
            spread.add()

        @pl.when((e >= skip) & (e < last - 1))
        def _():
            pl.semaphore_signal(
                pair_free, inc=1, device_id={"dp": spread.partner}, device_id_type=MESH
            )

        @pl.when((e >= skip) & (e < last))
        def _():
            spread.spread()

    @pl.when(phase == 2)
    def _():
        for j in range(blocks):
            grad = tdot(gact_s[...], g_s[:, j * ff : (j + 1) * ff]).astype(BF16)
            dw_ref[:, 0, j * depth : (j + 1) * depth, :] = grad.reshape(shards, depth, ff)

    @pl.when(at == 4 * local - 1)
    def _():
        begun.wait()
        chain.finish(total, True)
        output_ref[...] = total[...].astype(BF16)
        for s in range(n):
            y_s[s] = tdot(pick_s[s], mix_s[s]).astype(BF16)
        ended.start()
        spread.pair_sent()
        gate_out(last - 1).wait()
        ended.wait()


def experts(n, chips, chosen, small, n2, cots, cot, hidden, w):
    _, rows, width = n2.shape
    shards, local, depth, ff = w.shape
    local = local // 3
    cap = rows * TOPK * 5 // (4 * local * n)
    tall = n * cap
    padded = chosen.shape[1] // n
    skip = min(2, local - 2)
    once = pl.Buffered(1)

    def const(shape):
        return pl.BlockSpec(shape, lambda i: (0,) * len(shape), pipeline_mode=once)

    def place(i):
        later = jnp.maximum(i - local, 0)
        return jnp.where(i < local, i, later // 3), later % 3

    def weight(k):
        return pl.BlockSpec((shards, 1, depth, ff), lambda i: (0, k * local + place(i)[0], 0, 0))

    def grads(i):
        later = jnp.maximum(i - local, 0)
        e, phase = later // 3, later % 3
        before = jnp.where(e < skip, 2 * local + e, local + e - 1)
        before = jnp.where(e == local - 1, 2 * local + skip, before)
        return (0, jnp.where(phase == 1, e, jnp.where(phase == 2, local + e, before)), 0, 0)

    sds, vm = jax.ShapeDtypeStruct, pltpu.VMEM
    hbm = pl.BlockSpec(memory_space=pltpu.HBM)
    across = vm((chips, depth, ff), BF16)
    saved, half = vm((local, tall, ff), BF16), vm((tall, ff), BF16)
    return pl.pallas_call(
        functools.partial(expert_kernel, n, chips),
        grid=(4 * local,),
        in_specs=[
            const(chosen.shape), const(small.shape), const(n2.shape), const(cots.shape),
            const(cot.shape), hbm, weight(0), weight(1), weight(2),
        ],
        out_specs=[
            pl.BlockSpec((shards, 1, depth, ff), grads),
            hbm, const((n, padded, rows)), const(hidden.shape), hbm,
        ],
        out_shape=[
            sds((shards, 2 * local + skip + 1, depth, ff), BF16), sds(n2.shape, BF16),
            sds((n, padded, rows), F32), sds(hidden.shape, BF16), sds((local - 1 - skip, depth, ff), BF16),
        ],
        scratch_shapes=[
            vm((tall, width), BF16), vm((tall, width), BF16), saved, saved, saved, half, half, half,
            vm((n, local * cap, rows), BF16), vm((n, local * cap, width), BF16), vm(n2.shape, BF16),
            vm((n + 1, rows, width), BF16), vm(hidden.shape, F32), vm(chosen.shape, F32), vm(chosen.shape, jnp.int32),
            vm((n, rows, width - cots.shape[2]), BF16), vm((shards, depth, ff), BF16), across, across,
            across, vm((depth, ff), F32), vm((depth, ff), BF16), pltpu.SemaphoreType.DMA((3,)),
            pltpu.SemaphoreType.REGULAR, pltpu.SemaphoreType.REGULAR,
        ]
        + chain_sems(n) + chain_sems(n) + direct_sems(chips) + direct_sems(chips),
        compiler_params=pltpu.CompilerParams(
            collective_id=6, has_side_effects=True, vmem_limit_bytes=LIMIT,
            dimension_semantics=("arbitrary",),
        ),
        cost_estimate=pl.CostEstimate(
            flops=95 * 10**9, transcendentals=0, bytes_accessed=60 * 10**6
        ),
        name="experts",
    )(chosen, small, n2, cots, cot, hidden, w, w, w)


def finish_kernel(
    n, shares_far, pieces_far, gates_far, sums_far, y_far, grad_far, q_ref, k_ref, v_ref, o_ref, gains_ref,
    router_ref, gate_ref, up_ref, down_ref, output_ref, input_ref, shares_ref, pieces_ref, gates_ref, sums_ref, sems,
):
    copies = [
        pltpu.make_async_copy(source, target, sems.at[j])
        for j, (source, target) in enumerate(
            (
                (shares_far, shares_ref), (pieces_far, pieces_ref), (gates_far, gates_ref), (sums_far, sums_ref),
                (y_far, output_ref), (grad_far, input_ref),
            )
        )
    ]
    for copy in copies:
        copy.start()
    for copy in copies:
        copy.wait()
    q_cols, k_cols = q_ref.shape[1] // n, k_ref.shape[1] // n
    piece = pieces_ref.shape[2]
    cols = shares_ref.shape[2] - 128
    shard = q_ref.shape[0]
    small = jnp.zeros((shard, 128), F32)
    for z in range(n):
        at = 0
        for ref, part in ((q_ref, q_cols), (k_ref, k_cols), (v_ref, k_cols)):
            ref[:, z * part : (z + 1) * part] = shares_ref[z, :, at : at + part].astype(F32)
            at += part
        small = small + shares_ref[z, :, cols:].astype(F32)
        o_ref[:, z * piece : (z + 1) * piece] = pieces_ref[z].astype(F32)
    local, depth, _ = down_ref.shape
    padded = -(-local // 8) * 8
    for z in range(n):
        router_ref[:, z * local : (z + 1) * local] = small[
            :, 8 + z * padded : 8 + z * padded + local
        ]
    gap = -(-shard // 128) * 128 - shard
    gains_ref[...] = jnp.concatenate([small, jnp.zeros((gap, 128), F32)], axis=0).T[:8, :shard]
    ff = gate_ref.shape[2]
    skip = local - 1 - gates_ref.shape[0]
    gate_ref[:skip] = sums_ref[2 * local : 2 * local + skip].astype(F32)
    gate_ref[skip : local - 1] = gates_ref[...].astype(F32)
    gate_ref[local - 1] = sums_ref[2 * local + skip].astype(F32)
    up_ref[...] = sums_ref[:local].astype(F32)
    for j in range(down_ref.shape[2] // ff):
        down_ref[:, :, j * ff : (j + 1) * ff] = sums_ref[
            local : 2 * local, j * depth : (j + 1) * depth, :
        ].astype(F32)


def finish(n, k_width, depth, shares, pieces, gates, sums, y, grad):
    _, shard, _ = shares.shape
    width = y.shape[1]
    local, ff = (sums.shape[0] + gates.shape[0]) // 3, sums.shape[2]
    sds = jax.ShapeDtypeStruct
    square, narrow, expert = (
        sds((shard, width), F32), sds((shard, k_width), F32), sds((local, shard, ff), F32)
    )
    vmem, hbm = pl.BlockSpec(memory_space=pltpu.VMEM), pl.BlockSpec(memory_space=pltpu.HBM)
    return pl.pallas_call(
        functools.partial(finish_kernel, n),
        in_specs=[hbm] * 6,
        out_specs=[vmem] * 11,
        scratch_shapes=[
            pltpu.VMEM(a.shape, BF16) for a in (shares, pieces, gates, sums)
        ] + [pltpu.SemaphoreType.DMA((6,))],
        out_shape=[
            square, narrow, narrow, square, sds((8, shard), F32), sds((shard, n * local), F32),
            expert, expert,
            sds((local, depth, width), F32), sds(y.shape, BF16), sds(y.shape, BF16),
        ],
        compiler_params=pltpu.CompilerParams(vmem_limit_bytes=LIMIT),
        name="finish",
    )(shares, pieces, gates, sums, y, grad)


def rotary_tables(length):
    half = HEAD_SIZE // 2
    freqs = THETA ** (-(np.arange(half, dtype=np.float32) * 2.0 / HEAD_SIZE)).astype(np.float32)
    angles = np.arange(length, dtype=np.float32)[:, None] * freqs[None, :]
    cosine, sine = np.cos(angles), np.sin(angles)
    cosine = np.concatenate([cosine, cosine, cosine, cosine], axis=1)
    sine = np.concatenate([-sine, sine, -sine, sine], axis=1)
    return jnp.asarray(cosine, F32), jnp.asarray(sine, F32)


def per_device(
    tokens, attn_gain, q_weight, key_matrix, value_matrix, o_weight, ffn_gain, router_weight,
    expert_gate, expert_up, expert_down, routes, starts, cotangent,
):
    n = lax.axis_size("expert")
    member = lax.axis_index("expert")
    rows, width = tokens.shape
    length = rows * n
    kv_local = KEY_VALUE_HEADS // n
    q_cols = QUERY_HEADS // n * HEAD_SIZE
    k_cols = kv_local * HEAD_SIZE
    local, shard, _ = expert_gate.shape
    padded = -(-local // 8) * 8

    wide = width // 2
    used = q_cols + 2 * k_cols
    stacked, packed = stack(
        n, member, wide, expert_gate, expert_up, expert_down, q_weight, key_matrix, value_matrix,
        attn_gain, ffn_gain, router_weight,
    )
    packed = lax.all_gather(packed, "dp").reshape(width, -1)
    experts_w = lax.all_gather(stacked, "dp")

    hot = routes[:, :, None] == jnp.arange(n * local, dtype=jnp.int32)
    chosen = jnp.any(hot, axis=1).astype(F32).T.reshape(n, local, rows)
    chosen = jnp.pad(chosen, ((0, 0), (0, padded - local), (0, 0))).reshape(n * padded, rows)
    cosine, sine = rotary_tables(length)
    chips = lax.axis_size("dp") // 2

    cols = -(-used // 128) * 128
    tokens_all, w_all, w_o = gather_tokens(
        n, cols, tokens, q_weight, key_matrix, value_matrix, o_weight
    )
    w_o = w_o.reshape(width, width)
    norms, q, k, v, lse, out, att, cots, small, chosen_all = attend(
        n, kv_local, tokens_all, packed, cosine, sine, starts, cotangent, chosen
    )
    w_all, att = lax.optimization_barrier((w_all, att))
    w_all = lax.all_gather(w_all, "dp").reshape(width, n * cols)
    hidden, twos, two = mix(n, tokens, att, w_o, small)
    grad_experts, back, gg, output, gate_sums = experts(
        n, chips, chosen_all, small, twos, cots, cotangent, hidden, experts_w
    )
    expert_grads = lax.psum_scatter(grad_experts, "dp", scatter_dimension=0)
    grad_hidden, ga, sums_o, extra = give_back(
        n, chips, back, gg, chosen, small, hidden, two, cotangent, att, w_o
    )
    input_grad, shares, o_grad = attend_back(
        n, kv_local, (q, k, v, lse, out), ga, starts, cosine, sine, norms, w_all, tokens,
        small, grad_hidden, extra, sums_o,
    )
    (
        q_grad, k_grad, v_grad, o_grad, gains, router_grad, gate_grad, up_grad, down_grad, output,
        input_grad,
    ) = finish(
        n, key_matrix.shape[1], expert_down.shape[1], shares, o_grad, gate_sums, expert_grads, output,
        input_grad,
    )
    return (
        output, input_grad, gains[0] / attn_gain.astype(F32), q_grad, k_grad, v_grad, o_grad,
        gains[1], router_grad, gate_grad, up_grad, down_grad,
    )


def solution(mesh):
    rows, split, expert = P(("dp", "expert"), None), P("dp", None), P("expert", "dp", None)
    return jax.shard_map(
        per_device,
        mesh=mesh,
        in_specs=(
            rows, P("dp"), split, split, split, split, P("dp"), split,
            expert, expert, expert, rows, split, rows,
        ),
        out_specs=(
            rows, rows, P("dp"), split, split, split, split, P("dp"), split,
            expert, expert, expert,
        ),
        check_vma=False,
    )
```
